32 devices in a mesh: gx: 8 (over y, x, core), gy: 4 (over z).
Axes of the slice: x: 2, y: 2, z: 4, core: 2. Of those that a mesh axis runs over, the one named last changes fastest.
Arguments:
- eigen_block: float32 [16, 64, 64, 128], P(None, 'gx', 'gy'), may hold values from -25 to 25, as said below
- search_dirs: float32 [16, 64, 64, 128], P(None, 'gx', 'gy'), may hold values from -3 to 3
Outputs:
- new_block: float32 [16, 64, 64, 128], P(None, 'gx', 'gy')
- new_search: float32 [16, 64, 64, 128], P(None, 'gx', 'gy')
The draws below stay inside these ranges and needn't reach their ends.
Inputs may be any that keep to these rules, and one draw needn't show every extreme that they name: `eigen_block`: real numbers whose typical size changes along the first grid dimension.
All inputs are finite; a program needn't handle non-finite values.
Results may differ from the reference program's by a relative error of at most 0.0003.
Values sent between devices are 32-bit elements; how exact they have to be, the bound alone decides.
No kernel may reach another device: no remote copies, remote signals or barrier semaphores. Data moves between devices by JAX's collectives and lax.ppermute only.
A program may use at most 64 MiB of HBM per device.

```python
import jax
import jax.numpy as jnp
from jax import lax

K = 16
NZ = 128
NU_PRE = 2
NU_POST = 2
NC = 4
NX = 64
NY = 64


def draw_eigen_block(key, part):
    key_base, key_rough = jax.random.split(jax.random.fold_in(key, 11))
    shape = (K, NX, NY, NZ)
    plane = jnp.arange(NX, dtype=jnp.float32) / jnp.float32(max(NX - 1, 1))
    rising = jnp.exp(jnp.log(3.0) * plane)[None, :, None, None]
    rough = jnp.exp(jax.random.uniform(key_rough, shape, jnp.float32, -0.7, 0.7))
    base = jnp.clip(jax.random.normal(key_base, shape, jnp.float32), -4.0, 4.0)
    return base * rough * rising


def block_scale(key, dims, shards, smallest, high):
    level = 1.0
    for position, parts in shards:
        heights = jax.random.uniform(jax.random.fold_in(jax.random.fold_in(key, 6), position), (parts,), jnp.float32, smallest / len(shards), high / len(shards))
        level = level * jnp.repeat(jnp.exp(heights), dims[position] // parts).reshape((-1,) + (1,) * (len(dims) - 1 - position))
    return level


def normal_values(stream_key, dims, deviation, reach, cuts=(), kind=jnp.bfloat16):
    entries = jax.random.normal(stream_key, dims, jnp.float32) * deviation
    if len(cuts) > 0:
        entries = block_scale(stream_key, dims, cuts, -0.22, 0.18) * entries
    return jnp.clip(entries, min=-reach, max=reach).astype(kind)


def setup_inputs(seed: int = 0) -> dict:
    splits = jax.random.split(jax.random.key(seed), 3)
    return {
        "eigen_block": draw_eigen_block(jax.random.fold_in(splits[2], 71), 0),
        "search_dirs": normal_values(splits[1], (K, NX, NY, NZ), 0.5, 3.0, ((1, 8), (2, 4)), jnp.float32),
    }


relax = 1.0 / 9.0
coarse_relax = 1.0 / 36.0
shift_value = 13.0

def stencil(full):
    center = full[..., 1:-1, 1:-1, 1:-1]
    beside = full[..., 2:, 1:-1, 1:-1] + full[..., :-2, 1:-1, 1:-1]
    beside = beside + full[..., 1:-1, 2:, 1:-1] + full[..., 1:-1, :-2, 1:-1]
    beside = beside + full[..., 1:-1, 1:-1, 2:] + full[..., 1:-1, 1:-1, :-2]
    return 6.0 * center - beside

def apply_lap(field):
    return stencil(jnp.pad(field, 1))

def restrict(field):
    sx, sy, sz = field.shape
    return field.reshape(sx // 2, 2, sy // 2, 2, sz // 2, 2).sum(axis=(1, 3, 5))

def prolong(field):
    sx, sy, sz = field.shape
    wide = jnp.broadcast_to(field[:, None, :, None, :, None], (sx, 2, sy, 2, sz, 2))
    return wide.reshape(sx * 2, sy * 2, sz * 2)

def vcycle(resid):
    corr = relax * resid
    for sweep in range(NU_PRE):
        corr = corr + relax * (resid - apply_lap(corr))
    rest = resid - apply_lap(corr)
    coarse_r = restrict(rest)
    coarse = coarse_relax * coarse_r
    for sweep in range(NC - 1):
        coarse = coarse + coarse_relax * (coarse_r - 4.0 * apply_lap(coarse))
    corr = corr + prolong(coarse)
    for sweep in range(NU_POST):
        corr = corr + relax * (resid - apply_lap(corr))
    return corr

def ritz_coef(gram, proj, ncells):
    hp = lax.Precision.HIGHEST
    proj = 0.5 * (proj + proj.T)
    lower = jnp.linalg.cholesky(gram)
    inner = jax.scipy.linalg.solve_triangular(lower, proj, lower=True)
    ritz = jax.scipy.linalg.solve_triangular(lower, inner.T, lower=True)
    ritz = 0.5 * (ritz + ritz.T)
    nbasis = gram.shape[0]
    kcount = nbasis // 3
    filtered = shift_value * jnp.eye(nbasis, dtype=jnp.float32)[:, :kcount] - ritz[:, :kcount]
    small = jnp.linalg.cholesky(jnp.dot(filtered.T, filtered, precision=hp))
    scaled = jax.scipy.linalg.solve_triangular(small, filtered.T, lower=True).T
    coef = jax.scipy.linalg.solve_triangular(lower, scaled, lower=True, trans='T')
    return coef * jnp.sqrt(jnp.float32(ncells))

def reference(eigen_block, search_dirs):
    hp = lax.Precision.HIGHEST
    image_x = lax.map(apply_lap, eigen_block)
    image_p = lax.map(apply_lap, search_dirs)
    numer = lax.optimization_barrier(jnp.sum(eigen_block * image_x, axis=(1, 2, 3)))
    denom = lax.optimization_barrier(jnp.sum(eigen_block * eigen_block, axis=(1, 2, 3)))
    theta = numer / denom
    resid = image_x - theta[:, None, None, None] * eigen_block
    precond = lax.map(vcycle, resid)
    image_w = lax.map(apply_lap, precond)
    basis = jnp.concatenate([eigen_block, precond, search_dirs], axis=0)
    images = jnp.concatenate([image_x, image_w, image_p], axis=0)
    gram = jnp.einsum('kxyz,lxyz->kl', basis, basis, precision=hp)
    proj = jnp.einsum('kxyz,lxyz->kl', images, basis, precision=hp)
    coef = ritz_coef(gram, proj, NX * NY * NZ)
    kcount = eigen_block.shape[0]
    coef_p = jnp.concatenate([jnp.zeros((kcount, kcount), jnp.float32), coef[kcount:]], axis=0)
    new_block = jnp.einsum('lk,lxyz->kxyz', coef, basis, precision=hp)
    new_search = jnp.einsum('lk,lxyz->kxyz', coef_p, basis, precision=hp)
    return (new_block, new_search)
```

```python
import functools

import jax
import jax.numpy as jnp
from jax import lax
from jax.experimental import pallas as pl
from jax.experimental.pallas import tpu as pltpu
from jax.sharding import PartitionSpec as P

RELAX = 1.0 / 9.0
COARSE_RELAX = 1.0 / 36.0
SHIFT = 13.0
DEEP = 4
POST = 3
CO = 3
PAD = 8

F32 = jnp.float32
VMEM = pl.BlockSpec(memory_space=pltpu.VMEM)
SMEM = pl.BlockSpec(memory_space=pltpu.SMEM)


def shape(*dims):
    return jax.ShapeDtypeStruct(dims, F32)


def call(kernel, outs, scratch, args, name, smem=0):
    specs = [SMEM] * smem + [VMEM] * (len(args) - smem)
    return pl.pallas_call(
        kernel,
        out_shape=outs,
        in_specs=specs,
        out_specs=[VMEM] * len(outs),
        scratch_shapes=scratch,
        name=name,
    )(*args)


def along_z(plane, step, lanes):
    size = plane.shape[-1]
    low = jnp.where(lanes >= step, pltpu.roll(plane, step, 1), 0.0)
    high = jnp.where(lanes < size - step, pltpu.roll(plane, size - step, 1), 0.0)
    return low + high


def beside(work, i, row, rows, center, before, after, lanes, step=1):
    total = before + after
    total = total + work[i, pl.ds(row - 1, rows), :] + work[i, pl.ds(row + 1, rows), :]
    return total + along_z(center, step, lanes)


def lane_index(rows):
    return lax.broadcasted_iota(jnp.int32, (rows, 128), 1)


def pack_kernel(x_ref, p_ref, ylo, yhi, xlo, xhi):
    cols, nx, ny, _ = x_ref.shape

    def body(f, carry):
        for i in range(nx):
            ylo[f, pl.ds(i * DEEP, DEEP), :] = x_ref[f, i, pl.ds(0, DEEP), :]
            yhi[f, pl.ds(i * DEEP, DEEP), :] = x_ref[f, i, pl.ds(ny - DEEP, DEEP), :]
            ylo[f, pl.ds(nx * DEEP + i, 1), :] = p_ref[f, i, pl.ds(0, 1), :]
            yhi[f, pl.ds(nx * DEEP + i, 1), :] = p_ref[f, i, pl.ds(ny - 1, 1), :]
        for i in range(DEEP):
            xlo[f, i] = x_ref[f, i]
            xhi[f, i] = x_ref[f, nx - DEEP + i]
        xlo[f, DEEP] = p_ref[f, 0]
        xhi[f, DEEP] = p_ref[f, nx - 1]
        return carry

    lax.fori_loop(0, cols, body, 0)


def theta_kernel(x_ref, ylo, yhi, xlo, xhi, out_ref, clo, chi, work):
    cols, nx, ny, _ = x_ref.shape
    lanes = lane_index(ny)
    spot = lane_index(8)
    half = nx // 2 * DEEP

    def body(f, carry):
        work[0, pl.ds(PAD, ny), :] = xlo[f, DEEP - 1]
        work[nx + 1, pl.ds(PAD, ny), :] = xhi[f, 0]
        for i in range(nx):
            work[i + 1, pl.ds(PAD, ny), :] = x_ref[f, i]
            work[i + 1, pl.ds(PAD - 1, 1), :] = ylo[f, pl.ds(i * DEEP + DEEP - 1, 1), :]
            work[i + 1, pl.ds(PAD + ny, 1), :] = yhi[f, pl.ds(i * DEEP, 1), :]
        numer = jnp.zeros((ny, 128), F32)
        denom = jnp.zeros((ny, 128), F32)
        before = work[0, pl.ds(PAD, ny), :]
        center = work[1, pl.ds(PAD, ny), :]
        for i in range(nx):
            after = work[i + 2, pl.ds(PAD, ny), :]
            image = 6.0 * center - beside(work, i + 1, PAD, ny, center, before, after, lanes)
            numer = numer + center * image
            denom = denom + center * center
            before, center = center, after
        numer = jnp.sum(numer, axis=(0, 1), keepdims=True)
        denom = jnp.sum(denom, axis=(0, 1), keepdims=True)
        clo[f, pl.ds(0, half), :] = ylo[f, pl.ds(0, half), :]
        clo[f, pl.ds(half, half), :] = yhi[f, pl.ds(0, half), :]
        chi[f, pl.ds(0, half), :] = ylo[f, pl.ds(half, half), :]
        chi[f, pl.ds(half, half), :] = yhi[f, pl.ds(half, half), :]
        carry = jnp.where(spot == f, numer, carry)
        return jnp.where(spot == f + cols, denom, carry)

    sums = lax.fori_loop(0, cols, body, jnp.zeros((8, 128), F32))
    for k in range(out_ref.shape[0]):
        out_ref[k] = sums


def pre_kernel(
    flags, sums, x_ref, ylo, yhi, xlo, xhi, clo, chi,
    r_ref, e_ref, c_ref, slo, shi,
    work, other, rhs, small, coarse,
):
    cols, nx, ny, _ = x_ref.shape
    tall = ny + 2 * DEEP
    wide = nx + 2 * DEEP
    lanes = lane_index(tall)
    own = lane_index(ny)
    spot = lane_index(8)
    has = [flags[k].astype(F32) for k in range(4)]
    row = lax.broadcasted_iota(jnp.int32, (tall, 128), 0)
    mask_y = RELAX * jnp.where(row < DEEP, has[2], jnp.where(row >= ny + DEEP, has[3], 1.0))

    def relax_of(i):
        if i < DEEP:
            return mask_y * has[0]
        if i >= nx + DEEP:
            return mask_y * has[1]
        return mask_y

    total = sums[0]
    for k in range(1, sums.shape[0]):
        total = total + sums[k]
    theta = total / pltpu.roll(total, 128 - cols, 1)

    @pl.when(jnp.bool_(True))
    def _():
        zero = jnp.zeros((8, 128), F32)
        for i in range(wide):
            for buf in (work, other):
                buf[i, pl.ds(0, PAD), :] = zero
                buf[i, pl.ds(PAD + tall, 8), :] = zero

    data = pl.ds(PAD, tall)

    def body(f, carry):
        th = jnp.sum(jnp.where(spot == f, theta, 0.0)) * 0.125
        for i in range(DEEP):
            lo, hi = i, nx + DEEP + i
            work[lo, pl.ds(PAD + DEEP, ny), :] = xlo[f, i]
            work[hi, pl.ds(PAD + DEEP, ny), :] = xhi[f, i]
            for plane, buf in ((lo, clo), (hi, chi)):
                work[plane, pl.ds(PAD, DEEP), :] = buf[f, pl.ds(i * DEEP, DEEP), :]
                work[plane, pl.ds(PAD + DEEP + ny, DEEP), :] = buf[
                    f, pl.ds(DEEP * DEEP + i * DEEP, DEEP), :
                ]
        for i in range(nx):
            work[i + DEEP, pl.ds(PAD + DEEP, ny), :] = x_ref[f, i]
            work[i + DEEP, pl.ds(PAD, DEEP), :] = ylo[f, pl.ds(i * DEEP, DEEP), :]
            work[i + DEEP, pl.ds(PAD + DEEP + ny, DEEP), :] = yhi[f, pl.ds(i * DEEP, DEEP), :]
        before = work[0, data, :]
        center = work[1, data, :]
        for i in range(1, wide - 1):
            after = work[i + 1, data, :]
            image = 6.0 * center - beside(work, i, PAD, tall, center, before, after, lanes)
            res = image - th * center
            rhs[i] = res
            other[i, data, :] = relax_of(i) * res
            before, center = center, after
        src, dst = other, work
        for depth in (2, 3):
            before = src[depth - 1, data, :]
            center = src[depth, data, :]
            for i in range(depth, wide - depth):
                after = src[i + 1, data, :]
                near = beside(src, i, PAD, tall, center, before, after, lanes)
                dst[i, data, :] = center + relax_of(i) * (rhs[i] - 6.0 * center + near)
                before, center = center, after
            src, dst = dst, src
        own_rows = pl.ds(PAD + DEEP, ny)
        before = src[DEEP - 1, own_rows, :]
        center = src[DEEP, own_rows, :]
        held = None
        for i in range(DEEP, nx + DEEP):
            after = src[i + 1, own_rows, :]
            near = beside(src, i, PAD + DEEP, ny, center, before, after, own)
            rest = rhs[i, pl.ds(DEEP, ny), :] - 6.0 * center + near
            e_ref[f, i - DEEP] = center
            if held is None:
                held = rest
            else:
                small[...] = held + rest
                pair = small[pl.ds(0, ny // 2, stride=2), :] + small[pl.ds(1, ny // 2, stride=2), :]
                mate = jnp.where(
                    spot % 2 == 0, pltpu.roll(pair, 127, 1), pltpu.roll(pair, 1, 1)
                )
                coarse[f, (i - DEEP) // 2] = pair + mate
                held = None
            before, center = center, after
        for i in range(2, wide - 2):
            r_ref[f, i - 2] = rhs[i]
        return carry

    lax.fori_loop(0, cols, body, 0)
    half, cx, cy = cols // 2, nx // 2, ny // 2
    even = spot % 2 == 0
    for g in range(half):
        for i in range(cx):
            both = jnp.where(even, coarse[g, i], coarse[g + half, i])
            c_ref[g, i] = both
            small[pl.ds(0, 8), :] = both
            at = (g * cx + i) * CO
            slo[pl.ds(at, CO), :] = small[pl.ds(0, CO), :]
            shi[pl.ds(at, CO), :] = small[pl.ds(cy - CO, CO), :]


def coarse_pack_kernel(c_ref, ylo, yhi, xlo, xhi):
    half, cx, cy, _ = c_ref.shape
    tall = cy + 2 * CO
    for g in range(half):
        for out, first in ((xlo, 0), (xhi, cx - CO)):
            for i in range(CO):
                at = (g * CO + i) * tall
                src = (g * cx + first + i) * CO
                out[pl.ds(at, CO), :] = ylo[pl.ds(src, CO), :]
                out[pl.ds(at + CO, cy), :] = c_ref[g, first + i]
                out[pl.ds(at + CO + cy, CO), :] = yhi[pl.ds(src, CO), :]


def coarse_kernel(
    flags, c_ref, ylo, yhi, xlo, xhi, e_ref, corr_ref, slo, shi, work, other, rhs, small
):
    half, cx, cy, _ = c_ref.shape
    cols, nx, ny, _ = e_ref.shape
    tall = cy + 2 * CO
    full = 16
    wide = cx + 2 * CO
    lanes = lane_index(full)
    spot = lane_index(8)
    odd = spot % 2 == 1
    has = [flags[k].astype(F32) for k in range(4)]
    row = lax.broadcasted_iota(jnp.int32, (full, 128), 0)
    mask_y = COARSE_RELAX * jnp.where(row < CO, has[2], jnp.where(row >= cy + CO, has[3], 1.0))
    zero = jnp.zeros((8, 128), F32)
    for i in range(wide):
        rhs[i, pl.ds(8, 8), :] = zero
        for buf in (work, other):
            buf[i, pl.ds(0, PAD), :] = zero
            buf[i, pl.ds(PAD + full, 8), :] = zero

    def relax_of(i):
        if i < CO:
            return mask_y * has[0]
        if i >= cx + CO:
            return mask_y * has[1]
        return mask_y

    data = pl.ds(PAD, full)

    def body(g, carry):
        for i in range(CO):
            rhs[i, pl.ds(0, tall), :] = xlo[pl.ds((g * CO + i) * tall, tall), :]
            rhs[cx + CO + i, pl.ds(0, tall), :] = xhi[pl.ds((g * CO + i) * tall, tall), :]
        for i in range(cx):
            at = pl.ds((g * cx + i) * CO, CO)
            rhs[i + CO, pl.ds(0, CO), :] = ylo[at, :]
            rhs[i + CO, pl.ds(CO, cy), :] = c_ref[g, i]
            rhs[i + CO, pl.ds(CO + cy, CO), :] = yhi[at, :]
        for i in range(wide):
            work[i, data, :] = relax_of(i) * rhs[i]
        src, dst = work, other
        for depth in (1, 2, 3):
            before = src[depth - 1, data, :]
            center = src[depth, data, :]
            for i in range(depth, wide - depth):
                after = src[i + 1, data, :]
                near = beside(src, i, PAD, full, center, before, after, lanes, 2)
                dst[i, data, :] = center + relax_of(i) * (rhs[i] - 4.0 * (6.0 * center - near))
                before, center = center, after
            src, dst = dst, src
        for i in range(cx):
            both = src[i + CO, pl.ds(PAD + CO, cy), :]
            first = jnp.where(odd, pltpu.roll(both, 1, 1), both)
            second = jnp.where(odd, both, pltpu.roll(both, 127, 1))
            for f, value in ((g, first), (g + half, second)):
                small[pl.ds(0, cy, stride=2), :] = value
                small[pl.ds(1, cy, stride=2), :] = value
                for k in (2 * i, 2 * i + 1):
                    corr = e_ref[f, k] + small[...]
                    corr_ref[f, k] = corr
                    slo[f, pl.ds(k * POST, POST), :] = corr_ref[f, k, pl.ds(0, POST), :]
                    shi[f, pl.ds(k * POST, POST), :] = corr_ref[f, k, pl.ds(ny - POST, POST), :]
        return carry

    lax.fori_loop(0, half, body, 0)


def post_pack_kernel(corr_ref, ylo, yhi, xlo, xhi):
    cols, nx, ny, _ = corr_ref.shape
    tall = ny + 2 * POST

    def body(f, carry):
        for out, first in ((xlo, 0), (xhi, nx - POST)):
            for i in range(POST):
                at = i * tall
                src = pl.ds((first + i) * POST, POST)
                out[f, pl.ds(at, POST), :] = ylo[f, src, :]
                out[f, pl.ds(at + POST, ny), :] = corr_ref[f, first + i]
                out[f, pl.ds(at + POST + ny, POST), :] = yhi[f, src, :]
        return carry

    lax.fori_loop(0, cols, body, 0)


def post_kernel(
    flags, corr_ref, ylo, yhi, xlo, xhi, r_ref, w_ref, image_ref, work, other
):
    cols, nx, ny, _ = corr_ref.shape
    tall = ny + 2 * DEEP
    wide = nx + 2 * POST
    span = ny + 2 * POST
    gap = DEEP - POST
    lanes = lane_index(tall)
    own = lane_index(ny)
    has = [flags[k].astype(F32) for k in range(4)]
    row = lax.broadcasted_iota(jnp.int32, (tall, 128), 0)
    mask_y = RELAX * jnp.where(row < DEEP, has[2], jnp.where(row >= ny + DEEP, has[3], 1.0))
    zero = jnp.zeros((PAD + 8, 128), F32)
    for i in range(wide):
        for buf in (work, other):
            buf[i, pl.ds(0, PAD + 8), :] = zero
            buf[i, pl.ds(PAD + tall - 8, 16), :] = zero

    def relax_of(i):
        if i < POST:
            return mask_y * has[0]
        if i >= nx + POST:
            return mask_y * has[1]
        return mask_y

    data = pl.ds(PAD, tall)

    def body(f, carry):
        for i in range(POST):
            work[i, pl.ds(PAD + gap, span), :] = xlo[f, pl.ds(i * span, span), :]
            work[nx + POST + i, pl.ds(PAD + gap, span), :] = xhi[f, pl.ds(i * span, span), :]
        for i in range(nx):
            at = pl.ds(i * POST, POST)
            work[i + POST, pl.ds(PAD + gap, POST), :] = ylo[f, at, :]
            work[i + POST, pl.ds(PAD + DEEP, ny), :] = corr_ref[f, i]
            work[i + POST, pl.ds(PAD + DEEP + ny, POST), :] = yhi[f, at, :]
        src, dst = work, other
        for depth in (1, 2):
            before = src[depth - 1, data, :]
            center = src[depth, data, :]
            for i in range(depth, wide - depth):
                after = src[i + 1, data, :]
                near = beside(src, i, PAD, tall, center, before, after, lanes)
                dst[i, data, :] = center + relax_of(i) * (r_ref[f, i - 1] - 6.0 * center + near)
                before, center = center, after
            src, dst = dst, src
        own_rows = pl.ds(PAD + DEEP, ny)
        before = src[POST - 1, own_rows, :]
        center = src[POST, own_rows, :]
        for i in range(POST, nx + POST):
            after = src[i + 1, own_rows, :]
            near = beside(src, i, PAD + DEEP, ny, center, before, after, own)
            w_ref[f, i - POST] = center
            image_ref[f, i - POST] = 6.0 * center - near
            before, center = center, after
        return carry

    lax.fori_loop(0, cols, body, 0)


def image_kernel(x_ref, p_ref, ylo, yhi, xlo, xhi, ax_ref, ap_ref, work):
    cols, nx, ny, _ = x_ref.shape
    lanes = lane_index(ny)

    def body(f, carry):
        for ref, out, lo, hi, base, deep in (
            (x_ref, ax_ref, DEEP - 1, 0, 0, DEEP),
            (p_ref, ap_ref, DEEP, DEEP, nx * DEEP, 1),
        ):
            work[0, pl.ds(PAD, ny), :] = xlo[f, lo]
            work[nx + 1, pl.ds(PAD, ny), :] = xhi[f, hi]
            for i in range(nx):
                work[i + 1, pl.ds(PAD, ny), :] = ref[f, i]
                work[i + 1, pl.ds(PAD - 1, 1), :] = ylo[f, pl.ds(base + i * deep + deep - 1, 1), :]
                work[i + 1, pl.ds(PAD + ny, 1), :] = yhi[f, pl.ds(base + i * deep, 1), :]
            before = work[0, pl.ds(PAD, ny), :]
            center = work[1, pl.ds(PAD, ny), :]
            for i in range(nx):
                after = work[i + 2, pl.ds(PAD, ny), :]
                near = beside(work, i + 1, PAD, ny, center, before, after, lanes)
                out[f, i] = 6.0 * center - near
                before, center = center, after
        return carry

    lax.fori_loop(0, cols, body, 0)


def from_low(value, axis):
    count = lax.axis_size(axis)
    return lax.ppermute(value, axis, [(i, i + 1) for i in range(count - 1)])


def from_high(value, axis):
    count = lax.axis_size(axis)
    return lax.ppermute(value, axis, [(i + 1, i) for i in range(count - 1)])


def radices(count):
    out = []
    if count % 2 == 0 and count % 4 == 0 and (count.bit_length() - 1) % 2 == 1:
        out.append(2)
        count //= 2
    while count % 4 == 0:
        out.append(4)
        count //= 4
    if count > 1:
        out.append(count)
    return out


def sum_all(value):
    for axis in ("gx", "gy"):
        count = lax.axis_size(axis)
        stride = 1
        for radix in radices(count):
            index = lax.axis_index(axis)
            parts = [value]
            for k in range(1, radix):
                pairs = []
                for i in range(count):
                    digit = i // stride % radix
                    target = i + ((digit + k) % radix - digit) * stride
                    pairs.append((i, target))
                parts.append(lax.ppermute(value, axis, pairs))
            digit = index // stride % radix
            if radix == 2:
                value = parts[0] + parts[1]
            elif radix == 4:
                even = parts[0] + parts[2]
                odd = parts[1] + parts[3]
                value = even + odd
            else:
                value = functools.reduce(jnp.add, parts)
            stride *= radix
    return value


def ritz_coef(gram, proj, ncells):
    hp = lax.Precision.HIGHEST
    proj = 0.5 * (proj + proj.T)
    lower = jnp.linalg.cholesky(gram)
    inner = jax.scipy.linalg.solve_triangular(lower, proj, lower=True)
    ritz = jax.scipy.linalg.solve_triangular(lower, inner.T, lower=True)
    ritz = 0.5 * (ritz + ritz.T)
    nbasis = gram.shape[0]
    kcount = nbasis // 3
    filtered = SHIFT * jnp.eye(nbasis, dtype=jnp.float32)[:, :kcount] - ritz[:, :kcount]
    small = jnp.linalg.cholesky(jnp.dot(filtered.T, filtered, precision=hp))
    scaled = jax.scipy.linalg.solve_triangular(small, filtered.T, lower=True).T
    coef = jax.scipy.linalg.solve_triangular(lower, scaled, lower=True, trans="T")
    return coef * jnp.sqrt(jnp.float32(ncells))


def body(x, p):
    hp = lax.Precision.HIGHEST
    cols, nx, ny, nz = x.shape
    ngx, ngy = lax.axis_size("gx"), lax.axis_size("gy")
    ix, iy = lax.axis_index("gx"), lax.axis_index("gy")
    flags = jnp.stack([ix > 0, ix < ngx - 1, iy > 0, iy < ngy - 1]).astype(jnp.int32)
    half, cx, cy = cols // 2, nx // 2, ny // 2
    work = pltpu.VMEM

    yrows = nx * DEEP + nx
    to_ylo, to_yhi, to_xlo, to_xhi = call(
        pack_kernel,
        [shape(cols, yrows, nz)] * 2 + [shape(cols, DEEP + 1, ny, nz)] * 2,
        [], (x, p), "pack",
    )
    ylo, yhi = from_low(to_yhi, "gy"), from_high(to_ylo, "gy")
    xlo, xhi = from_low(to_xhi, "gx"), from_high(to_xlo, "gx")

    devices = ngx * ngy
    sums, to_clo, to_chi = call(
        theta_kernel,
        [shape(devices, 8, 128)] + [shape(cols, nx * DEEP, nz)] * 2,
        [work((nx + 2, PAD + ny + 8, nz), F32)],
        (x, ylo, yhi, xlo, xhi), "theta",
    )
    clo, chi = from_low(to_chi, "gx"), from_high(to_clo, "gx")
    sums = lax.all_to_all(sums, ("gx", "gy"), 0, 0)

    tall, wide = ny + 2 * DEEP, nx + 2 * DEEP
    plane = PAD + tall + 8
    r, e, c, to_ylo, to_yhi = call(
        pre_kernel,
        [shape(cols, wide - 4, tall, nz), shape(cols, nx, ny, nz), shape(half, cx, cy, nz)]
        + [shape(half * cx * CO, nz)] * 2,
        [work((wide, plane, nz), F32)] * 2
        + [work((wide, tall, nz), F32), work((ny, nz), F32), work((cols, cx, cy, nz), F32)],
        (flags, sums, x, ylo, yhi, xlo, xhi, clo, chi), "pre", smem=1,
    )

    cylo, cyhi = from_low(to_yhi, "gy"), from_high(to_ylo, "gy")
    to_xlo, to_xhi = call(
        coarse_pack_kernel, [shape(half * CO * (cy + 2 * CO), nz)] * 2, [], (c, cylo, cyhi), "cpack"
    )
    cxlo, cxhi = from_low(to_xhi, "gx"), from_high(to_xlo, "gx")
    cwide = cx + 2 * CO
    corr, to_ylo, to_yhi = call(
        coarse_kernel,
        [shape(cols, nx, ny, nz)] + [shape(cols, nx * POST, nz)] * 2,
        [work((cwide, PAD + 16 + 8, nz), F32)] * 2
        + [work((cwide, 16, nz), F32), work((ny, nz), F32)],
        (flags, c, cylo, cyhi, cxlo, cxhi, e), "coarse", smem=1,
    )

    eylo, eyhi = from_low(to_yhi, "gy"), from_high(to_ylo, "gy")
    to_xlo, to_xhi = call(
        post_pack_kernel, [shape(cols, POST * (ny + 2 * POST), nz)] * 2, [], (corr, eylo, eyhi), "ppack"
    )
    exlo, exhi = from_low(to_xhi, "gx"), from_high(to_xlo, "gx")

    image_x, image_p = call(
        image_kernel, [shape(cols, nx, ny, nz)] * 2,
        [work((nx + 2, PAD + ny + 8, nz), F32)],
        (x, p, ylo, yhi, xlo, xhi), "image",
    )
    w, image_w = call(
        post_kernel, [shape(cols, nx, ny, nz)] * 2,
        [work((nx + 2 * POST, plane, nz), F32)] * 2,
        (flags, corr, eylo, eyhi, exlo, exhi, r), "post", smem=1,
    )

    basis = jnp.concatenate([x, w, p], axis=0)
    images = jnp.concatenate([image_x, image_w, image_p], axis=0)
    both = jnp.concatenate([basis, images], axis=0)
    part = jnp.einsum("kxyz,lxyz->kl", basis, both, precision=hp)
    part = sum_all(part)
    nb = 3 * cols
    coef = ritz_coef(part[:, :nb], part[:, nb:], nx * ny * nz * devices)
    new_search = jnp.einsum("lk,lxyz->kxyz", coef[cols:], basis[cols:], precision=hp)
    new_block = new_search + jnp.einsum("lk,lxyz->kxyz", coef[:cols], x, precision=hp)
    return (new_block, new_search)


def solution(mesh):
    spec = P(None, "gx", "gy", None)
    return jax.shard_map(
        body, mesh=mesh, in_specs=(spec, spec), out_specs=(spec, spec), check_vma=False
    )
```

```python
import functools

import jax
import jax.numpy as jnp
from jax import lax
from jax.experimental import pallas as pl
from jax.experimental.pallas import tpu as pltpu
from jax.sharding import PartitionSpec as P

RELAX = 1.0 / 9.0
COARSE_RELAX = 1.0 / 36.0
SHIFT = 13.0
DEEP = 4
POST = 3
CO = 3
PAD = 8

F32 = jnp.float32
VMEM = pl.BlockSpec(memory_space=pltpu.VMEM)
SMEM = pl.BlockSpec(memory_space=pltpu.SMEM)


def shape(*dims):
    return jax.ShapeDtypeStruct(dims, F32)


def call(kernel, outs, scratch, args, name, smem=0):
    specs = [SMEM] * smem + [VMEM] * (len(args) - smem)
    return pl.pallas_call(
        kernel,
        out_shape=outs,
        in_specs=specs,
        out_specs=[VMEM] * len(outs),
        scratch_shapes=scratch,
        name=name,
    )(*args)


def along_z(plane, step, lanes):
    size = plane.shape[-1]
    low = jnp.where(lanes >= step, pltpu.roll(plane, step, 1), 0.0)
    high = jnp.where(lanes < size - step, pltpu.roll(plane, size - step, 1), 0.0)
    return low + high


def beside(work, i, row, rows, center, before, after, lanes, step=1):
    total = before + after
    total = total + work[i, pl.ds(row - 1, rows), :] + work[i, pl.ds(row + 1, rows), :]
    return total + along_z(center, step, lanes)


def dot_nt(a, b):
    return lax.dot_general(
        a, b, (((1,), (1,)), ((), ())),
        precision=lax.Precision.HIGHEST, preferred_element_type=F32,
    )


def lane_index(rows):
    return lax.broadcasted_iota(jnp.int32, (rows, 128), 1)


def pack_kernel(x_ref, p_ref, ylo, yhi, xlo, xhi):
    cols, nx, ny, _ = x_ref.shape

    def body(f, carry):
        for i in range(nx):
            ylo[f, pl.ds(i * DEEP, DEEP), :] = x_ref[f, i, pl.ds(0, DEEP), :]
            yhi[f, pl.ds(i * DEEP, DEEP), :] = x_ref[f, i, pl.ds(ny - DEEP, DEEP), :]
            ylo[f, pl.ds(nx * DEEP + i, 1), :] = p_ref[f, i, pl.ds(0, 1), :]
            yhi[f, pl.ds(nx * DEEP + i, 1), :] = p_ref[f, i, pl.ds(ny - 1, 1), :]
        for i in range(DEEP):
            xlo[f, i] = x_ref[f, i]
            xhi[f, i] = x_ref[f, nx - DEEP + i]
        xlo[f, DEEP] = p_ref[f, 0]
        xhi[f, DEEP] = p_ref[f, nx - 1]
        return carry

    lax.fori_loop(0, cols, body, 0)


def theta_kernel(x_ref, ylo, yhi, xlo, xhi, out_ref, clo, chi, work, parts):
    cols, nx, ny, _ = x_ref.shape
    lanes = lane_index(ny)
    half = nx // 2 * DEEP
    parts[pl.ds(2 * cols * 8, 128 * 8 - 2 * cols * 8), :] = jnp.ones((128 * 8 - 2 * cols * 8, 128), F32)

    def body(f, carry):
        work[0, pl.ds(PAD, ny), :] = xlo[f, DEEP - 1]
        work[nx + 1, pl.ds(PAD, ny), :] = xhi[f, 0]
        for i in range(nx):
            work[i + 1, pl.ds(PAD, ny), :] = x_ref[f, i]
            work[i + 1, pl.ds(PAD - 1, 1), :] = ylo[f, pl.ds(i * DEEP + DEEP - 1, 1), :]
            work[i + 1, pl.ds(PAD + ny, 1), :] = yhi[f, pl.ds(i * DEEP, 1), :]
        numer = jnp.zeros((ny, 128), F32)
        denom = jnp.zeros((ny, 128), F32)
        before = work[0, pl.ds(PAD, ny), :]
        center = work[1, pl.ds(PAD, ny), :]
        for i in range(nx):
            after = work[i + 2, pl.ds(PAD, ny), :]
            image = 6.0 * center - beside(work, i + 1, PAD, ny, center, before, after, lanes)
            numer = numer + center * image
            denom = denom + center * center
            before, center = center, after
        parts[pl.ds(pl.multiple_of(f * 8, 8), 8), :] = numer[0:8] + numer[8:16]
        parts[pl.ds(pl.multiple_of((cols + f) * 8, 8), 8), :] = denom[0:8] + denom[8:16]
        clo[f, pl.ds(0, half), :] = ylo[f, pl.ds(0, half), :]
        clo[f, pl.ds(half, half), :] = yhi[f, pl.ds(0, half), :]
        chi[f, pl.ds(0, half), :] = ylo[f, pl.ds(half, half), :]
        chi[f, pl.ds(half, half), :] = yhi[f, pl.ds(half, half), :]
        return carry

    lax.fori_loop(0, cols, body, 0)
    total = parts[pl.ds(0, 128, stride=8), :]
    for k in range(1, 8):
        total = total + parts[pl.ds(k, 128, stride=8), :]
    sums = dot_nt(jnp.ones((8, 128), F32), total)

    def spread(k, carry):
        out_ref[k] = sums
        return carry

    lax.fori_loop(0, out_ref.shape[0], spread, 0)


def pre_kernel(
    flags, sums, x_ref, ylo, yhi, xlo, xhi, clo, chi,
    r_ref, e_ref, c_ref, slo, shi,
    work, other, rhs, small, coarse,
):
    cols, nx, ny, _ = x_ref.shape
    tall = ny + 2 * DEEP
    wide = nx + 2 * DEEP
    lanes = lane_index(tall)
    own = lane_index(ny)
    spot = lane_index(8)
    has = [flags[k].astype(F32) for k in range(4)]
    row = lax.broadcasted_iota(jnp.int32, (tall, 128), 0)
    mask_y = RELAX * jnp.where(row < DEEP, has[2], jnp.where(row >= ny + DEEP, has[3], 1.0))

    def relax_of(i):
        if i < DEEP:
            return mask_y * has[0]
        if i >= nx + DEEP:
            return mask_y * has[1]
        return mask_y

    total = sums[0]
    for k in range(1, sums.shape[0]):
        total = total + sums[k]
    theta = total / pltpu.roll(total, 128 - cols, 1)

    @pl.when(jnp.bool_(True))
    def _():
        zero = jnp.zeros((8, 128), F32)
        for i in range(wide):
            for buf in (work, other):
                buf[i, pl.ds(0, PAD), :] = zero
                buf[i, pl.ds(PAD + tall, 8), :] = zero

    data = pl.ds(PAD, tall)

    def body(f, carry):
        th = jnp.sum(jnp.where(spot == f, theta, 0.0)) * 0.125
        for i in range(DEEP):
            lo, hi = i, nx + DEEP + i
            work[lo, pl.ds(PAD + DEEP, ny), :] = xlo[f, i]
            work[hi, pl.ds(PAD + DEEP, ny), :] = xhi[f, i]
            for plane, buf in ((lo, clo), (hi, chi)):
                work[plane, pl.ds(PAD, DEEP), :] = buf[f, pl.ds(i * DEEP, DEEP), :]
                work[plane, pl.ds(PAD + DEEP + ny, DEEP), :] = buf[
                    f, pl.ds(DEEP * DEEP + i * DEEP, DEEP), :
                ]
        for i in range(nx):
            work[i + DEEP, pl.ds(PAD + DEEP, ny), :] = x_ref[f, i]
            work[i + DEEP, pl.ds(PAD, DEEP), :] = ylo[f, pl.ds(i * DEEP, DEEP), :]
            work[i + DEEP, pl.ds(PAD + DEEP + ny, DEEP), :] = yhi[f, pl.ds(i * DEEP, DEEP), :]
        before = work[0, data, :]
        center = work[1, data, :]
        for i in range(1, wide - 1):
            after = work[i + 1, data, :]
            image = 6.0 * center - beside(work, i, PAD, tall, center, before, after, lanes)
            res = image - th * center
            rhs[i] = res
            other[i, data, :] = relax_of(i) * res
            before, center = center, after
        src, dst = other, work
        for depth in (2, 3):
            before = src[depth - 1, data, :]
            center = src[depth, data, :]
            for i in range(depth, wide - depth):
                after = src[i + 1, data, :]
                near = beside(src, i, PAD, tall, center, before, after, lanes)
                dst[i, data, :] = center + relax_of(i) * (rhs[i] - 6.0 * center + near)
                before, center = center, after
            src, dst = dst, src
        own_rows = pl.ds(PAD + DEEP, ny)
        before = src[DEEP - 1, own_rows, :]
        center = src[DEEP, own_rows, :]
        held = None
        for i in range(DEEP, nx + DEEP):
            after = src[i + 1, own_rows, :]
            near = beside(src, i, PAD + DEEP, ny, center, before, after, own)
            rest = rhs[i, pl.ds(DEEP, ny), :] - 6.0 * center + near
            e_ref[f, i - DEEP] = center
            if held is None:
                held = rest
            else:
                small[...] = held + rest
                pair = small[pl.ds(0, ny // 2, stride=2), :] + small[pl.ds(1, ny // 2, stride=2), :]
                mate = jnp.where(
                    spot % 2 == 0, pltpu.roll(pair, 127, 1), pltpu.roll(pair, 1, 1)
                )
                coarse[f, (i - DEEP) // 2] = pair + mate
                held = None
            before, center = center, after
        for i in range(2, wide - 2):
            r_ref[f, i - 2] = rhs[i]
        return carry

    lax.fori_loop(0, cols, body, 0)
    half, cx, cy = cols // 2, nx // 2, ny // 2
    even = spot % 2 == 0
    for g in range(half):
        for i in range(cx):
            both = jnp.where(even, coarse[g, i], coarse[g + half, i])
            c_ref[g, i] = both
            small[pl.ds(0, 8), :] = both
            at = (g * cx + i) * CO
            slo[pl.ds(at, CO), :] = small[pl.ds(0, CO), :]
            shi[pl.ds(at, CO), :] = small[pl.ds(cy - CO, CO), :]


def coarse_pack_kernel(c_ref, ylo, yhi, xlo, xhi):
    half, cx, cy, _ = c_ref.shape
    tall = cy + 2 * CO
    for g in range(half):
        for out, first in ((xlo, 0), (xhi, cx - CO)):
            for i in range(CO):
                at = (g * CO + i) * tall
                src = (g * cx + first + i) * CO
                out[pl.ds(at, CO), :] = ylo[pl.ds(src, CO), :]
                out[pl.ds(at + CO, cy), :] = c_ref[g, first + i]
                out[pl.ds(at + CO + cy, CO), :] = yhi[pl.ds(src, CO), :]


def coarse_kernel(
    flags, c_ref, ylo, yhi, xlo, xhi, e_ref, corr_ref, slo, shi, work, other, rhs, small
):
    half, cx, cy, _ = c_ref.shape
    cols, nx, ny, _ = e_ref.shape
    tall = cy + 2 * CO
    full = 16
    wide = cx + 2 * CO
    lanes = lane_index(full)
    spot = lane_index(8)
    odd = spot % 2 == 1
    has = [flags[k].astype(F32) for k in range(4)]
    row = lax.broadcasted_iota(jnp.int32, (full, 128), 0)
    mask_y = COARSE_RELAX * jnp.where(row < CO, has[2], jnp.where(row >= cy + CO, has[3], 1.0))
    zero = jnp.zeros((8, 128), F32)
    for i in range(wide):
        rhs[i, pl.ds(8, 8), :] = zero
        for buf in (work, other):
            buf[i, pl.ds(0, PAD), :] = zero
            buf[i, pl.ds(PAD + full, 8), :] = zero

    def relax_of(i):
        if i < CO:
            return mask_y * has[0]
        if i >= cx + CO:
            return mask_y * has[1]
        return mask_y

    data = pl.ds(PAD, full)

    def body(g, carry):
        for i in range(CO):
            rhs[i, pl.ds(0, tall), :] = xlo[pl.ds((g * CO + i) * tall, tall), :]
            rhs[cx + CO + i, pl.ds(0, tall), :] = xhi[pl.ds((g * CO + i) * tall, tall), :]
        for i in range(cx):
            at = pl.ds((g * cx + i) * CO, CO)
            rhs[i + CO, pl.ds(0, CO), :] = ylo[at, :]
            rhs[i + CO, pl.ds(CO, cy), :] = c_ref[g, i]
            rhs[i + CO, pl.ds(CO + cy, CO), :] = yhi[at, :]
        for i in range(wide):
            work[i, data, :] = relax_of(i) * rhs[i]
        src, dst = work, other
        for depth in (1, 2, 3):
            before = src[depth - 1, data, :]
            center = src[depth, data, :]
            for i in range(depth, wide - depth):
                after = src[i + 1, data, :]
                near = beside(src, i, PAD, full, center, before, after, lanes, 2)
                dst[i, data, :] = center + relax_of(i) * (rhs[i] - 4.0 * (6.0 * center - near))
                before, center = center, after
            src, dst = dst, src
        for i in range(cx):
            both = src[i + CO, pl.ds(PAD + CO, cy), :]
            first = jnp.where(odd, pltpu.roll(both, 1, 1), both)
            second = jnp.where(odd, both, pltpu.roll(both, 127, 1))
            for f, value in ((g, first), (g + half, second)):
                small[pl.ds(0, cy, stride=2), :] = value
                small[pl.ds(1, cy, stride=2), :] = value
                for k in (2 * i, 2 * i + 1):
                    corr = e_ref[f, k] + small[...]
                    corr_ref[f, k] = corr
                    slo[f, pl.ds(k * POST, POST), :] = corr_ref[f, k, pl.ds(0, POST), :]
                    shi[f, pl.ds(k * POST, POST), :] = corr_ref[f, k, pl.ds(ny - POST, POST), :]
        return carry

    lax.fori_loop(0, half, body, 0)


def post_pack_kernel(corr_ref, ylo, yhi, xlo, xhi):
    cols, nx, ny, _ = corr_ref.shape
    tall = ny + 2 * POST

    def body(f, carry):
        for out, first in ((xlo, 0), (xhi, nx - POST)):
            for i in range(POST):
                at = (f * POST + i) * tall
                src = pl.ds((first + i) * POST, POST)
                out[pl.ds(at, POST), :] = ylo[f, src, :]
                out[pl.ds(at + POST, ny), :] = corr_ref[f, first + i]
                out[pl.ds(at + POST + ny, POST), :] = yhi[f, src, :]
        return carry

    lax.fori_loop(0, cols, body, 0)


def post_kernel(
    flags, corr_ref, ylo, yhi, xlo, xhi, r_ref, w_ref, image_ref, work, other
):
    cols, nx, ny, _ = corr_ref.shape
    tall = ny + 2 * DEEP
    wide = nx + 2 * POST
    span = ny + 2 * POST
    gap = DEEP - POST
    lanes = lane_index(tall)
    own = lane_index(ny)
    has = [flags[k].astype(F32) for k in range(4)]
    row = lax.broadcasted_iota(jnp.int32, (tall, 128), 0)
    mask_y = RELAX * jnp.where(row < DEEP, has[2], jnp.where(row >= ny + DEEP, has[3], 1.0))
    zero = jnp.zeros((PAD + 8, 128), F32)
    for i in range(wide):
        for buf in (work, other):
            buf[i, pl.ds(0, PAD + 8), :] = zero
            buf[i, pl.ds(PAD + tall - 8, 16), :] = zero

    def relax_of(i):
        if i < POST:
            return mask_y * has[0]
        if i >= nx + POST:
            return mask_y * has[1]
        return mask_y

    data = pl.ds(PAD, tall)

    def body(f, carry):
        for i in range(POST):
            at = pl.ds((f * POST + i) * span, span)
            work[i, pl.ds(PAD + gap, span), :] = xlo[at, :]
            work[nx + POST + i, pl.ds(PAD + gap, span), :] = xhi[at, :]
        for i in range(nx):
            at = pl.ds(i * POST, POST)
            work[i + POST, pl.ds(PAD + gap, POST), :] = ylo[f, at, :]
            work[i + POST, pl.ds(PAD + DEEP, ny), :] = corr_ref[f, i]
            work[i + POST, pl.ds(PAD + DEEP + ny, POST), :] = yhi[f, at, :]
        src, dst = work, other
        for depth in (1, 2):
            before = src[depth - 1, data, :]
            center = src[depth, data, :]
            for i in range(depth, wide - depth):
                after = src[i + 1, data, :]
                near = beside(src, i, PAD, tall, center, before, after, lanes)
                dst[i, data, :] = center + relax_of(i) * (r_ref[f, i - 1] - 6.0 * center + near)
                before, center = center, after
            src, dst = dst, src
        own_rows = pl.ds(PAD + DEEP, ny)
        before = src[POST - 1, own_rows, :]
        center = src[POST, own_rows, :]
        for i in range(POST, nx + POST):
            after = src[i + 1, own_rows, :]
            near = beside(src, i, PAD + DEEP, ny, center, before, after, own)
            w_ref[f, i - POST] = center
            image_ref[f, i - POST] = 6.0 * center - near
            before, center = center, after
        return carry

    lax.fori_loop(0, cols, body, 0)


def image_kernel(x_ref, p_ref, ylo, yhi, xlo, xhi, ax_ref, ap_ref, work):
    cols, nx, ny, _ = x_ref.shape
    lanes = lane_index(ny)

    def body(f, carry):
        for ref, out, lo, hi, base, deep in (
            (x_ref, ax_ref, DEEP - 1, 0, 0, DEEP),
            (p_ref, ap_ref, DEEP, DEEP, nx * DEEP, 1),
        ):
            work[0, pl.ds(PAD, ny), :] = xlo[f, lo]
            work[nx + 1, pl.ds(PAD, ny), :] = xhi[f, hi]
            for i in range(nx):
                work[i + 1, pl.ds(PAD, ny), :] = ref[f, i]
                work[i + 1, pl.ds(PAD - 1, 1), :] = ylo[f, pl.ds(base + i * deep + deep - 1, 1), :]
                work[i + 1, pl.ds(PAD + ny, 1), :] = yhi[f, pl.ds(base + i * deep, 1), :]
            before = work[0, pl.ds(PAD, ny), :]
            center = work[1, pl.ds(PAD, ny), :]
            for i in range(nx):
                after = work[i + 2, pl.ds(PAD, ny), :]
                near = beside(work, i + 1, PAD, ny, center, before, after, lanes)
                out[f, i] = 6.0 * center - near
                before, center = center, after
        return carry

    lax.fori_loop(0, cols, body, 0)


def from_low(value, axis):
    count = lax.axis_size(axis)
    return lax.ppermute(value, axis, [(i, i + 1) for i in range(count - 1)])


def from_high(value, axis):
    count = lax.axis_size(axis)
    return lax.ppermute(value, axis, [(i + 1, i) for i in range(count - 1)])


def radices(count):
    out = []
    if count % 2 == 0 and count % 4 == 0 and (count.bit_length() - 1) % 2 == 1:
        out.append(2)
        count //= 2
    while count % 4 == 0:
        out.append(4)
        count //= 4
    if count > 1:
        out.append(count)
    return out


def sum_all(value):
    for axis in ("gx", "gy"):
        count = lax.axis_size(axis)
        stride = 1
        for radix in radices(count):
            index = lax.axis_index(axis)
            parts = [value]
            for k in range(1, radix):
                pairs = []
                for i in range(count):
                    digit = i // stride % radix
                    target = i + ((digit + k) % radix - digit) * stride
                    pairs.append((i, target))
                parts.append(lax.ppermute(value, axis, pairs))
            digit = index // stride % radix
            if radix == 2:
                value = parts[0] + parts[1]
            elif radix == 4:
                even = parts[0] + parts[2]
                odd = parts[1] + parts[3]
                value = even + odd
            else:
                value = functools.reduce(jnp.add, parts)
            stride *= radix
    return value


BF16 = jnp.bfloat16


def gram_kernel(x_ref, w_ref, p_ref, ax_ref, aw_ref, ap_ref, out_ref, s_ref, image):
    chunks, rows, wide = s_ref.shape
    cols = rows // 6
    ny = wide // 128
    stride = x_ref.shape[0] // cols

    def body(c, carry):
        for k, (b_ref, a_ref) in enumerate(((x_ref, ax_ref), (w_ref, aw_ref), (p_ref, ap_ref))):
            for y in range(ny):
                pick = pl.ds(c * ny + y, cols, stride=stride)
                at = pl.ds(y * 128, 128)
                for ref, put in (
                    (b_ref, lambda r, v: s_ref.__setitem__((c, r, at), v)),
                    (a_ref, lambda r, v: image.__setitem__((r, at), v)),
                ):
                    value = ref[pick, :]
                    high = value.astype(BF16)
                    low = (value - high.astype(F32)).astype(BF16)
                    put(pl.ds(k * cols, cols), high)
                    put(pl.ds((3 + k) * cols, cols), low)
        left = s_ref[c]
        dims = (((1,), (1,)), ((), ()))
        proj = lax.dot_general(left, image[...], dims, preferred_element_type=F32)
        gram = lax.dot_general(left, left, dims, preferred_element_type=F32)
        return (carry[0] + proj, carry[1] + gram)

    zero = jnp.zeros((rows, rows), F32)
    proj, gram = lax.fori_loop(0, chunks, body, (zero, zero))
    nb = 3 * cols
    for k, full in enumerate((proj, gram)):
        full = full[:nb] + full[nb:]
        out_ref[:, pl.ds(k * nb, nb)] = full[:, :nb] + full[:, nb:]


def eliminate(left, right, first):
    size = left.shape[0]
    row = lax.broadcasted_iota(jnp.int32, (size, 1), 0)
    scale = jnp.zeros((size, 1), F32)
    for k in range(size):
        pivot = left[k : k + 1, first + k : first + k + 1]
        column = left[:, first + k : first + k + 1]
        factor = jnp.where(row > k, column / pivot, 0.0)
        scale = jnp.where(row == k, pivot, scale)
        line, other = left[k : k + 1], right[k : k + 1]
        left = left - factor * line
        right = right - factor * other
    scale = lax.rsqrt(scale)
    return left * scale, right * scale


def finish_kernel(ncells, sums_ref, s_ref, block_ref, search_ref, bufs, sems):
    nb = sums_ref.shape[0]
    cols = nb // 3
    chunks, rows, wide = s_ref.shape
    ny = wide // 128
    row = lax.broadcasted_iota(jnp.int32, (nb, 128), 0)
    lane = lax.broadcasted_iota(jnp.int32, (nb, 128), 1)
    eye = jnp.where((lane == row) | (lane == row + nb), 1.0, 0.0)
    left, inverse = eliminate(sums_ref[...], eye, nb)
    flat = -dot_nt(inverse[:cols, :nb], left[:, :nb])
    flat = flat + jnp.where(lane[:cols, :nb] == row[:cols, :nb], SHIFT, 0.0)
    _, scaled = eliminate(dot_nt(flat, flat), flat, 0)
    coef = jnp.dot(
        scaled, inverse, precision=lax.Precision.HIGHEST, preferred_element_type=F32
    )
    coef = coef[:, :rows] * jnp.sqrt(F32(ncells))
    slot = lax.broadcasted_iota(jnp.int32, (cols, rows), 1)
    first = (slot < cols) | ((slot >= nb) & (slot < nb + cols))
    terms = []
    for part in (jnp.where(first, coef, 0.0), jnp.where(first, 0.0, coef)):
        high = part.astype(BF16)
        terms += [high, (part - high.astype(F32)).astype(BF16)]
    terms = jnp.concatenate(terms, axis=0)

    def copies(c, slot):
        return [
            pltpu.make_async_copy(bufs.at[slot, k], ref.at[:, c], sems.at[slot, k])
            for k, ref in enumerate((block_ref, search_ref))
        ]

    for c in range(chunks):
        slot = c % 2
        if c >= 2:
            for copy in copies(c - 2, slot):
                copy.wait()
        for y in range(0, ny, 2):
            got = jnp.dot(
                terms, s_ref[c, :, pl.ds(y * 128, 256)], preferred_element_type=F32
            )
            search = got[2 * cols : 3 * cols] + got[3 * cols :]
            block = search + (got[:cols] + got[cols : 2 * cols])
            for k, value in enumerate((block, search)):
                for j in range(2):
                    bufs[slot, k, :, y + j, :] = value[:, j * 128 : (j + 1) * 128]
        for copy in copies(c, slot):
            copy.start()
    for c in range(max(chunks - 2, 0), chunks):
        for copy in copies(c, c % 2):
            copy.wait()


def body(x, p):
    cols, nx, ny, nz = x.shape
    ngx, ngy = lax.axis_size("gx"), lax.axis_size("gy")
    ix, iy = lax.axis_index("gx"), lax.axis_index("gy")
    flags = jnp.stack([ix > 0, ix < ngx - 1, iy > 0, iy < ngy - 1]).astype(jnp.int32)
    half, cx, cy = cols // 2, nx // 2, ny // 2
    work = pltpu.VMEM

    yrows = nx * DEEP + nx
    to_ylo, to_yhi, to_xlo, to_xhi = call(
        pack_kernel,
        [shape(cols, yrows, nz)] * 2 + [shape(cols, DEEP + 1, ny, nz)] * 2,
        [], (x, p), "pack",
    )
    ylo, yhi = from_low(to_yhi, "gy"), from_high(to_ylo, "gy")
    xlo, xhi = from_low(to_xhi, "gx"), from_high(to_xlo, "gx")

    devices = ngx * ngy
    sums, to_clo, to_chi = call(
        theta_kernel,
        [shape(devices, 8, 128)] + [shape(cols, nx * DEEP, nz)] * 2,
        [work((nx + 2, PAD + ny + 8, nz), F32), work((128 * 8, nz), F32)],
        (x, ylo, yhi, xlo, xhi), "theta",
    )
    clo, chi = from_low(to_chi, "gx"), from_high(to_clo, "gx")
    sums = lax.all_to_all(sums, ("gx", "gy"), 0, 0)

    tall, wide = ny + 2 * DEEP, nx + 2 * DEEP
    plane = PAD + tall + 8
    r, e, c, to_ylo, to_yhi = call(
        pre_kernel,
        [shape(cols, wide - 4, tall, nz), shape(cols, nx, ny, nz), shape(half, cx, cy, nz)]
        + [shape(half * cx * CO, nz)] * 2,
        [work((wide, plane, nz), F32)] * 2
        + [work((wide, tall, nz), F32), work((ny, nz), F32), work((cols, cx, cy, nz), F32)],
        (flags, sums, x, ylo, yhi, xlo, xhi, clo, chi), "pre", smem=1,
    )

    cylo, cyhi = from_low(to_yhi, "gy"), from_high(to_ylo, "gy")
    to_xlo, to_xhi = call(
        coarse_pack_kernel, [shape(half * CO * (cy + 2 * CO), nz)] * 2, [], (c, cylo, cyhi), "cpack"
    )
    cxlo, cxhi = from_low(to_xhi, "gx"), from_high(to_xlo, "gx")
    cwide = cx + 2 * CO
    corr, to_ylo, to_yhi = call(
        coarse_kernel,
        [shape(cols, nx, ny, nz)] + [shape(cols, nx * POST, nz)] * 2,
        [work((cwide, PAD + 16 + 8, nz), F32)] * 2
        + [work((cwide, 16, nz), F32), work((ny, nz), F32)],
        (flags, c, cylo, cyhi, cxlo, cxhi, e), "coarse", smem=1,
    )

    eylo, eyhi = from_low(to_yhi, "gy"), from_high(to_ylo, "gy")
    to_xlo, to_xhi = call(
        post_pack_kernel, [shape(cols * POST * (ny + 2 * POST), nz)] * 2, [], (corr, eylo, eyhi), "ppack"
    )
    exlo, exhi = from_low(to_xhi, "gx"), from_high(to_xlo, "gx")

    image_x, image_p = call(
        image_kernel, [shape(cols, nx, ny, nz)] * 2,
        [work((nx + 2, PAD + ny + 8, nz), F32)],
        (x, p, ylo, yhi, xlo, xhi), "image",
    )
    w, image_w = call(
        post_kernel, [shape(cols, nx, ny, nz)] * 2,
        [work((nx + 2 * POST, plane, nz), F32)] * 2,
        (flags, corr, eylo, eyhi, exlo, exhi, r), "post", smem=1,
    )

    flat = [v.reshape(cols * nx * ny, nz) for v in (x, w, p, image_x, image_w, image_p)]
    nb = 3 * cols
    part, split = call(
        gram_kernel,
        [shape(nb, 128), jax.ShapeDtypeStruct((nx, 2 * nb, ny * nz), BF16)],
        [work((2 * nb, ny * nz), BF16)],
        flat, "gram",
    )
    part = sum_all(part)
    any_space = pl.BlockSpec(memory_space=pl.ANY)
    new_block, new_search = pl.pallas_call(
        functools.partial(finish_kernel, nx * ny * nz * devices),
        out_shape=[shape(cols, nx, ny, nz)] * 2,
        in_specs=[VMEM, VMEM],
        out_specs=[any_space] * 2,
        scratch_shapes=[
            work((2, 2, cols, ny, nz), F32),
            pltpu.SemaphoreType.DMA((2, 2)),
        ],
        name="finish",
    )(part, split)
    return (new_block, new_search)


def solution(mesh):
    spec = P(None, "gx", "gy", None)
    return jax.shard_map(
        body, mesh=mesh, in_specs=(spec, spec), out_specs=(spec, spec), check_vma=False
    )
```

```python
import functools

import jax
import jax.numpy as jnp
from jax import lax
from jax.experimental import pallas as pl
from jax.experimental.pallas import tpu as pltpu
from jax.sharding import PartitionSpec as P

RELAX = 1.0 / 9.0
COARSE_RELAX = 1.0 / 36.0
SHIFT = 13.0
DEEP = 4
POST = 3
CO = 3
PAD = 8

GRANT = 20 << 20

F32 = jnp.float32
VMEM = pl.BlockSpec(memory_space=pltpu.VMEM)
SMEM = pl.BlockSpec(memory_space=pltpu.SMEM)


def shape(*dims):
    return pltpu.VMEM(dims, F32)


def call(kernel, outs, scratch, args, name, smem=0):
    specs = [SMEM] * smem + [VMEM] * (len(args) - smem)
    return pl.pallas_call(
        kernel,
        out_shape=outs,
        in_specs=specs,
        out_specs=[VMEM] * len(outs),
        scratch_shapes=scratch,
        compiler_params=pltpu.CompilerParams(vmem_limit_bytes=GRANT),
        name=name,
    )(*args)


def along_z(plane, step, lanes):
    size = plane.shape[-1]
    low = jnp.where(lanes >= step, pltpu.roll(plane, step, 1), 0.0)
    high = jnp.where(lanes < size - step, pltpu.roll(plane, size - step, 1), 0.0)
    return low + high


def beside(work, i, row, rows, center, before, after, lanes, step=1):
    total = before + after
    total = total + work[i, pl.ds(row - 1, rows), :] + work[i, pl.ds(row + 1, rows), :]
    return total + along_z(center, step, lanes)


def dot_nt(a, b):
    return lax.dot_general(
        a, b, (((1,), (1,)), ((), ())),
        precision=lax.Precision.HIGHEST, preferred_element_type=F32,
    )


def lane_index(rows):
    return lax.broadcasted_iota(jnp.int32, (rows, 128), 1)


def pack_kernel(x_ref, p_ref, ylo, yhi, xlo, xhi):
    cols, nx, ny, _ = x_ref.shape

    def body(f, carry):
        for i in range(nx):
            ylo[f, pl.ds(i * DEEP, DEEP), :] = x_ref[f, i, pl.ds(0, DEEP), :]
            yhi[f, pl.ds(i * DEEP, DEEP), :] = x_ref[f, i, pl.ds(ny - DEEP, DEEP), :]
            ylo[f, pl.ds(nx * DEEP + i, 1), :] = p_ref[f, i, pl.ds(0, 1), :]
            yhi[f, pl.ds(nx * DEEP + i, 1), :] = p_ref[f, i, pl.ds(ny - 1, 1), :]
        for i in range(DEEP):
            xlo[f, i] = x_ref[f, i]
            xhi[f, i] = x_ref[f, nx - DEEP + i]
        xlo[f, DEEP] = p_ref[f, 0]
        xhi[f, DEEP] = p_ref[f, nx - 1]
        return carry

    lax.fori_loop(0, cols, body, 0)


def theta_kernel(x_ref, ylo, yhi, xlo, xhi, out_ref, clo, chi, work, parts):
    cols, nx, ny, _ = x_ref.shape
    lanes = lane_index(ny)
    half = nx // 2 * DEEP
    parts[pl.ds(2 * cols * 8, 128 * 8 - 2 * cols * 8), :] = jnp.ones((128 * 8 - 2 * cols * 8, 128), F32)

    def body(f, carry):
        work[0, pl.ds(PAD, ny), :] = xlo[f, DEEP - 1]
        work[nx + 1, pl.ds(PAD, ny), :] = xhi[f, 0]
        for i in range(nx):
            work[i + 1, pl.ds(PAD, ny), :] = x_ref[f, i]
            work[i + 1, pl.ds(PAD - 1, 1), :] = ylo[f, pl.ds(i * DEEP + DEEP - 1, 1), :]
            work[i + 1, pl.ds(PAD + ny, 1), :] = yhi[f, pl.ds(i * DEEP, 1), :]
        numer = jnp.zeros((ny, 128), F32)
        denom = jnp.zeros((ny, 128), F32)
        before = work[0, pl.ds(PAD, ny), :]
        center = work[1, pl.ds(PAD, ny), :]
        for i in range(nx):
            after = work[i + 2, pl.ds(PAD, ny), :]
            image = 6.0 * center - beside(work, i + 1, PAD, ny, center, before, after, lanes)
            numer = numer + center * image
            denom = denom + center * center
            before, center = center, after
        parts[pl.ds(pl.multiple_of(f * 8, 8), 8), :] = numer[0:8] + numer[8:16]
        parts[pl.ds(pl.multiple_of((cols + f) * 8, 8), 8), :] = denom[0:8] + denom[8:16]
        clo[f, pl.ds(0, half), :] = ylo[f, pl.ds(0, half), :]
        clo[f, pl.ds(half, half), :] = yhi[f, pl.ds(0, half), :]
        chi[f, pl.ds(0, half), :] = ylo[f, pl.ds(half, half), :]
        chi[f, pl.ds(half, half), :] = yhi[f, pl.ds(half, half), :]
        return carry

    lax.fori_loop(0, cols, body, 0)
    total = parts[pl.ds(0, 128, stride=8), :]
    for k in range(1, 8):
        total = total + parts[pl.ds(k, 128, stride=8), :]
    sums = dot_nt(jnp.ones((8, 128), F32), total)

    def spread(k, carry):
        out_ref[k] = sums
        return carry

    lax.fori_loop(0, out_ref.shape[0], spread, 0)


def pre_kernel(
    flags, sums, x_ref, ylo, yhi, xlo, xhi, clo, chi,
    r_ref, e_ref, c_ref, slo, shi,
    work, other, rhs, small, coarse,
):
    cols, nx, ny, _ = x_ref.shape
    tall = ny + 2 * DEEP
    wide = nx + 2 * DEEP
    lanes = lane_index(tall)
    own = lane_index(ny)
    spot = lane_index(8)
    has = [flags[k].astype(F32) for k in range(4)]
    row = lax.broadcasted_iota(jnp.int32, (tall, 128), 0)
    mask_y = RELAX * jnp.where(row < DEEP, has[2], jnp.where(row >= ny + DEEP, has[3], 1.0))

    def relax_of(i):
        if i < DEEP:
            return mask_y * has[0]
        if i >= nx + DEEP:
            return mask_y * has[1]
        return mask_y

    total = sums[0]
    for k in range(1, sums.shape[0]):
        total = total + sums[k]
    theta = total / pltpu.roll(total, 128 - cols, 1)

    @pl.when(jnp.bool_(True))
    def _():
        zero = jnp.zeros((8, 128), F32)
        for i in range(wide):
            for buf in (work, other):
                buf[i, pl.ds(0, PAD), :] = zero
                buf[i, pl.ds(PAD + tall, 8), :] = zero

    data = pl.ds(PAD, tall)

    def body(f, carry):
        th = jnp.sum(jnp.where(spot == f, theta, 0.0)) * 0.125
        for i in range(DEEP):
            lo, hi = i, nx + DEEP + i
            work[lo, pl.ds(PAD + DEEP, ny), :] = xlo[f, i]
            work[hi, pl.ds(PAD + DEEP, ny), :] = xhi[f, i]
            for plane, buf in ((lo, clo), (hi, chi)):
                work[plane, pl.ds(PAD, DEEP), :] = buf[f, pl.ds(i * DEEP, DEEP), :]
                work[plane, pl.ds(PAD + DEEP + ny, DEEP), :] = buf[
                    f, pl.ds(DEEP * DEEP + i * DEEP, DEEP), :
                ]
        for i in range(nx):
            work[i + DEEP, pl.ds(PAD + DEEP, ny), :] = x_ref[f, i]
            work[i + DEEP, pl.ds(PAD, DEEP), :] = ylo[f, pl.ds(i * DEEP, DEEP), :]
            work[i + DEEP, pl.ds(PAD + DEEP + ny, DEEP), :] = yhi[f, pl.ds(i * DEEP, DEEP), :]
        before = work[0, data, :]
        center = work[1, data, :]
        for i in range(1, wide - 1):
            after = work[i + 1, data, :]
            image = 6.0 * center - beside(work, i, PAD, tall, center, before, after, lanes)
            res = image - th * center
            rhs[i] = res
            other[i, data, :] = relax_of(i) * res
            before, center = center, after
        src, dst = other, work
        for depth in (2, 3):
            before = src[depth - 1, data, :]
            center = src[depth, data, :]
            for i in range(depth, wide - depth):
                after = src[i + 1, data, :]
                near = beside(src, i, PAD, tall, center, before, after, lanes)
                dst[i, data, :] = center + relax_of(i) * (rhs[i] - 6.0 * center + near)
                before, center = center, after
            src, dst = dst, src
        own_rows = pl.ds(PAD + DEEP, ny)
        before = src[DEEP - 1, own_rows, :]
        center = src[DEEP, own_rows, :]
        held = None
        for i in range(DEEP, nx + DEEP):
            after = src[i + 1, own_rows, :]
            near = beside(src, i, PAD + DEEP, ny, center, before, after, own)
            rest = rhs[i, pl.ds(DEEP, ny), :] - 6.0 * center + near
            e_ref[f, i - DEEP] = center
            if held is None:
                held = rest
            else:
                small[...] = held + rest
                pair = small[pl.ds(0, ny // 2, stride=2), :] + small[pl.ds(1, ny // 2, stride=2), :]
                mate = jnp.where(
                    spot % 2 == 0, pltpu.roll(pair, 127, 1), pltpu.roll(pair, 1, 1)
                )
                coarse[f, (i - DEEP) // 2] = pair + mate
                held = None
            before, center = center, after
        for i in range(2, wide - 2):
            r_ref[f, i - 2] = rhs[i]
        return carry

    lax.fori_loop(0, cols, body, 0)
    half, cx, cy = cols // 2, nx // 2, ny // 2
    even = spot % 2 == 0
    for g in range(half):
        for i in range(cx):
            both = jnp.where(even, coarse[g, i], coarse[g + half, i])
            c_ref[g, i] = both
            small[pl.ds(0, 8), :] = both
            at = (g * cx + i) * CO
            slo[pl.ds(at, CO), :] = small[pl.ds(0, CO), :]
            shi[pl.ds(at, CO), :] = small[pl.ds(cy - CO, CO), :]


def coarse_pack_kernel(c_ref, ylo, yhi, xlo, xhi):
    half, cx, cy, _ = c_ref.shape
    tall = cy + 2 * CO
    for g in range(half):
        for out, first in ((xlo, 0), (xhi, cx - CO)):
            for i in range(CO):
                at = (g * CO + i) * tall
                src = (g * cx + first + i) * CO
                out[pl.ds(at, CO), :] = ylo[pl.ds(src, CO), :]
                out[pl.ds(at + CO, cy), :] = c_ref[g, first + i]
                out[pl.ds(at + CO + cy, CO), :] = yhi[pl.ds(src, CO), :]


def coarse_kernel(
    flags, c_ref, ylo, yhi, xlo, xhi, e_ref, corr_ref, slo, shi, work, other, rhs, small
):
    half, cx, cy, _ = c_ref.shape
    cols, nx, ny, _ = e_ref.shape
    tall = cy + 2 * CO
    full = 16
    wide = cx + 2 * CO
    lanes = lane_index(full)
    spot = lane_index(8)
    odd = spot % 2 == 1
    has = [flags[k].astype(F32) for k in range(4)]
    row = lax.broadcasted_iota(jnp.int32, (full, 128), 0)
    mask_y = COARSE_RELAX * jnp.where(row < CO, has[2], jnp.where(row >= cy + CO, has[3], 1.0))
    zero = jnp.zeros((8, 128), F32)
    for i in range(wide):
        rhs[i, pl.ds(8, 8), :] = zero
        for buf in (work, other):
            buf[i, pl.ds(0, PAD), :] = zero
            buf[i, pl.ds(PAD + full, 8), :] = zero

    def relax_of(i):
        if i < CO:
            return mask_y * has[0]
        if i >= cx + CO:
            return mask_y * has[1]
        return mask_y

    data = pl.ds(PAD, full)

    def body(g, carry):
        for i in range(CO):
            rhs[i, pl.ds(0, tall), :] = xlo[pl.ds((g * CO + i) * tall, tall), :]
            rhs[cx + CO + i, pl.ds(0, tall), :] = xhi[pl.ds((g * CO + i) * tall, tall), :]
        for i in range(cx):
            at = pl.ds((g * cx + i) * CO, CO)
            rhs[i + CO, pl.ds(0, CO), :] = ylo[at, :]
            rhs[i + CO, pl.ds(CO, cy), :] = c_ref[g, i]
            rhs[i + CO, pl.ds(CO + cy, CO), :] = yhi[at, :]
        for i in range(wide):
            work[i, data, :] = relax_of(i) * rhs[i]
        src, dst = work, other
        for depth in (1, 2, 3):
            before = src[depth - 1, data, :]
            center = src[depth, data, :]
            for i in range(depth, wide - depth):
                after = src[i + 1, data, :]
                near = beside(src, i, PAD, full, center, before, after, lanes, 2)
                dst[i, data, :] = center + relax_of(i) * (rhs[i] - 4.0 * (6.0 * center - near))
                before, center = center, after
            src, dst = dst, src
        for i in range(cx):
            both = src[i + CO, pl.ds(PAD + CO, cy), :]
            first = jnp.where(odd, pltpu.roll(both, 1, 1), both)
            second = jnp.where(odd, both, pltpu.roll(both, 127, 1))
            for f, value in ((g, first), (g + half, second)):
                small[pl.ds(0, cy, stride=2), :] = value
                small[pl.ds(1, cy, stride=2), :] = value
                for k in (2 * i, 2 * i + 1):
                    corr = e_ref[f, k] + small[...]
                    corr_ref[f, k] = corr
                    slo[f, pl.ds(k * POST, POST), :] = corr_ref[f, k, pl.ds(0, POST), :]
                    shi[f, pl.ds(k * POST, POST), :] = corr_ref[f, k, pl.ds(ny - POST, POST), :]
        return carry

    lax.fori_loop(0, half, body, 0)


def post_pack_kernel(corr_ref, ylo, yhi, xlo, xhi):
    cols, nx, ny, _ = corr_ref.shape
    tall = ny + 2 * POST

    def body(f, carry):
        for out, first in ((xlo, 0), (xhi, nx - POST)):
            for i in range(POST):
                at = (f * POST + i) * tall
                src = pl.ds((first + i) * POST, POST)
                out[pl.ds(at, POST), :] = ylo[f, src, :]
                out[pl.ds(at + POST, ny), :] = corr_ref[f, first + i]
                out[pl.ds(at + POST + ny, POST), :] = yhi[f, src, :]
        return carry

    lax.fori_loop(0, cols, body, 0)


def post_kernel(
    flags, corr_ref, ylo, yhi, xlo, xhi, r_ref, w_ref, image_ref, work, other
):
    cols, nx, ny, _ = corr_ref.shape
    tall = ny + 2 * DEEP
    wide = nx + 2 * POST
    span = ny + 2 * POST
    gap = DEEP - POST
    lanes = lane_index(tall)
    own = lane_index(ny)
    has = [flags[k].astype(F32) for k in range(4)]
    row = lax.broadcasted_iota(jnp.int32, (tall, 128), 0)
    mask_y = RELAX * jnp.where(row < DEEP, has[2], jnp.where(row >= ny + DEEP, has[3], 1.0))
    zero = jnp.zeros((PAD + 8, 128), F32)
    for i in range(wide):
        for buf in (work, other):
            buf[i, pl.ds(0, PAD + 8), :] = zero
            buf[i, pl.ds(PAD + tall - 8, 16), :] = zero

    def relax_of(i):
        if i < POST:
            return mask_y * has[0]
        if i >= nx + POST:
            return mask_y * has[1]
        return mask_y

    data = pl.ds(PAD, tall)

    def body(f, carry):
        for i in range(POST):
            at = pl.ds((f * POST + i) * span, span)
            work[i, pl.ds(PAD + gap, span), :] = xlo[at, :]
            work[nx + POST + i, pl.ds(PAD + gap, span), :] = xhi[at, :]
        for i in range(nx):
            at = pl.ds(i * POST, POST)
            work[i + POST, pl.ds(PAD + gap, POST), :] = ylo[f, at, :]
            work[i + POST, pl.ds(PAD + DEEP, ny), :] = corr_ref[f, i]
            work[i + POST, pl.ds(PAD + DEEP + ny, POST), :] = yhi[f, at, :]
        src, dst = work, other
        for depth in (1, 2):
            before = src[depth - 1, data, :]
            center = src[depth, data, :]
            for i in range(depth, wide - depth):
                after = src[i + 1, data, :]
                near = beside(src, i, PAD, tall, center, before, after, lanes)
                dst[i, data, :] = center + relax_of(i) * (r_ref[f, i - 1] - 6.0 * center + near)
                before, center = center, after
            src, dst = dst, src
        own_rows = pl.ds(PAD + DEEP, ny)
        before = src[POST - 1, own_rows, :]
        center = src[POST, own_rows, :]
        for i in range(POST, nx + POST):
            after = src[i + 1, own_rows, :]
            near = beside(src, i, PAD + DEEP, ny, center, before, after, own)
            w_ref[f, i - POST] = center
            image_ref[f, i - POST] = 6.0 * center - near
            before, center = center, after
        return carry

    lax.fori_loop(0, cols, body, 0)


def image_kernel(x_ref, p_ref, ylo, yhi, xlo, xhi, ax_ref, ap_ref, work):
    cols, nx, ny, _ = x_ref.shape
    lanes = lane_index(ny)

    def body(f, carry):
        for ref, out, lo, hi, base, deep in (
            (x_ref, ax_ref, DEEP - 1, 0, 0, DEEP),
            (p_ref, ap_ref, DEEP, DEEP, nx * DEEP, 1),
        ):
            work[0, pl.ds(PAD, ny), :] = xlo[f, lo]
            work[nx + 1, pl.ds(PAD, ny), :] = xhi[f, hi]
            for i in range(nx):
                work[i + 1, pl.ds(PAD, ny), :] = ref[f, i]
                work[i + 1, pl.ds(PAD - 1, 1), :] = ylo[f, pl.ds(base + i * deep + deep - 1, 1), :]
                work[i + 1, pl.ds(PAD + ny, 1), :] = yhi[f, pl.ds(base + i * deep, 1), :]
            before = work[0, pl.ds(PAD, ny), :]
            center = work[1, pl.ds(PAD, ny), :]
            for i in range(nx):
                after = work[i + 2, pl.ds(PAD, ny), :]
                near = beside(work, i + 1, PAD, ny, center, before, after, lanes)
                out[f, i] = 6.0 * center - near
                before, center = center, after
        return carry

    lax.fori_loop(0, cols, body, 0)


def from_low(value, axis):
    count = lax.axis_size(axis)
    return lax.ppermute(value, axis, [(i, i + 1) for i in range(count - 1)])


def from_high(value, axis):
    count = lax.axis_size(axis)
    return lax.ppermute(value, axis, [(i + 1, i) for i in range(count - 1)])


def radices(count):
    out = []
    if count % 2 == 0 and count % 4 == 0 and (count.bit_length() - 1) % 2 == 1:
        out.append(2)
        count //= 2
    while count % 4 == 0:
        out.append(4)
        count //= 4
    if count > 1:
        out.append(count)
    return out


def sum_all(value):
    for axis in ("gx", "gy"):
        count = lax.axis_size(axis)
        stride = 1
        for radix in radices(count):
            index = lax.axis_index(axis)
            parts = [value]
            for k in range(1, radix):
                pairs = []
                for i in range(count):
                    digit = i // stride % radix
                    target = i + ((digit + k) % radix - digit) * stride
                    pairs.append((i, target))
                parts.append(lax.ppermute(value, axis, pairs))
            digit = index // stride % radix
            if radix == 2:
                value = parts[0] + parts[1]
            elif radix == 4:
                even = parts[0] + parts[2]
                odd = parts[1] + parts[3]
                value = even + odd
            else:
                value = functools.reduce(jnp.add, parts)
            stride *= radix
    return value


BF16 = jnp.bfloat16


def gram_kernel(x_ref, w_ref, p_ref, ax_ref, aw_ref, ap_ref, out_ref, s_ref, image):
    chunks, rows, wide = s_ref.shape
    cols = rows // 6
    ny = wide // 128
    stride = x_ref.shape[0] // cols

    def body(c, carry):
        for k, (b_ref, a_ref) in enumerate(((x_ref, ax_ref), (w_ref, aw_ref), (p_ref, ap_ref))):
            for y in range(ny):
                pick = pl.ds(c * ny + y, cols, stride=stride)
                at = pl.ds(y * 128, 128)
                for ref, put in (
                    (b_ref, lambda r, v: s_ref.__setitem__((c, r, at), v)),
                    (a_ref, lambda r, v: image.__setitem__((r, at), v)),
                ):
                    value = ref[pick, :]
                    high = value.astype(BF16)
                    low = (value - high.astype(F32)).astype(BF16)
                    put(pl.ds(k * cols, cols), high)
                    put(pl.ds((3 + k) * cols, cols), low)
        left = s_ref[c]
        dims = (((1,), (1,)), ((), ()))
        proj = lax.dot_general(left, image[...], dims, preferred_element_type=F32)
        gram = lax.dot_general(left, left, dims, preferred_element_type=F32)
        return (carry[0] + proj, carry[1] + gram)

    zero = jnp.zeros((rows, rows), F32)
    proj, gram = lax.fori_loop(0, chunks, body, (zero, zero))
    nb = 3 * cols
    for k, full in enumerate((proj, gram)):
        full = full[:nb] + full[nb:]
        out_ref[:, pl.ds(k * nb, nb)] = full[:, :nb] + full[:, nb:]


def eliminate(left, right, first):
    size = left.shape[0]
    row = lax.broadcasted_iota(jnp.int32, (size, 1), 0)
    scale = jnp.zeros((size, 1), F32)
    for k in range(size):
        pivot = left[k : k + 1, first + k : first + k + 1]
        column = left[:, first + k : first + k + 1]
        factor = jnp.where(row > k, column / pivot, 0.0)
        scale = jnp.where(row == k, pivot, scale)
        line, other = left[k : k + 1], right[k : k + 1]
        left = left - factor * line
        right = right - factor * other
    scale = lax.rsqrt(scale)
    return left * scale, right * scale


def finish_kernel(ncells, sums_ref, s_ref, block_ref, search_ref, bufs, sems):
    nb = sums_ref.shape[0]
    cols = nb // 3
    chunks, rows, wide = s_ref.shape
    ny = wide // 128
    row = lax.broadcasted_iota(jnp.int32, (nb, 128), 0)
    lane = lax.broadcasted_iota(jnp.int32, (nb, 128), 1)
    eye = jnp.where((lane == row) | (lane == row + nb), 1.0, 0.0)
    left, inverse = eliminate(sums_ref[...], eye, nb)
    flat = -dot_nt(inverse[:cols, :nb], left[:, :nb])
    flat = flat + jnp.where(lane[:cols, :nb] == row[:cols, :nb], SHIFT, 0.0)
    _, scaled = eliminate(dot_nt(flat, flat), flat, 0)
    coef = jnp.dot(
        scaled, inverse, precision=lax.Precision.HIGHEST, preferred_element_type=F32
    )
    coef = coef[:, :rows] * jnp.sqrt(F32(ncells))
    slot = lax.broadcasted_iota(jnp.int32, (cols, rows), 1)
    first = (slot < cols) | ((slot >= nb) & (slot < nb + cols))
    terms = []
    for part in (jnp.where(first, coef, 0.0), jnp.where(first, 0.0, coef)):
        high = part.astype(BF16)
        terms += [high, (part - high.astype(F32)).astype(BF16)]
    terms = jnp.concatenate(terms, axis=0)

    def copies(c, slot):
        return [
            pltpu.make_async_copy(bufs.at[slot, k], ref.at[:, c], sems.at[slot, k])
            for k, ref in enumerate((block_ref, search_ref))
        ]

    for c in range(chunks):
        slot = c % 2
        if c >= 2:
            for copy in copies(c - 2, slot):
                copy.wait()
        for y in range(0, ny, 2):
            got = jnp.dot(
                terms, s_ref[c, :, pl.ds(y * 128, 256)], preferred_element_type=F32
            )
            search = got[2 * cols : 3 * cols] + got[3 * cols :]
            block = search + (got[:cols] + got[cols : 2 * cols])
            for k, value in enumerate((block, search)):
                for j in range(2):
                    bufs[slot, k, :, y + j, :] = value[:, j * 128 : (j + 1) * 128]
        for copy in copies(c, slot):
            copy.start()
    for c in range(max(chunks - 2, 0), chunks):
        for copy in copies(c, c % 2):
            copy.wait()


def body(x, p):
    cols, nx, ny, nz = x.shape
    ngx, ngy = lax.axis_size("gx"), lax.axis_size("gy")
    ix, iy = lax.axis_index("gx"), lax.axis_index("gy")
    flags = jnp.stack([ix > 0, ix < ngx - 1, iy > 0, iy < ngy - 1]).astype(jnp.int32)
    half, cx, cy = cols // 2, nx // 2, ny // 2
    work = pltpu.VMEM

    yrows = nx * DEEP + nx
    to_ylo, to_yhi, to_xlo, to_xhi = call(
        pack_kernel,
        [shape(cols, yrows, nz)] * 2 + [shape(cols, DEEP + 1, ny, nz)] * 2,
        [], (x, p), "pack",
    )
    ylo, yhi = from_low(to_yhi, "gy"), from_high(to_ylo, "gy")
    xlo, xhi = from_low(to_xhi, "gx"), from_high(to_xlo, "gx")

    devices = ngx * ngy
    sums, to_clo, to_chi = call(
        theta_kernel,
        [shape(devices, 8, 128)] + [shape(cols, nx * DEEP, nz)] * 2,
        [work((nx + 2, PAD + ny + 8, nz), F32), work((128 * 8, nz), F32)],
        (x, ylo, yhi, xlo, xhi), "theta",
    )
    clo, chi = from_low(to_chi, "gx"), from_high(to_clo, "gx")
    sums = lax.all_to_all(sums, ("gx", "gy"), 0, 0)

    tall, wide = ny + 2 * DEEP, nx + 2 * DEEP
    plane = PAD + tall + 8
    r, e, c, to_ylo, to_yhi = call(
        pre_kernel,
        [shape(cols, wide - 4, tall, nz), shape(cols, nx, ny, nz), shape(half, cx, cy, nz)]
        + [shape(half * cx * CO, nz)] * 2,
        [work((wide, plane, nz), F32)] * 2
        + [work((wide, tall, nz), F32), work((ny, nz), F32), work((cols, cx, cy, nz), F32)],
        (flags, sums, x, ylo, yhi, xlo, xhi, clo, chi), "pre", smem=1,
    )

    cylo, cyhi = from_low(to_yhi, "gy"), from_high(to_ylo, "gy")
    to_xlo, to_xhi = call(
        coarse_pack_kernel, [shape(half * CO * (cy + 2 * CO), nz)] * 2, [], (c, cylo, cyhi), "cpack"
    )
    cxlo, cxhi = from_low(to_xhi, "gx"), from_high(to_xlo, "gx")
    cwide = cx + 2 * CO
    corr, to_ylo, to_yhi = call(
        coarse_kernel,
        [shape(cols, nx, ny, nz)] + [shape(cols, nx * POST, nz)] * 2,
        [work((cwide, PAD + 16 + 8, nz), F32)] * 2
        + [work((cwide, 16, nz), F32), work((ny, nz), F32)],
        (flags, c, cylo, cyhi, cxlo, cxhi, e), "coarse", smem=1,
    )

    eylo, eyhi = from_low(to_yhi, "gy"), from_high(to_ylo, "gy")
    to_xlo, to_xhi = call(
        post_pack_kernel, [shape(cols * POST * (ny + 2 * POST), nz)] * 2, [], (corr, eylo, eyhi), "ppack"
    )
    exlo, exhi = from_low(to_xhi, "gx"), from_high(to_xlo, "gx")

    image_x, image_p = call(
        image_kernel, [shape(cols, nx, ny, nz)] * 2,
        [work((nx + 2, PAD + ny + 8, nz), F32)],
        (x, p, ylo, yhi, xlo, xhi), "image",
    )
    w, image_w = call(
        post_kernel, [shape(cols, nx, ny, nz)] * 2,
        [work((nx + 2 * POST, plane, nz), F32)] * 2,
        (flags, corr, eylo, eyhi, exlo, exhi, r), "post", smem=1,
    )

    flat = [v.reshape(cols * nx * ny, nz) for v in (x, w, p, image_x, image_w, image_p)]
    nb = 3 * cols
    part, split = call(
        gram_kernel,
        [shape(nb, 128), pltpu.VMEM((nx, 2 * nb, ny * nz), BF16)],
        [work((2 * nb, ny * nz), BF16)],
        flat, "gram",
    )
    part = sum_all(part)
    any_space = pl.BlockSpec(memory_space=pl.ANY)
    new_block, new_search = pl.pallas_call(
        functools.partial(finish_kernel, nx * ny * nz * devices),
        out_shape=[jax.ShapeDtypeStruct((cols, nx, ny, nz), F32)] * 2,
        in_specs=[VMEM, VMEM],
        out_specs=[any_space] * 2,
        scratch_shapes=[
            work((2, 2, cols, ny, nz), F32),
            pltpu.SemaphoreType.DMA((2, 2)),
        ],
        compiler_params=pltpu.CompilerParams(vmem_limit_bytes=GRANT),
        name="finish",
    )(part, split)
    return (new_block, new_search)


def solution(mesh):
    spec = P(None, "gx", "gy", None)
    return jax.shard_map(
        body, mesh=mesh, in_specs=(spec, spec), out_specs=(spec, spec), check_vma=False
    )
```

```python
import functools

import jax
import jax.numpy as jnp
from jax import lax
from jax.experimental import pallas as pl
from jax.experimental.pallas import tpu as pltpu
from jax.sharding import PartitionSpec as P


RELAX = 1.0 / 9.0
COARSE_RELAX = 1.0 / 36.0
SHIFT = 13.0
DEEP = 4
POST = 3
CO = 3
CP = 2
PAD = 8

GRANT = 20 << 20

F32 = jnp.float32
VMEM = pl.BlockSpec(memory_space=pltpu.VMEM)
SMEM = pl.BlockSpec(memory_space=pltpu.SMEM)


def shape(*dims):
    return pltpu.VMEM(dims, F32)


def call(kernel, outs, scratch, args, smem=0):
    specs = [SMEM] * smem + [VMEM] * (len(args) - smem)
    return pl.pallas_call(
        kernel,
        out_shape=outs,
        in_specs=specs,
        out_specs=[VMEM] * len(outs),
        scratch_shapes=scratch,
        compiler_params=pltpu.CompilerParams(vmem_limit_bytes=GRANT),
    )(*args)


def along_z(plane, step, lanes):
    size = plane.shape[-1]
    low = jnp.where(lanes >= step, pltpu.roll(plane, step, 1), 0.0)
    high = jnp.where(lanes < size - step, pltpu.roll(plane, size - step, 1), 0.0)
    return low + high


def beside(work, i, row, rows, center, before, after, lanes, step=1):
    total = before + after
    total = total + work[i, pl.ds(row - 1, rows), :] + work[i, pl.ds(row + 1, rows), :]
    return total + along_z(center, step, lanes)


def dot_nt(a, b):
    return lax.dot_general(
        a, b, (((1,), (1,)), ((), ())),
        precision=lax.Precision.HIGHEST, preferred_element_type=F32,
    )


def lane_index(rows):
    return lax.broadcasted_iota(jnp.int32, (rows, 128), 1)


def pack_kernel(flags, x_ref, p_ref, ylo, yhi, xa, xb):
    cols, nx, ny, _ = x_ref.shape
    even = flags[4]

    def body(f, carry):
        for i in range(nx):
            ylo[f, pl.ds(i * DEEP, DEEP), :] = x_ref[f, i, pl.ds(0, DEEP), :]
            yhi[f, pl.ds(i * DEEP, DEEP), :] = x_ref[f, i, pl.ds(ny - DEEP, DEEP), :]
            ylo[f, pl.ds(nx * DEEP + i, 1), :] = p_ref[f, i, pl.ds(0, 1), :]
            yhi[f, pl.ds(nx * DEEP + i, 1), :] = p_ref[f, i, pl.ds(ny - 1, 1), :]
        for out, high in ((xa, even), (xb, 1 - even)):
            for i in range(DEEP):
                out[f, i] = x_ref[f, high * (nx - DEEP) + i]
            out[f, DEEP] = p_ref[f, high * (nx - 1)]
        return carry

    lax.fori_loop(0, cols, body, 0)


def theta_kernel(flags, x_ref, ylo, yhi, xa, xb, out_ref, ca, cb, work, parts):
    cols, nx, ny, _ = x_ref.shape
    lanes = lane_index(ny)
    half = nx // 2 * DEEP
    even = flags[4]
    parts[pl.ds(2 * cols * 8, 128 * 8 - 2 * cols * 8), :] = jnp.ones((128 * 8 - 2 * cols * 8, 128), F32)

    def body(f, carry):
        for buf, high in ((xa, even), (xb, 1 - even)):
            work[high * (nx + 1), pl.ds(PAD, ny), :] = buf[f, (1 - high) * (DEEP - 1)]
        for i in range(nx):
            work[i + 1, pl.ds(PAD, ny), :] = x_ref[f, i]
            work[i + 1, pl.ds(PAD - 1, 1), :] = ylo[f, pl.ds(i * DEEP + DEEP - 1, 1), :]
            work[i + 1, pl.ds(PAD + ny, 1), :] = yhi[f, pl.ds(i * DEEP, 1), :]
        numer = jnp.zeros((ny, 128), F32)
        denom = jnp.zeros((ny, 128), F32)
        before = work[0, pl.ds(PAD, ny), :]
        center = work[1, pl.ds(PAD, ny), :]
        for i in range(nx):
            after = work[i + 2, pl.ds(PAD, ny), :]
            image = 6.0 * center - beside(work, i + 1, PAD, ny, center, before, after, lanes)
            numer = numer + center * image
            denom = denom + center * center
            before, center = center, after
        parts[pl.ds(pl.multiple_of(f * 8, 8), 8), :] = numer[0:8] + numer[8:16]
        parts[pl.ds(pl.multiple_of((cols + f) * 8, 8), 8), :] = denom[0:8] + denom[8:16]
        for out, high in ((ca, even), (cb, 1 - even)):
            rows = pl.ds(pl.multiple_of(high * half, half), half)
            out[f, pl.ds(0, half), :] = ylo[f, rows, :]
            out[f, pl.ds(half, half), :] = yhi[f, rows, :]
        return carry

    lax.fori_loop(0, cols, body, 0)
    total = parts[pl.ds(0, 128, stride=8), :]
    for k in range(1, 8):
        total = total + parts[pl.ds(k, 128, stride=8), :]
    sums = dot_nt(jnp.ones((8, 128), F32), total)

    def spread(k, carry):
        out_ref[k] = sums
        return carry

    lax.fori_loop(0, out_ref.shape[0], spread, 0)


def pre_kernel(
    flags, sums, x_ref, ylo, yhi, xa, xb, ca, cb,
    r_ref, e_ref, c_ref, slo, shi, elo, ehi,
    work, other, rhs, small, coarse,
):
    cols, nx, ny, _ = x_ref.shape
    tall = ny + 2 * DEEP
    wide = nx + 2 * DEEP
    lanes = lane_index(tall)
    own = lane_index(ny)
    spot = lane_index(8)
    has = [flags[k].astype(F32) for k in range(4)]
    row = lax.broadcasted_iota(jnp.int32, (tall, 128), 0)
    mask_y = RELAX * jnp.where(row < DEEP, has[2], jnp.where(row >= ny + DEEP, has[3], 1.0))

    def relax_of(i):
        if i < DEEP:
            return mask_y * has[0]
        if i >= nx + DEEP:
            return mask_y * has[1]
        return mask_y

    even = flags[4]
    total = sums[0]
    for k in range(1, sums.shape[0]):
        total = total + sums[k]
    theta = total / pltpu.roll(total, 128 - cols, 1)

    @pl.when(jnp.bool_(True))
    def _():
        zero = jnp.zeros((8, 128), F32)
        for i in range(wide):
            for buf in (work, other):
                buf[i, pl.ds(0, PAD), :] = zero
                buf[i, pl.ds(PAD + tall, 8), :] = zero

    data = pl.ds(PAD, tall)

    def body(f, carry):
        th = jnp.sum(jnp.where(spot == f, theta, 0.0)) * 0.125
        for i in range(DEEP):
            for buf, corner, high in ((xa, ca, even), (xb, cb, 1 - even)):
                plane = high * (nx + DEEP) + i
                work[plane, pl.ds(PAD + DEEP, ny), :] = buf[f, i]
                buf = corner
                work[plane, pl.ds(PAD, DEEP), :] = buf[f, pl.ds(i * DEEP, DEEP), :]
                work[plane, pl.ds(PAD + DEEP + ny, DEEP), :] = buf[
                    f, pl.ds(DEEP * DEEP + i * DEEP, DEEP), :
                ]
        for i in range(nx):
            work[i + DEEP, pl.ds(PAD + DEEP, ny), :] = x_ref[f, i]
            work[i + DEEP, pl.ds(PAD, DEEP), :] = ylo[f, pl.ds(i * DEEP, DEEP), :]
            work[i + DEEP, pl.ds(PAD + DEEP + ny, DEEP), :] = yhi[f, pl.ds(i * DEEP, DEEP), :]
        before = work[0, data, :]
        center = work[1, data, :]
        for i in range(1, wide - 1):
            after = work[i + 1, data, :]
            image = 6.0 * center - beside(work, i, PAD, tall, center, before, after, lanes)
            res = image - th * center
            rhs[i] = res
            other[i, data, :] = relax_of(i) * res
            before, center = center, after
        src, dst = other, work
        for depth in (2, 3):
            before = src[depth - 1, data, :]
            center = src[depth, data, :]
            for i in range(depth, wide - depth):
                after = src[i + 1, data, :]
                near = beside(src, i, PAD, tall, center, before, after, lanes)
                dst[i, data, :] = center + relax_of(i) * (rhs[i] - 6.0 * center + near)
                before, center = center, after
            src, dst = dst, src
        own_rows = pl.ds(PAD + DEEP, ny)
        before = src[DEEP - 1, own_rows, :]
        center = src[DEEP, own_rows, :]
        held = None
        for i in range(DEEP, nx + DEEP):
            after = src[i + 1, own_rows, :]
            near = beside(src, i, PAD + DEEP, ny, center, before, after, own)
            rest = rhs[i, pl.ds(DEEP, ny), :] - 6.0 * center + near
            k = i - DEEP
            e_ref[f, k] = center
            elo[f, pl.ds(k * POST, POST), :] = e_ref[f, k, pl.ds(0, POST), :]
            ehi[f, pl.ds(k * POST, POST), :] = e_ref[f, k, pl.ds(ny - POST, POST), :]
            if held is None:
                held = rest
            else:
                small[...] = held + rest
                pair = small[pl.ds(0, ny // 2, stride=2), :] + small[pl.ds(1, ny // 2, stride=2), :]
                mate = jnp.where(
                    spot % 2 == 0, pltpu.roll(pair, 127, 1), pltpu.roll(pair, 1, 1)
                )
                coarse[f, (i - DEEP) // 2] = pair + mate
                held = None
            before, center = center, after
        for i in range(2, wide - 2):
            r_ref[f, i - 2] = rhs[i]
        return carry

    lax.fori_loop(0, cols, body, 0)
    half, cx, cy = cols // 2, nx // 2, ny // 2
    even = spot % 2 == 0
    for g in range(half):
        for i in range(cx):
            both = jnp.where(even, coarse[g, i], coarse[g + half, i])
            c_ref[g, i] = both
            small[pl.ds(0, 8), :] = both
            at = (g * cx + i) * CO
            slo[pl.ds(at, CO), :] = small[pl.ds(0, CO), :]
            shi[pl.ds(at, CO), :] = small[pl.ds(cy - CO, CO), :]


def coarse_pack_kernel(deep, flags, c_ref, ylo, yhi, xa, xb):
    half, cx, cy, _ = c_ref.shape
    even = flags[4]
    tall = cy + 2 * deep
    for g in range(half):
        for out, first in ((xa, even * (cx - deep)), (xb, (1 - even) * (cx - deep))):
            for i in range(deep):
                at = (g * deep + i) * tall
                src = (g * cx + first + i) * deep
                out[pl.ds(at, deep), :] = ylo[pl.ds(src, deep), :]
                out[pl.ds(at + deep, cy), :] = c_ref[g, first + i]
                out[pl.ds(at + deep + cy, deep), :] = yhi[pl.ds(src, deep), :]


def coarse_kernel(
    flags, c_ref, ylo, yhi, xa, xb, corr_ref, slo, shi, work, other, rhs
):
    half, cx, cy, _ = c_ref.shape
    tall = cy + 2 * CO
    full = 16
    wide = cx + 2 * CO
    even = flags[4]
    lanes = lane_index(full)
    has = [flags[k].astype(F32) for k in range(4)]
    row = lax.broadcasted_iota(jnp.int32, (full, 128), 0)
    mask_y = COARSE_RELAX * jnp.where(row < CO, has[2], jnp.where(row >= cy + CO, has[3], 1.0))
    zero = jnp.zeros((8, 128), F32)
    for i in range(wide):
        rhs[i, pl.ds(8, 8), :] = zero
        for buf in (work, other):
            buf[i, pl.ds(0, PAD), :] = zero
            buf[i, pl.ds(PAD + full, 8), :] = zero

    def relax_of(i):
        if i < CO:
            return mask_y * has[0]
        if i >= cx + CO:
            return mask_y * has[1]
        return mask_y

    data = pl.ds(PAD, full)

    def body(g, carry):
        for i in range(CO):
            for buf, high in ((xa, even), (xb, 1 - even)):
                plane = high * (cx + CO) + i
                rhs[plane, pl.ds(0, tall), :] = buf[pl.ds((g * CO + i) * tall, tall), :]
        for i in range(cx):
            at = pl.ds((g * cx + i) * CO, CO)
            rhs[i + CO, pl.ds(0, CO), :] = ylo[at, :]
            rhs[i + CO, pl.ds(CO, cy), :] = c_ref[g, i]
            rhs[i + CO, pl.ds(CO + cy, CO), :] = yhi[at, :]
        for i in range(wide):
            work[i, data, :] = relax_of(i) * rhs[i]
        src, dst = work, other
        for depth in (1, 2, 3):
            before = src[depth - 1, data, :]
            center = src[depth, data, :]
            for i in range(depth, wide - depth):
                after = src[i + 1, data, :]
                near = beside(src, i, PAD, full, center, before, after, lanes, 2)
                dst[i, data, :] = center + relax_of(i) * (rhs[i] - 4.0 * (6.0 * center - near))
                before, center = center, after
            src, dst = dst, src
        for i in range(cx):
            corr_ref[g, i] = src[i + CO, pl.ds(PAD + CO, cy), :]
            at = pl.ds((g * cx + i) * CP, CP)
            slo[at, :] = src[i + CO, pl.ds(PAD + CO, CP), :]
            shi[at, :] = src[i + CO, pl.ds(PAD + CO + cy - CP, CP), :]
        return carry

    lax.fori_loop(0, half, body, 0)


def post_pack_kernel(flags, corr_ref, ylo, yhi, xa, xb):
    cols, nx, ny, _ = corr_ref.shape
    even = flags[4]
    tall = ny + 2 * POST

    def body(f, carry):
        for out, first in ((xa, even * (nx - POST)), (xb, (1 - even) * (nx - POST))):
            for i in range(POST):
                at = (f * POST + i) * tall
                src = pl.ds((first + i) * POST, POST)
                out[pl.ds(at, POST), :] = ylo[f, src, :]
                out[pl.ds(at + POST, ny), :] = corr_ref[f, first + i]
                out[pl.ds(at + POST + ny, POST), :] = yhi[f, src, :]
        return carry

    lax.fori_loop(0, cols, body, 0)


def post_kernel(
    flags, e_ref, ylo, yhi, xa, xb, c_ref, cylo, cyhi, cxa, cxb, r_ref,
    w_ref, image_ref, work, other, coarse, small,
):
    cols, nx, ny, _ = e_ref.shape
    half, cx, cy, _ = c_ref.shape
    ctall = cy + 2 * CP
    parity = lane_index(16) % 2
    coarse[:, pl.ds(8, 8), :] = jnp.zeros((cx + 2 * CP, 8, 128), F32)
    tall = ny + 2 * DEEP
    wide = nx + 2 * POST
    span = ny + 2 * POST
    gap = DEEP - POST
    even = flags[4]
    lanes = lane_index(tall)
    own = lane_index(ny)
    has = [flags[k].astype(F32) for k in range(4)]
    row = lax.broadcasted_iota(jnp.int32, (tall, 128), 0)
    mask_y = RELAX * jnp.where(row < DEEP, has[2], jnp.where(row >= ny + DEEP, has[3], 1.0))
    zero = jnp.zeros((PAD + 8, 128), F32)
    for i in range(wide):
        for buf in (work, other):
            buf[i, pl.ds(0, PAD + 8), :] = zero
            buf[i, pl.ds(PAD + tall - 8, 16), :] = zero

    def relax_of(i):
        if i < POST:
            return mask_y * has[0]
        if i >= nx + POST:
            return mask_y * has[1]
        return mask_y

    data = pl.ds(PAD, tall)

    def body(f, carry):
        g = lax.rem(f, half)
        for i in range(CP):
            at = pl.ds((g * CP + i) * ctall, ctall)
            for buf, high in ((cxa, even), (cxb, 1 - even)):
                coarse[high * (cx + CP) + i, pl.ds(0, ctall), :] = buf[at, :]
        for i in range(cx):
            at = pl.ds((g * cx + i) * CP, CP)
            coarse[i + CP, pl.ds(0, CP), :] = cylo[at, :]
            coarse[i + CP, pl.ds(CP, cy), :] = c_ref[g, i]
            coarse[i + CP, pl.ds(CP + cy, CP), :] = cyhi[at, :]
        for i in range(POST):
            at = pl.ds((f * POST + i) * span, span)
            for buf, high in ((xa, even), (xb, 1 - even)):
                work[high * (nx + POST) + i, pl.ds(PAD + gap, span), :] = buf[at, :]
        for i in range(nx):
            at = pl.ds(i * POST, POST)
            work[i + POST, pl.ds(PAD + gap, POST), :] = ylo[f, at, :]
            work[i + POST, pl.ds(PAD + DEEP, ny), :] = e_ref[f, i]
            work[i + POST, pl.ds(PAD + DEEP + ny, POST), :] = yhi[f, at, :]
        upper = jnp.where(f >= half, 1, 0)
        for m in range(cx + 2 * CP):
            both = coarse[m]
            moved = jnp.where(parity == 1, pltpu.roll(both, 1, 1), pltpu.roll(both, 127, 1))
            value = jnp.where(parity == upper, both, moved)
            small[m % 2, pl.ds(0, 16, stride=2), :] = value
            small[m % 2, pl.ds(1, 16, stride=2), :] = value
            up = small[m % 2, pl.ds(0, tall), :]
            for i in (2 * m - 1, 2 * m):
                if 0 <= i < wide:
                    work[i, data, :] = work[i, data, :] + up
        src, dst = work, other
        for depth in (1, 2):
            before = src[depth - 1, data, :]
            center = src[depth, data, :]
            for i in range(depth, wide - depth):
                after = src[i + 1, data, :]
                near = beside(src, i, PAD, tall, center, before, after, lanes)
                dst[i, data, :] = center + relax_of(i) * (r_ref[f, i - 1] - 6.0 * center + near)
                before, center = center, after
            src, dst = dst, src
        own_rows = pl.ds(PAD + DEEP, ny)
        before = src[POST - 1, own_rows, :]
        center = src[POST, own_rows, :]
        for i in range(POST, nx + POST):
            after = src[i + 1, own_rows, :]
            near = beside(src, i, PAD + DEEP, ny, center, before, after, own)
            w_ref[f, i - POST] = center
            image_ref[f, i - POST] = 6.0 * center - near
            before, center = center, after
        return carry

    lax.fori_loop(0, cols, body, 0)


def image_kernel(flags, x_ref, p_ref, ylo, yhi, xa, xb, ax_ref, ap_ref, work):
    cols, nx, ny, _ = x_ref.shape
    even = flags[4]
    lanes = lane_index(ny)

    def body(f, carry):
        for ref, out, first, base, deep in (
            (x_ref, ax_ref, 0, 0, DEEP),
            (p_ref, ap_ref, DEEP, nx * DEEP, 1),
        ):
            for buf, high in ((xa, even), (xb, 1 - even)):
                plane = first + (1 - high) * (deep - 1)
                work[high * (nx + 1), pl.ds(PAD, ny), :] = buf[f, plane]
            for i in range(nx):
                work[i + 1, pl.ds(PAD, ny), :] = ref[f, i]
                work[i + 1, pl.ds(PAD - 1, 1), :] = ylo[f, pl.ds(base + i * deep + deep - 1, 1), :]
                work[i + 1, pl.ds(PAD + ny, 1), :] = yhi[f, pl.ds(base + i * deep, 1), :]
            before = work[0, pl.ds(PAD, ny), :]
            center = work[1, pl.ds(PAD, ny), :]
            for i in range(nx):
                after = work[i + 2, pl.ds(PAD, ny), :]
                near = beside(work, i + 1, PAD, ny, center, before, after, lanes)
                out[f, i] = 6.0 * center - near
                before, center = center, after
        return carry

    lax.fori_loop(0, cols, body, 0)


def from_low(value, axis):
    count = lax.axis_size(axis)
    return lax.ppermute(value, axis, [(i, i + 1) for i in range(count - 1)])


def from_high(value, axis):
    count = lax.axis_size(axis)
    return lax.ppermute(value, axis, [(i + 1, i) for i in range(count - 1)])


def swap(one, two, axis):
    count = lax.axis_size(axis)
    pairs = [[], []]
    for i in range(count - 1):
        pairs[i % 2] += [(i, i + 1), (i + 1, i)]
    two = lax.ppermute(two, axis, pairs[1])
    return lax.ppermute(one, axis, pairs[0]), two


def radices(count):
    out = []
    if count % 2 == 0 and count % 4 == 0 and (count.bit_length() - 1) % 2 == 1:
        out.append(2)
        count //= 2
    while count % 4 == 0:
        out.append(4)
        count //= 4
    if count > 1:
        out.append(count)
    return out


def sum_all(value):
    for axis in ("gx", "gy"):
        count = lax.axis_size(axis)
        stride = 1
        for radix in radices(count):
            index = lax.axis_index(axis)
            parts = [value]
            for k in range(1, radix):
                pairs = []
                for i in range(count):
                    digit = i // stride % radix
                    target = i + ((digit + k) % radix - digit) * stride
                    pairs.append((i, target))
                parts.append(lax.ppermute(value, axis, pairs))
            digit = index // stride % radix
            if radix == 2:
                value = parts[0] + parts[1]
            elif radix == 4:
                even = parts[0] + parts[2]
                odd = parts[1] + parts[3]
                value = even + odd
            else:
                value = functools.reduce(jnp.add, parts)
            stride *= radix
    return value


BF16 = jnp.bfloat16


def gram_kernel(x_ref, w_ref, p_ref, ax_ref, aw_ref, ap_ref, out_ref, s_ref, image):
    chunks, rows, wide = s_ref.shape
    cols = rows // 6
    ny = wide // 128
    stride = x_ref.shape[0] // cols

    def body(c, carry):
        for k, (b_ref, a_ref) in enumerate(((x_ref, ax_ref), (w_ref, aw_ref), (p_ref, ap_ref))):
            for y in range(ny):
                pick = pl.ds(c * ny + y, cols, stride=stride)
                at = pl.ds(y * 128, 128)
                for ref, put in (
                    (b_ref, lambda r, v: s_ref.__setitem__((c, r, at), v)),
                    (a_ref, lambda r, v: image.__setitem__((r, at), v)),
                ):
                    value = ref[pick, :]
                    high = value.astype(BF16)
                    low = (value - high.astype(F32)).astype(BF16)
                    put(pl.ds(k * cols, cols), high)
                    put(pl.ds((3 + k) * cols, cols), low)
        left = s_ref[c]
        dims = (((1,), (1,)), ((), ()))
        proj = lax.dot_general(left, image[...], dims, preferred_element_type=F32)
        gram = lax.dot_general(left, left, dims, preferred_element_type=F32)
        return (carry[0] + proj, carry[1] + gram)

    zero = jnp.zeros((rows, rows), F32)
    proj, gram = lax.fori_loop(0, chunks, body, (zero, zero))
    nb = 3 * cols
    for k, full in enumerate((proj, gram)):
        full = full[:nb] + full[nb:]
        out_ref[:, pl.ds(k * nb, nb)] = full[:, :nb] + full[:, nb:]


def eliminate(left, right, first):
    size = left.shape[0]
    row = lax.broadcasted_iota(jnp.int32, (size, 1), 0)
    scale = jnp.zeros((size, 1), F32)
    for k in range(size):
        pivot = left[k : k + 1, first + k : first + k + 1]
        column = left[:, first + k : first + k + 1]
        factor = jnp.where(row > k, column / pivot, 0.0)
        scale = jnp.where(row == k, pivot, scale)
        line, other = left[k : k + 1], right[k : k + 1]
        left = left - factor * line
        right = right - factor * other
    scale = lax.rsqrt(scale)
    return left * scale, right * scale


def finish_kernel(ncells, sums_ref, s_ref, block_ref, search_ref, bufs, sems):
    nb = sums_ref.shape[0]
    cols = nb // 3
    chunks, rows, wide = s_ref.shape
    ny = wide // 128
    row = lax.broadcasted_iota(jnp.int32, (nb, 128), 0)
    lane = lax.broadcasted_iota(jnp.int32, (nb, 128), 1)
    eye = jnp.where((lane == row) | (lane == row + nb), 1.0, 0.0)
    left, inverse = eliminate(sums_ref[...], eye, nb)
    flat = -dot_nt(inverse[:cols, :nb], left[:, :nb])
    flat = flat + jnp.where(lane[:cols, :nb] == row[:cols, :nb], SHIFT, 0.0)
    _, scaled = eliminate(dot_nt(flat, flat), flat, 0)
    coef = jnp.dot(
        scaled, inverse, precision=lax.Precision.HIGHEST, preferred_element_type=F32
    )
    coef = coef[:, :rows] * jnp.sqrt(F32(ncells))
    slot = lax.broadcasted_iota(jnp.int32, (cols, rows), 1)
    first = (slot < cols) | ((slot >= nb) & (slot < nb + cols))
    terms = []
    for part in (jnp.where(first, coef, 0.0), jnp.where(first, 0.0, coef)):
        high = part.astype(BF16)
        terms += [high, (part - high.astype(F32)).astype(BF16)]
    terms = jnp.concatenate(terms, axis=0)

    def copies(c):
        return [
            pltpu.make_async_copy(bufs.at[c, k], ref.at[:, c], sems.at[c, k])
            for k, ref in enumerate((block_ref, search_ref))
        ]

    for c in range(chunks):
        for y in range(0, ny, 2):
            got = jnp.dot(
                terms, s_ref[c, :, pl.ds(y * 128, 256)], preferred_element_type=F32
            )
            search = got[2 * cols : 3 * cols] + got[3 * cols :]
            block = search + (got[:cols] + got[cols : 2 * cols])
            for k, value in enumerate((block, search)):
                for j in range(2):
                    flat = bufs.at[c, k].reshape(cols * ny, 128)
                    flat[pl.ds(y + j, cols, stride=ny), :] = value[:, j * 128 : (j + 1) * 128]
        for copy in copies(c):
            copy.start()
    for c in range(chunks):
        for copy in copies(c):
            copy.wait()


def step(x, p):
    cols, nx, ny, nz = x.shape
    ngx, ngy = lax.axis_size("gx"), lax.axis_size("gy")
    ix, iy = lax.axis_index("gx"), lax.axis_index("gy")
    flags = jnp.stack([ix > 0, ix < ngx - 1, iy > 0, iy < ngy - 1, ix % 2 == 0]).astype(jnp.int32)
    half, cx, cy = cols // 2, nx // 2, ny // 2
    work = pltpu.VMEM

    yrows = nx * DEEP + nx
    to_ylo, to_yhi, to_xlo, to_xhi = call(
        pack_kernel,
        [shape(cols, yrows, nz)] * 2 + [shape(cols, DEEP + 1, ny, nz)] * 2,
        [], (flags, x, p), smem=1,
    )
    ylo, yhi = from_low(to_yhi, "gy"), from_high(to_ylo, "gy")
    xlo, xhi = swap(to_xlo, to_xhi, "gx")

    devices = ngx * ngy
    sums, to_clo, to_chi = call(
        theta_kernel,
        [shape(devices, 8, 128)] + [shape(cols, nx * DEEP, nz)] * 2,
        [work((nx + 2, PAD + ny + 8, nz), F32), work((128 * 8, nz), F32)],
        (flags, x, ylo, yhi, xlo, xhi), smem=1,
    )
    clo, chi = swap(to_clo, to_chi, "gx")
    sums = lax.all_to_all(sums, ("gx", "gy"), 0, 0)

    tall, wide = ny + 2 * DEEP, nx + 2 * DEEP
    plane = PAD + tall + 8
    r, e, c, to_ylo, to_yhi, to_eylo, to_eyhi = call(
        pre_kernel,
        [shape(cols, wide - 4, tall, nz), shape(cols, nx, ny, nz), shape(half, cx, cy, nz)]
        + [shape(half * cx * CO, nz)] * 2
        + [shape(cols, nx * POST, nz)] * 2,
        [work((wide, plane, nz), F32)] * 2
        + [work((wide, tall, nz), F32), work((ny, nz), F32), work((cols, cx, cy, nz), F32)],
        (flags, sums, x, ylo, yhi, xlo, xhi, clo, chi), smem=1,
    )

    cylo, cyhi = from_low(to_yhi, "gy"), from_high(to_ylo, "gy")
    eylo, eyhi = from_low(to_eyhi, "gy"), from_high(to_eylo, "gy")
    to_xlo, to_xhi = call(
        functools.partial(coarse_pack_kernel, CO),
        [shape(half * CO * (cy + 2 * CO), nz)] * 2, [], (flags, c, cylo, cyhi), smem=1,
    )
    cxlo, cxhi = swap(to_xlo, to_xhi, "gx")
    to_exlo, to_exhi = call(
        post_pack_kernel, [shape(cols * POST * (ny + 2 * POST), nz)] * 2, [],
        (flags, e, eylo, eyhi), smem=1,
    )
    exlo, exhi = swap(to_exlo, to_exhi, "gx")
    cwide = cx + 2 * CO
    d, to_ylo, to_yhi = call(
        coarse_kernel,
        [shape(half, cx, cy, nz)] + [shape(half * cx * CP, nz)] * 2,
        [work((cwide, PAD + 16 + 8, nz), F32)] * 2 + [work((cwide, 16, nz), F32)],
        (flags, c, cylo, cyhi, cxlo, cxhi), smem=1,
    )
    dylo, dyhi = from_low(to_yhi, "gy"), from_high(to_ylo, "gy")
    to_xlo, to_xhi = call(
        functools.partial(coarse_pack_kernel, CP),
        [shape(half * CP * (cy + 2 * CP), nz)] * 2, [], (flags, d, dylo, dyhi), smem=1,
    )
    dxlo, dxhi = swap(to_xlo, to_xhi, "gx")

    image_x, image_p = call(
        image_kernel, [shape(cols, nx, ny, nz)] * 2,
        [work((nx + 2, PAD + ny + 8, nz), F32)],
        (flags, x, p, ylo, yhi, xlo, xhi), smem=1,
    )
    w, image_w = call(
        post_kernel, [shape(cols, nx, ny, nz)] * 2,
        [work((nx + 2 * POST, plane, nz), F32)] * 2
        + [work((cx + 2 * CP, 16, nz), F32), work((2, 32, nz), F32)],
        (flags, e, eylo, eyhi, exlo, exhi, d, dylo, dyhi, dxlo, dxhi, r), smem=1,
    )

    flat = [v.reshape(cols * nx * ny, nz) for v in (x, w, p, image_x, image_w, image_p)]
    nb = 3 * cols
    part, split = call(
        gram_kernel,
        [shape(nb, 128), pltpu.VMEM((nx, 2 * nb, ny * nz), BF16)],
        [work((2 * nb, ny * nz), BF16)],
        flat,
    )
    part = sum_all(part)
    any_space = pl.BlockSpec(memory_space=pl.ANY)
    new_block, new_search = pl.pallas_call(
        functools.partial(finish_kernel, nx * ny * nz * devices),
        out_shape=[jax.ShapeDtypeStruct((cols, nx, ny, nz), F32)] * 2,
        in_specs=[VMEM, VMEM],
        out_specs=[any_space] * 2,
        scratch_shapes=[
            work((nx, 2, cols, ny, nz), F32),
            pltpu.SemaphoreType.DMA((nx, 2)),
        ],
        compiler_params=pltpu.CompilerParams(vmem_limit_bytes=GRANT),
        name="finish",
    )(part, split)
    return (new_block, new_search)


def solution(mesh):
    spec = P(None, "gx", "gy", None)
    return jax.shard_map(
        step, mesh=mesh, in_specs=(spec, spec), out_specs=(spec, spec), check_vma=False
    )
```

```python
import functools

import jax
import jax.numpy as jnp
from jax import lax
from jax.experimental import pallas as pl
from jax.experimental.pallas import tpu as pltpu
from jax.sharding import PartitionSpec as P


RELAX = 1.0 / 9.0
COARSE_RELAX = 1.0 / 36.0
SHIFT = 13.0
DEEP = 4
POST = 3
CO = 3
CP = 2
PAD = 8

GRANT = 20 << 20

F32 = jnp.float32
VMEM = pl.BlockSpec(memory_space=pltpu.VMEM)
SMEM = pl.BlockSpec(memory_space=pltpu.SMEM)


def shape(*dims):
    return pltpu.VMEM(dims, F32)


def call(kernel, outs, scratch, args, smem=0):
    specs = [SMEM] * smem + [VMEM] * (len(args) - smem)
    return pl.pallas_call(
        kernel,
        out_shape=outs,
        in_specs=specs,
        out_specs=[VMEM] * len(outs),
        scratch_shapes=scratch,
        compiler_params=pltpu.CompilerParams(vmem_limit_bytes=GRANT),
    )(*args)


def along_z(plane, step, lanes):
    size = plane.shape[-1]
    low = jnp.where(lanes >= step, pltpu.roll(plane, step, 1), 0.0)
    high = jnp.where(lanes < size - step, pltpu.roll(plane, size - step, 1), 0.0)
    return low + high


def beside(work, i, row, rows, center, before, after, lanes, step=1):
    total = before + after
    total = total + work[i, pl.ds(row - 1, rows), :] + work[i, pl.ds(row + 1, rows), :]
    return total + along_z(center, step, lanes)


def dot_nt(a, b):
    return lax.dot_general(
        a, b, (((1,), (1,)), ((), ())),
        precision=lax.Precision.HIGHEST, preferred_element_type=F32,
    )


def by_pairs(cols, one):
    def body(h, carry):
        for u in range(2):
            one(h + u * (cols // 2), u)
        return carry

    lax.fori_loop(0, cols // 2, body, 0)


def lane_index(rows):
    return lax.broadcasted_iota(jnp.int32, (rows, 128), 1)


def pack_kernel(flags, x_ref, p_ref, ylo, yhi, xa, xb):
    cols, nx, ny, _ = x_ref.shape
    even = flags[4]

    def body(f, carry):
        for i in range(nx):
            ylo[f, pl.ds(i * DEEP, DEEP), :] = x_ref[f, i, pl.ds(0, DEEP), :]
            yhi[f, pl.ds(i * DEEP, DEEP), :] = x_ref[f, i, pl.ds(ny - DEEP, DEEP), :]
            ylo[f, pl.ds(nx * DEEP + i, 1), :] = p_ref[f, i, pl.ds(0, 1), :]
            yhi[f, pl.ds(nx * DEEP + i, 1), :] = p_ref[f, i, pl.ds(ny - 1, 1), :]
        for out, high in ((xa, even), (xb, 1 - even)):
            for i in range(DEEP):
                out[f, i] = x_ref[f, high * (nx - DEEP) + i]
            out[f, DEEP] = p_ref[f, high * (nx - 1)]
        return carry

    lax.fori_loop(0, cols, body, 0)


def theta_kernel(flags, x_ref, ylo, yhi, xa, xb, out_ref, ca, cb, works, parts):
    cols, nx, ny, _ = x_ref.shape
    lanes = lane_index(ny)
    half = nx // 2 * DEEP
    even = flags[4]
    parts[pl.ds(2 * cols * 8, 128 * 8 - 2 * cols * 8), :] = jnp.ones((128 * 8 - 2 * cols * 8, 128), F32)

    def one(f, u):
        work = works.at[u]
        for buf, high in ((xa, even), (xb, 1 - even)):
            work[high * (nx + 1), pl.ds(PAD, ny), :] = buf[f, (1 - high) * (DEEP - 1)]
        for i in range(nx):
            work[i + 1, pl.ds(PAD, ny), :] = x_ref[f, i]
            work[i + 1, pl.ds(PAD - 1, 1), :] = ylo[f, pl.ds(i * DEEP + DEEP - 1, 1), :]
            work[i + 1, pl.ds(PAD + ny, 1), :] = yhi[f, pl.ds(i * DEEP, 1), :]
        numer = jnp.zeros((ny, 128), F32)
        denom = jnp.zeros((ny, 128), F32)
        before = work[0, pl.ds(PAD, ny), :]
        center = work[1, pl.ds(PAD, ny), :]
        for i in range(nx):
            after = work[i + 2, pl.ds(PAD, ny), :]
            image = 6.0 * center - beside(work, i + 1, PAD, ny, center, before, after, lanes)
            numer = numer + center * image
            denom = denom + center * center
            before, center = center, after
        parts[pl.ds(pl.multiple_of(f * 8, 8), 8), :] = numer[0:8] + numer[8:16]
        parts[pl.ds(pl.multiple_of((cols + f) * 8, 8), 8), :] = denom[0:8] + denom[8:16]
        for out, high in ((ca, even), (cb, 1 - even)):
            rows = pl.ds(pl.multiple_of(high * half, half), half)
            out[f, pl.ds(0, half), :] = ylo[f, rows, :]
            out[f, pl.ds(half, half), :] = yhi[f, rows, :]

    by_pairs(cols, one)
    total = parts[pl.ds(0, 128, stride=8), :]
    for k in range(1, 8):
        total = total + parts[pl.ds(k, 128, stride=8), :]
    sums = dot_nt(jnp.ones((8, 128), F32), total)

    def spread(k, carry):
        out_ref[k] = sums
        return carry

    lax.fori_loop(0, out_ref.shape[0], spread, 0)


def pre_kernel(
    flags, sums, x_ref, ylo, yhi, xa, xb, ca, cb,
    r_ref, e_ref, c_ref, slo, shi, elo, ehi,
    works, others, rhss, smalls, coarse,
):
    cols, nx, ny, _ = x_ref.shape
    tall = ny + 2 * DEEP
    wide = nx + 2 * DEEP
    lanes = lane_index(tall)
    own = lane_index(ny)
    spot = lane_index(8)
    has = [flags[k].astype(F32) for k in range(4)]
    row = lax.broadcasted_iota(jnp.int32, (tall, 128), 0)
    mask_y = RELAX * jnp.where(row < DEEP, has[2], jnp.where(row >= ny + DEEP, has[3], 1.0))

    def relax_of(i):
        if i < DEEP:
            return mask_y * has[0]
        if i >= nx + DEEP:
            return mask_y * has[1]
        return mask_y

    even = flags[4]
    total = sums[0]
    for k in range(1, sums.shape[0]):
        total = total + sums[k]
    theta = total / pltpu.roll(total, 128 - cols, 1)

    @pl.when(jnp.bool_(True))
    def _():
        zero = jnp.zeros((8, 128), F32)
        for i in range(wide):
            for buf in (works, others):
                for u in range(2):
                    buf[u, i, pl.ds(0, PAD), :] = zero
                    buf[u, i, pl.ds(PAD + tall, 8), :] = zero

    data = pl.ds(PAD, tall)

    def one(f, u):
        work, other, rhs, small = works.at[u], others.at[u], rhss.at[u], smalls.at[u]
        th = jnp.sum(jnp.where(spot == f, theta, 0.0)) * 0.125
        for i in range(DEEP):
            for buf, corner, high in ((xa, ca, even), (xb, cb, 1 - even)):
                plane = high * (nx + DEEP) + i
                work[plane, pl.ds(PAD + DEEP, ny), :] = buf[f, i]
                buf = corner
                work[plane, pl.ds(PAD, DEEP), :] = buf[f, pl.ds(i * DEEP, DEEP), :]
                work[plane, pl.ds(PAD + DEEP + ny, DEEP), :] = buf[
                    f, pl.ds(DEEP * DEEP + i * DEEP, DEEP), :
                ]
        for i in range(nx):
            work[i + DEEP, pl.ds(PAD + DEEP, ny), :] = x_ref[f, i]
            work[i + DEEP, pl.ds(PAD, DEEP), :] = ylo[f, pl.ds(i * DEEP, DEEP), :]
            work[i + DEEP, pl.ds(PAD + DEEP + ny, DEEP), :] = yhi[f, pl.ds(i * DEEP, DEEP), :]
        before = work[0, data, :]
        center = work[1, data, :]
        for i in range(1, wide - 1):
            after = work[i + 1, data, :]
            image = 6.0 * center - beside(work, i, PAD, tall, center, before, after, lanes)
            res = image - th * center
            rhs[i] = res
            other[i, data, :] = relax_of(i) * res
            before, center = center, after
        src, dst = other, work
        for depth in (2, 3):
            before = src[depth - 1, data, :]
            center = src[depth, data, :]
            for i in range(depth, wide - depth):
                after = src[i + 1, data, :]
                near = beside(src, i, PAD, tall, center, before, after, lanes)
                dst[i, data, :] = center + relax_of(i) * (rhs[i] - 6.0 * center + near)
                before, center = center, after
            src, dst = dst, src
        own_rows = pl.ds(PAD + DEEP, ny)
        before = src[DEEP - 1, own_rows, :]
        center = src[DEEP, own_rows, :]
        held = None
        for i in range(DEEP, nx + DEEP):
            after = src[i + 1, own_rows, :]
            near = beside(src, i, PAD + DEEP, ny, center, before, after, own)
            rest = rhs[i, pl.ds(DEEP, ny), :] - 6.0 * center + near
            k = i - DEEP
            e_ref[f, k] = center
            elo[f, pl.ds(k * POST, POST), :] = e_ref[f, k, pl.ds(0, POST), :]
            ehi[f, pl.ds(k * POST, POST), :] = e_ref[f, k, pl.ds(ny - POST, POST), :]
            if held is None:
                held = rest
            else:
                small[...] = held + rest
                pair = small[pl.ds(0, ny // 2, stride=2), :] + small[pl.ds(1, ny // 2, stride=2), :]
                mate = jnp.where(
                    spot % 2 == 0, pltpu.roll(pair, 127, 1), pltpu.roll(pair, 1, 1)
                )
                coarse[f, (i - DEEP) // 2] = pair + mate
                held = None
            before, center = center, after
        for i in range(2, wide - 2):
            r_ref[f, i - 2] = rhs[i]

    by_pairs(cols, one)
    small = smalls.at[0]
    half, cx, cy = cols // 2, nx // 2, ny // 2
    even = spot % 2 == 0
    for g in range(half):
        for i in range(cx):
            both = jnp.where(even, coarse[g, i], coarse[g + half, i])
            c_ref[g, i] = both
            small[pl.ds(0, 8), :] = both
            at = (g * cx + i) * CO
            slo[pl.ds(at, CO), :] = small[pl.ds(0, CO), :]
            shi[pl.ds(at, CO), :] = small[pl.ds(cy - CO, CO), :]


def coarse_pack_kernel(deep, flags, c_ref, ylo, yhi, xa, xb):
    half, cx, cy, _ = c_ref.shape
    even = flags[4]
    tall = cy + 2 * deep
    for g in range(half):
        for out, first in ((xa, even * (cx - deep)), (xb, (1 - even) * (cx - deep))):
            for i in range(deep):
                at = (g * deep + i) * tall
                src = (g * cx + first + i) * deep
                out[pl.ds(at, deep), :] = ylo[pl.ds(src, deep), :]
                out[pl.ds(at + deep, cy), :] = c_ref[g, first + i]
                out[pl.ds(at + deep + cy, deep), :] = yhi[pl.ds(src, deep), :]


def coarse_kernel(
    flags, c_ref, ylo, yhi, xa, xb, corr_ref, slo, shi, work, other, rhs
):
    half, cx, cy, _ = c_ref.shape
    tall = cy + 2 * CO
    full = 16
    wide = cx + 2 * CO
    even = flags[4]
    lanes = lane_index(full)
    has = [flags[k].astype(F32) for k in range(4)]
    row = lax.broadcasted_iota(jnp.int32, (full, 128), 0)
    mask_y = COARSE_RELAX * jnp.where(row < CO, has[2], jnp.where(row >= cy + CO, has[3], 1.0))
    zero = jnp.zeros((8, 128), F32)
    for i in range(wide):
        rhs[i, pl.ds(8, 8), :] = zero
        for buf in (work, other):
            buf[i, pl.ds(0, PAD), :] = zero
            buf[i, pl.ds(PAD + full, 8), :] = zero

    def relax_of(i):
        if i < CO:
            return mask_y * has[0]
        if i >= cx + CO:
            return mask_y * has[1]
        return mask_y

    data = pl.ds(PAD, full)

    def body(g, carry):
        for i in range(CO):
            for buf, high in ((xa, even), (xb, 1 - even)):
                plane = high * (cx + CO) + i
                rhs[plane, pl.ds(0, tall), :] = buf[pl.ds((g * CO + i) * tall, tall), :]
        for i in range(cx):
            at = pl.ds((g * cx + i) * CO, CO)
            rhs[i + CO, pl.ds(0, CO), :] = ylo[at, :]
            rhs[i + CO, pl.ds(CO, cy), :] = c_ref[g, i]
            rhs[i + CO, pl.ds(CO + cy, CO), :] = yhi[at, :]
        for i in range(wide):
            work[i, data, :] = relax_of(i) * rhs[i]
        src, dst = work, other
        for depth in (1, 2, 3):
            before = src[depth - 1, data, :]
            center = src[depth, data, :]
            for i in range(depth, wide - depth):
                after = src[i + 1, data, :]
                near = beside(src, i, PAD, full, center, before, after, lanes, 2)
                dst[i, data, :] = center + relax_of(i) * (rhs[i] - 4.0 * (6.0 * center - near))
                before, center = center, after
            src, dst = dst, src
        for i in range(cx):
            corr_ref[g, i] = src[i + CO, pl.ds(PAD + CO, cy), :]
            at = pl.ds((g * cx + i) * CP, CP)
            slo[at, :] = src[i + CO, pl.ds(PAD + CO, CP), :]
            shi[at, :] = src[i + CO, pl.ds(PAD + CO + cy - CP, CP), :]
        return carry

    lax.fori_loop(0, half, body, 0)


def post_pack_kernel(flags, corr_ref, ylo, yhi, xa, xb):
    cols, nx, ny, _ = corr_ref.shape
    even = flags[4]
    tall = ny + 2 * POST

    def body(f, carry):
        for out, first in ((xa, even * (nx - POST)), (xb, (1 - even) * (nx - POST))):
            for i in range(POST):
                at = (f * POST + i) * tall
                src = pl.ds((first + i) * POST, POST)
                out[pl.ds(at, POST), :] = ylo[f, src, :]
                out[pl.ds(at + POST, ny), :] = corr_ref[f, first + i]
                out[pl.ds(at + POST + ny, POST), :] = yhi[f, src, :]
        return carry

    lax.fori_loop(0, cols, body, 0)


def post_kernel(
    flags, e_ref, ylo, yhi, xa, xb, c_ref, cylo, cyhi, cxa, cxb, r_ref,
    w_ref, image_ref, works, others, coarses, smalls,
):
    cols, nx, ny, _ = e_ref.shape
    _, cx, cy, _ = c_ref.shape
    ctall = cy + 2 * CP
    parity = lane_index(16) % 2
    coarses[:, :, pl.ds(8, 8), :] = jnp.zeros((2, cx + 2 * CP, 8, 128), F32)
    tall = ny + 2 * DEEP
    wide = nx + 2 * POST
    span = ny + 2 * POST
    gap = DEEP - POST
    even = flags[4]
    lanes = lane_index(tall)
    own = lane_index(ny)
    has = [flags[k].astype(F32) for k in range(4)]
    row = lax.broadcasted_iota(jnp.int32, (tall, 128), 0)
    mask_y = RELAX * jnp.where(row < DEEP, has[2], jnp.where(row >= ny + DEEP, has[3], 1.0))
    zero = jnp.zeros((PAD + 8, 128), F32)
    for i in range(wide):
        for buf in (works, others):
            for u in range(2):
                buf[u, i, pl.ds(0, PAD + 8), :] = zero
                buf[u, i, pl.ds(PAD + tall - 8, 16), :] = zero

    def relax_of(i):
        if i < POST:
            return mask_y * has[0]
        if i >= nx + POST:
            return mask_y * has[1]
        return mask_y

    data = pl.ds(PAD, tall)

    def one(f, u):
        work, other, coarse, small = works.at[u], others.at[u], coarses.at[0], smalls.at[u]
        if u == 0:
            g = f
            for i in range(CP):
                at = pl.ds((g * CP + i) * ctall, ctall)
                for buf, high in ((cxa, even), (cxb, 1 - even)):
                    coarse[high * (cx + CP) + i, pl.ds(0, ctall), :] = buf[at, :]
            for i in range(cx):
                at = pl.ds((g * cx + i) * CP, CP)
                coarse[i + CP, pl.ds(0, CP), :] = cylo[at, :]
                coarse[i + CP, pl.ds(CP, cy), :] = c_ref[g, i]
                coarse[i + CP, pl.ds(CP + cy, CP), :] = cyhi[at, :]
        for i in range(POST):
            at = pl.ds((f * POST + i) * span, span)
            for buf, high in ((xa, even), (xb, 1 - even)):
                work[high * (nx + POST) + i, pl.ds(PAD + gap, span), :] = buf[at, :]
        for i in range(nx):
            at = pl.ds(i * POST, POST)
            work[i + POST, pl.ds(PAD + gap, POST), :] = ylo[f, at, :]
            work[i + POST, pl.ds(PAD + DEEP, ny), :] = e_ref[f, i]
            work[i + POST, pl.ds(PAD + DEEP + ny, POST), :] = yhi[f, at, :]
        for m in range(cx + 2 * CP):
            both = coarse[m]
            value = jnp.where(parity == u, both, pltpu.roll(both, 127 if u else 1, 1))
            small[m % 2, pl.ds(0, 16, stride=2), :] = value
            small[m % 2, pl.ds(1, 16, stride=2), :] = value
            up = small[m % 2, pl.ds(0, tall), :]
            for i in (2 * m - 1, 2 * m):
                if 0 <= i < wide:
                    work[i, data, :] = work[i, data, :] + up
        src, dst = work, other
        for depth in (1, 2):
            before = src[depth - 1, data, :]
            center = src[depth, data, :]
            for i in range(depth, wide - depth):
                after = src[i + 1, data, :]
                near = beside(src, i, PAD, tall, center, before, after, lanes)
                dst[i, data, :] = center + relax_of(i) * (r_ref[f, i - 1] - 6.0 * center + near)
                before, center = center, after
            src, dst = dst, src
        own_rows = pl.ds(PAD + DEEP, ny)
        before = src[POST - 1, own_rows, :]
        center = src[POST, own_rows, :]
        for i in range(POST, nx + POST):
            after = src[i + 1, own_rows, :]
            near = beside(src, i, PAD + DEEP, ny, center, before, after, own)
            rows = pl.ds((i - POST) * ny * cols + f, ny, stride=cols)
            w_ref[rows, :] = center
            image_ref[rows, :] = 6.0 * center - near
            before, center = center, after

    by_pairs(cols, one)


def image_kernel(flags, x_ref, p_ref, ylo, yhi, xa, xb, tx_ref, tp_ref, ax_ref, ap_ref, work):
    cols, nx, ny, _ = x_ref.shape
    even = flags[4]
    lanes = lane_index(ny)

    def body(f, carry):
        for ref, same, out, first, base, deep in (
            (x_ref, tx_ref, ax_ref, 0, 0, DEEP),
            (p_ref, tp_ref, ap_ref, DEEP, nx * DEEP, 1),
        ):
            for buf, high in ((xa, even), (xb, 1 - even)):
                plane = first + (1 - high) * (deep - 1)
                work[high * (nx + 1), pl.ds(PAD, ny), :] = buf[f, plane]
            for i in range(nx):
                work[i + 1, pl.ds(PAD, ny), :] = ref[f, i]
                work[i + 1, pl.ds(PAD - 1, 1), :] = ylo[f, pl.ds(base + i * deep + deep - 1, 1), :]
                work[i + 1, pl.ds(PAD + ny, 1), :] = yhi[f, pl.ds(base + i * deep, 1), :]
            before = work[0, pl.ds(PAD, ny), :]
            center = work[1, pl.ds(PAD, ny), :]
            for i in range(nx):
                after = work[i + 2, pl.ds(PAD, ny), :]
                near = beside(work, i + 1, PAD, ny, center, before, after, lanes)
                rows = pl.ds(i * ny * cols + f, ny, stride=cols)
                same[rows, :] = center
                out[rows, :] = 6.0 * center - near
                before, center = center, after
        return carry

    lax.fori_loop(0, cols, body, 0)


def from_low(value, axis):
    count = lax.axis_size(axis)
    return lax.ppermute(value, axis, [(i, i + 1) for i in range(count - 1)])


def from_high(value, axis):
    count = lax.axis_size(axis)
    return lax.ppermute(value, axis, [(i + 1, i) for i in range(count - 1)])


def swap(one, two, axis):
    count = lax.axis_size(axis)
    pairs = [[], []]
    for i in range(count - 1):
        pairs[i % 2] += [(i, i + 1), (i + 1, i)]
    two = lax.ppermute(two, axis, pairs[1])
    return lax.ppermute(one, axis, pairs[0]), two


def radices(count):
    out = []
    if count % 2 == 0 and count % 4 == 0 and (count.bit_length() - 1) % 2 == 1:
        out.append(2)
        count //= 2
    while count % 4 == 0:
        out.append(4)
        count //= 4
    if count > 1:
        out.append(count)
    return out


def sum_all(value):
    for axis in ("gx", "gy"):
        count = lax.axis_size(axis)
        stride = 1
        for radix in radices(count):
            index = lax.axis_index(axis)
            parts = [value]
            for k in range(1, radix):
                pairs = []
                for i in range(count):
                    digit = i // stride % radix
                    target = i + ((digit + k) % radix - digit) * stride
                    pairs.append((i, target))
                parts.append(lax.ppermute(value, axis, pairs))
            digit = index // stride % radix
            if radix == 2:
                value = parts[0] + parts[1]
            elif radix == 4:
                even = parts[0] + parts[2]
                odd = parts[1] + parts[3]
                value = even + odd
            else:
                value = functools.reduce(jnp.add, parts)
            stride *= radix
    return value


BF16 = jnp.bfloat16


def gram_kernel(x_ref, w_ref, p_ref, ax_ref, aw_ref, ap_ref, out_ref, s_ref, image):
    chunks, rows, wide = s_ref.shape
    cols = rows // 6
    ny = wide // 128

    def body(c, carry):
        for k, (b_ref, a_ref) in enumerate(((x_ref, ax_ref), (w_ref, aw_ref), (p_ref, ap_ref))):
            for y in range(ny):
                pick = pl.ds(pl.multiple_of((c * ny + y) * cols, cols), cols)
                at = pl.ds(y * 128, 128)
                for ref, put in (
                    (b_ref, lambda r, v: s_ref.__setitem__((c, r, at), v)),
                    (a_ref, lambda r, v: image.__setitem__((r, at), v)),
                ):
                    value = ref[pick, :]
                    high = value.astype(BF16)
                    low = (value - high.astype(F32)).astype(BF16)
                    put(pl.ds(k * cols, cols), high)
                    put(pl.ds((3 + k) * cols, cols), low)
        left = s_ref[c]
        dims = (((1,), (1,)), ((), ()))
        proj = lax.dot_general(left, image[...], dims, preferred_element_type=F32)
        gram = lax.dot_general(left, left, dims, preferred_element_type=F32)
        return (carry[0] + proj, carry[1] + gram)

    zero = jnp.zeros((rows, rows), F32)
    proj, gram = lax.fori_loop(0, chunks, body, (zero, zero))
    nb = 3 * cols
    for k, full in enumerate((proj, gram)):
        full = full[:nb] + full[nb:]
        out_ref[:, pl.ds(k * nb, nb)] = full[:, :nb] + full[:, nb:]


def eliminate(left, right, first):
    size = left.shape[0]
    tiles = size // 8
    lefts = [left[8 * t : 8 * t + 8] for t in range(tiles)]
    rights = [right[8 * t : 8 * t + 8] for t in range(tiles)]
    row = lax.broadcasted_iota(jnp.int32, (8, 1), 0)
    scales = [jnp.zeros((8, 1), F32) for _ in range(tiles)]
    for k in range(size):
        own, at = k // 8, k % 8
        line, other = lefts[own][at : at + 1], rights[own][at : at + 1]
        pivot = line[:, first + k : first + k + 1]
        inverse = 1.0 / pivot
        line, other = line * inverse, other * inverse
        scales[own] = jnp.where(row == at, pivot, scales[own])
        for t in range(own, tiles):
            column = lefts[t][:, first + k : first + k + 1]
            if t == own:
                column = jnp.where(row > at, column, 0.0)
            lefts[t] = lefts[t] - column * line
            rights[t] = rights[t] - column * other
    scales = [lax.rsqrt(scale) for scale in scales]
    return (
        jnp.concatenate([v * scale for v, scale in zip(lefts, scales)], axis=0),
        jnp.concatenate([v * scale for v, scale in zip(rights, scales)], axis=0),
    )


def finish_kernel(ncells, sums_ref, s_ref, block_ref, search_ref, bufs, sems):
    nb = sums_ref.shape[0]
    cols = nb // 3
    chunks, rows, wide = s_ref.shape
    ny = wide // 128
    row = lax.broadcasted_iota(jnp.int32, (nb, 128), 0)
    lane = lax.broadcasted_iota(jnp.int32, (nb, 128), 1)
    eye = jnp.where((lane == row) | (lane == row + nb), 1.0, 0.0)
    left, inverse = eliminate(sums_ref[...], eye, nb)
    flat = -dot_nt(inverse[:cols, :nb], left[:, :nb])
    flat = flat + jnp.where(lane[:cols, :nb] == row[:cols, :nb], SHIFT, 0.0)
    _, scaled = eliminate(dot_nt(flat, flat), flat, 0)
    coef = jnp.dot(
        scaled, inverse, precision=lax.Precision.HIGHEST, preferred_element_type=F32
    )
    coef = coef[:, :rows] * jnp.sqrt(F32(ncells))
    slot = lax.broadcasted_iota(jnp.int32, (cols, rows), 1)
    first = (slot < cols) | ((slot >= nb) & (slot < nb + cols))
    terms = []
    for part in (jnp.where(first, coef, 0.0), jnp.where(first, 0.0, coef)):
        high = part.astype(BF16)
        terms += [high, (part - high.astype(F32)).astype(BF16)]
    terms = jnp.concatenate(terms, axis=0)

    def copies(c):
        return [
            pltpu.make_async_copy(bufs.at[c, k], ref.at[:, c], sems.at[c, k])
            for k, ref in enumerate((block_ref, search_ref))
        ]

    def chunk(c, carry):
        for y in range(0, ny, 2):
            got = jnp.dot(
                terms, s_ref[c, :, pl.ds(y * 128, 256)], preferred_element_type=F32
            )
            search = got[2 * cols : 3 * cols] + got[3 * cols :]
            block = search + (got[:cols] + got[cols : 2 * cols])
            for k, value in enumerate((block, search)):
                for j in range(2):
                    flat = bufs.at[c, k].reshape(cols * ny, 128)
                    flat[pl.ds(y + j, cols, stride=ny), :] = value[:, j * 128 : (j + 1) * 128]
        for copy in copies(c):
            copy.start()
        return carry

    def finish(c, carry):
        for copy in copies(c):
            copy.wait()
        return carry

    lax.fori_loop(0, chunks, chunk, 0, unroll=4 if chunks % 4 == 0 else 1)
    lax.fori_loop(0, chunks, finish, 0)


def step(x, p):
    cols, nx, ny, nz = x.shape
    ngx, ngy = lax.axis_size("gx"), lax.axis_size("gy")
    ix, iy = lax.axis_index("gx"), lax.axis_index("gy")
    flags = jnp.stack([ix > 0, ix < ngx - 1, iy > 0, iy < ngy - 1, ix % 2 == 0]).astype(jnp.int32)
    half, cx, cy = cols // 2, nx // 2, ny // 2
    work = pltpu.VMEM

    yrows = nx * DEEP + nx
    to_ylo, to_yhi, to_xlo, to_xhi = call(
        pack_kernel,
        [shape(cols, yrows, nz)] * 2 + [shape(cols, DEEP + 1, ny, nz)] * 2,
        [], (flags, x, p), smem=1,
    )
    ylo, yhi = from_low(to_yhi, "gy"), from_high(to_ylo, "gy")
    xlo, xhi = swap(to_xlo, to_xhi, "gx")

    devices = ngx * ngy
    sums, to_clo, to_chi = call(
        theta_kernel,
        [shape(devices, 8, 128)] + [shape(cols, nx * DEEP, nz)] * 2,
        [work((2, nx + 2, PAD + ny + 8, nz), F32), work((128 * 8, nz), F32)],
        (flags, x, ylo, yhi, xlo, xhi), smem=1,
    )
    clo, chi = swap(to_clo, to_chi, "gx")
    sums = lax.all_to_all(sums, ("gx", "gy"), 0, 0)

    tall, wide = ny + 2 * DEEP, nx + 2 * DEEP
    plane = PAD + tall + 8
    r, e, c, to_ylo, to_yhi, to_eylo, to_eyhi = call(
        pre_kernel,
        [shape(cols, wide - 4, tall, nz), shape(cols, nx, ny, nz), shape(half, cx, cy, nz)]
        + [shape(half * cx * CO, nz)] * 2
        + [shape(cols, nx * POST, nz)] * 2,
        [work((2, wide, plane, nz), F32)] * 2
        + [work((2, wide, tall, nz), F32), work((2, ny, nz), F32), work((cols, cx, cy, nz), F32)],
        (flags, sums, x, ylo, yhi, xlo, xhi, clo, chi), smem=1,
    )

    cylo, cyhi = from_low(to_yhi, "gy"), from_high(to_ylo, "gy")
    eylo, eyhi = from_low(to_eyhi, "gy"), from_high(to_eylo, "gy")
    to_xlo, to_xhi = call(
        functools.partial(coarse_pack_kernel, CO),
        [shape(half * CO * (cy + 2 * CO), nz)] * 2, [], (flags, c, cylo, cyhi), smem=1,
    )
    cxlo, cxhi = swap(to_xlo, to_xhi, "gx")
    to_exlo, to_exhi = call(
        post_pack_kernel, [shape(cols * POST * (ny + 2 * POST), nz)] * 2, [],
        (flags, e, eylo, eyhi), smem=1,
    )
    exlo, exhi = swap(to_exlo, to_exhi, "gx")
    cwide = cx + 2 * CO
    d, to_ylo, to_yhi = call(
        coarse_kernel,
        [shape(half, cx, cy, nz)] + [shape(half * cx * CP, nz)] * 2,
        [work((cwide, PAD + 16 + 8, nz), F32)] * 2 + [work((cwide, 16, nz), F32)],
        (flags, c, cylo, cyhi, cxlo, cxhi), smem=1,
    )
    dylo, dyhi = from_low(to_yhi, "gy"), from_high(to_ylo, "gy")
    to_xlo, to_xhi = call(
        functools.partial(coarse_pack_kernel, CP),
        [shape(half * CP * (cy + 2 * CP), nz)] * 2, [], (flags, d, dylo, dyhi), smem=1,
    )
    dxlo, dxhi = swap(to_xlo, to_xhi, "gx")

    flat_x, flat_p, image_x, image_p = call(
        image_kernel, [shape(nx * ny * cols, nz)] * 4,
        [work((nx + 2, PAD + ny + 8, nz), F32)],
        (flags, x, p, ylo, yhi, xlo, xhi), smem=1,
    )
    w, image_w = call(
        post_kernel, [shape(nx * ny * cols, nz)] * 2,
        [work((2, nx + 2 * POST, plane, nz), F32)] * 2
        + [work((2, cx + 2 * CP, 16, nz), F32), work((2, 2, 32, nz), F32)],
        (flags, e, eylo, eyhi, exlo, exhi, d, dylo, dyhi, dxlo, dxhi, r), smem=1,
    )

    flat = (flat_x, w, flat_p, image_x, image_w, image_p)
    nb = 3 * cols
    part, split = call(
        gram_kernel,
        [shape(nb, 128), pltpu.VMEM((nx, 2 * nb, ny * nz), BF16)],
        [work((2 * nb, ny * nz), BF16)],
        flat,
    )
    part = sum_all(part)
    any_space = pl.BlockSpec(memory_space=pl.ANY)
    new_block, new_search = pl.pallas_call(
        functools.partial(finish_kernel, nx * ny * nz * devices),
        out_shape=[jax.ShapeDtypeStruct((cols, nx, ny, nz), F32)] * 2,
        in_specs=[VMEM, VMEM],
        out_specs=[any_space] * 2,
        scratch_shapes=[
            work((nx, 2, cols, ny, nz), F32),
            pltpu.SemaphoreType.DMA((nx, 2)),
        ],
        compiler_params=pltpu.CompilerParams(vmem_limit_bytes=GRANT),
        name="finish",
    )(part, split)
    return (new_block, new_search)


def solution(mesh):
    spec = P(None, "gx", "gy", None)
    return jax.shard_map(
        step, mesh=mesh, in_specs=(spec, spec), out_specs=(spec, spec), check_vma=False
    )
```

```python
import functools

import jax
import jax.numpy as jnp
from jax import lax
from jax.experimental import pallas as pl
from jax.experimental.pallas import tpu as pltpu
from jax.sharding import PartitionSpec as P


RELAX = 1.0 / 9.0
COARSE_RELAX = 1.0 / 36.0
SHIFT = 13.0
DEEP = 4
POST = 3
CO = 3
CP = 2
PAD = 8

GRANT = 20 << 20

F32 = jnp.float32
VMEM = pl.BlockSpec(memory_space=pltpu.VMEM)
SMEM = pl.BlockSpec(memory_space=pltpu.SMEM)


def shape(*dims):
    return pltpu.VMEM(dims, F32)


def call(kernel, outs, scratch, args, smem=0):
    specs = [SMEM] * smem + [VMEM] * (len(args) - smem)
    return pl.pallas_call(
        kernel,
        out_shape=outs,
        in_specs=specs,
        out_specs=[VMEM] * len(outs),
        scratch_shapes=scratch,
        compiler_params=pltpu.CompilerParams(vmem_limit_bytes=GRANT),
    )(*args)


def along_z(plane, step, lanes):
    size = plane.shape[-1]
    low = jnp.where(lanes >= step, pltpu.roll(plane, step, 1), 0.0)
    high = jnp.where(lanes < size - step, pltpu.roll(plane, size - step, 1), 0.0)
    return low + high


def beside(work, i, row, rows, center, before, after, lanes, step=1):
    total = before + after
    total = total + work[i, pl.ds(row - 1, rows), :] + work[i, pl.ds(row + 1, rows), :]
    return total + along_z(center, step, lanes)


def dot_nt(a, b):
    return lax.dot_general(
        a, b, (((1,), (1,)), ((), ())),
        precision=lax.Precision.HIGHEST, preferred_element_type=F32,
    )


def by_pairs(cols, one):
    def body(h, carry):
        for u in range(2):
            one(h + u * (cols // 2), u)
        return carry

    lax.fori_loop(0, cols // 2, body, 0)


def lane_index(rows):
    return lax.broadcasted_iota(jnp.int32, (rows, 128), 1)


def pack_kernel(flags, x_ref, p_ref, ylo, yhi, xa, xb):
    cols, nx, ny, _ = x_ref.shape
    even = flags[4]

    def body(f, carry):
        for i in range(nx):
            ylo[f, pl.ds(i * DEEP, DEEP), :] = x_ref[f, i, pl.ds(0, DEEP), :]
            yhi[f, pl.ds(i * DEEP, DEEP), :] = x_ref[f, i, pl.ds(ny - DEEP, DEEP), :]
            ylo[f, pl.ds(nx * DEEP + i, 1), :] = p_ref[f, i, pl.ds(0, 1), :]
            yhi[f, pl.ds(nx * DEEP + i, 1), :] = p_ref[f, i, pl.ds(ny - 1, 1), :]
        for out, high in ((xa, even), (xb, 1 - even)):
            for i in range(DEEP):
                out[f, i] = x_ref[f, high * (nx - DEEP) + i]
            out[f, DEEP] = p_ref[f, high * (nx - 1)]
        return carry

    lax.fori_loop(0, cols, body, 0)


def theta_kernel(flags, x_ref, ylo, yhi, xa, xb, out_ref, ca, cb, works, parts):
    cols, nx, ny, _ = x_ref.shape
    lanes = lane_index(ny)
    half = nx // 2 * DEEP
    even = flags[4]
    parts[pl.ds(2 * cols * 8, 128 * 8 - 2 * cols * 8), :] = jnp.ones((128 * 8 - 2 * cols * 8, 128), F32)

    def one(f, u):
        work = works.at[u]
        for buf, high in ((xa, even), (xb, 1 - even)):
            work[high * (nx + 1), pl.ds(PAD, ny), :] = buf[f, (1 - high) * (DEEP - 1)]
        for i in range(nx):
            work[i + 1, pl.ds(PAD, ny), :] = x_ref[f, i]
            work[i + 1, pl.ds(PAD - 1, 1), :] = ylo[f, pl.ds(i * DEEP + DEEP - 1, 1), :]
            work[i + 1, pl.ds(PAD + ny, 1), :] = yhi[f, pl.ds(i * DEEP, 1), :]
        numer = jnp.zeros((ny, 128), F32)
        denom = jnp.zeros((ny, 128), F32)
        before = work[0, pl.ds(PAD, ny), :]
        center = work[1, pl.ds(PAD, ny), :]
        for i in range(nx):
            after = work[i + 2, pl.ds(PAD, ny), :]
            image = 6.0 * center - beside(work, i + 1, PAD, ny, center, before, after, lanes)
            numer = numer + center * image
            denom = denom + center * center
            before, center = center, after
        parts[pl.ds(pl.multiple_of(f * 8, 8), 8), :] = numer[0:8] + numer[8:16]
        parts[pl.ds(pl.multiple_of((cols + f) * 8, 8), 8), :] = denom[0:8] + denom[8:16]
        for out, high in ((ca, even), (cb, 1 - even)):
            rows = pl.ds(pl.multiple_of(high * half, half), half)
            out[f, pl.ds(0, half), :] = ylo[f, rows, :]
            out[f, pl.ds(half, half), :] = yhi[f, rows, :]

    by_pairs(cols, one)
    total = parts[pl.ds(0, 128, stride=8), :]
    for k in range(1, 8):
        total = total + parts[pl.ds(k, 128, stride=8), :]
    sums = dot_nt(jnp.ones((8, 128), F32), total)

    def spread(k, carry):
        out_ref[k] = sums
        return carry

    lax.fori_loop(0, out_ref.shape[0], spread, 0)


def pre_kernel(
    flags, sums, x_ref, ylo, yhi, xa, xb, ca, cb,
    r_ref, e_ref, c_ref, slo, shi, elo, ehi,
    works, others, rhss, smalls, coarse,
):
    cols, nx, ny, _ = x_ref.shape
    tall = ny + 2 * DEEP
    wide = nx + 2 * DEEP
    lanes = lane_index(tall)
    own = lane_index(ny)
    spot = lane_index(8)
    has = [flags[k].astype(F32) for k in range(4)]
    row = lax.broadcasted_iota(jnp.int32, (tall, 128), 0)
    mask_y = RELAX * jnp.where(row < DEEP, has[2], jnp.where(row >= ny + DEEP, has[3], 1.0))

    def relax_of(i):
        if i < DEEP:
            return mask_y * has[0]
        if i >= nx + DEEP:
            return mask_y * has[1]
        return mask_y

    even = flags[4]
    total = sums[0]
    for k in range(1, sums.shape[0]):
        total = total + sums[k]
    theta = total / pltpu.roll(total, 128 - cols, 1)

    @pl.when(jnp.bool_(True))
    def _():
        zero = jnp.zeros((8, 128), F32)
        for i in range(wide):
            for buf in (works, others):
                for u in range(2):
                    buf[u, i, pl.ds(0, PAD), :] = zero
                    buf[u, i, pl.ds(PAD + tall, 8), :] = zero

    data = pl.ds(PAD, tall)

    def one(f, u):
        work, other, rhs, small = works.at[u], others.at[u], rhss.at[u], smalls.at[u]
        th = jnp.sum(jnp.where(spot == f, theta, 0.0)) * 0.125
        for i in range(DEEP):
            for buf, corner, high in ((xa, ca, even), (xb, cb, 1 - even)):
                plane = high * (nx + DEEP) + i
                work[plane, pl.ds(PAD + DEEP, ny), :] = buf[f, i]
                buf = corner
                work[plane, pl.ds(PAD, DEEP), :] = buf[f, pl.ds(i * DEEP, DEEP), :]
                work[plane, pl.ds(PAD + DEEP + ny, DEEP), :] = buf[
                    f, pl.ds(DEEP * DEEP + i * DEEP, DEEP), :
                ]
        for i in range(nx):
            work[i + DEEP, pl.ds(PAD + DEEP, ny), :] = x_ref[f, i]
            work[i + DEEP, pl.ds(PAD, DEEP), :] = ylo[f, pl.ds(i * DEEP, DEEP), :]
            work[i + DEEP, pl.ds(PAD + DEEP + ny, DEEP), :] = yhi[f, pl.ds(i * DEEP, DEEP), :]
        before = work[0, data, :]
        center = work[1, data, :]
        for i in range(1, wide - 1):
            after = work[i + 1, data, :]
            image = 6.0 * center - beside(work, i, PAD, tall, center, before, after, lanes)
            res = image - th * center
            rhs[i] = res
            other[i, data, :] = relax_of(i) * res
            before, center = center, after
        src, dst = other, work
        for depth in (2, 3):
            before = src[depth - 1, data, :]
            center = src[depth, data, :]
            for i in range(depth, wide - depth):
                after = src[i + 1, data, :]
                near = beside(src, i, PAD, tall, center, before, after, lanes)
                dst[i, data, :] = center + relax_of(i) * (rhs[i] - 6.0 * center + near)
                before, center = center, after
            src, dst = dst, src
        own_rows = pl.ds(PAD + DEEP, ny)
        before = src[DEEP - 1, own_rows, :]
        center = src[DEEP, own_rows, :]
        held = None
        for i in range(DEEP, nx + DEEP):
            after = src[i + 1, own_rows, :]
            near = beside(src, i, PAD + DEEP, ny, center, before, after, own)
            rest = rhs[i, pl.ds(DEEP, ny), :] - 6.0 * center + near
            k = i - DEEP
            e_ref[f, k] = center
            elo[f, pl.ds(k * POST, POST), :] = e_ref[f, k, pl.ds(0, POST), :]
            ehi[f, pl.ds(k * POST, POST), :] = e_ref[f, k, pl.ds(ny - POST, POST), :]
            if held is None:
                held = rest
            else:
                small[...] = held + rest
                pair = small[pl.ds(0, ny // 2, stride=2), :] + small[pl.ds(1, ny // 2, stride=2), :]
                mate = jnp.where(
                    spot % 2 == 0, pltpu.roll(pair, 127, 1), pltpu.roll(pair, 1, 1)
                )
                coarse[f, (i - DEEP) // 2] = pair + mate
                held = None
            before, center = center, after
        for i in range(2, wide - 2):
            r_ref[f, i - 2] = rhs[i]

    by_pairs(cols, one)
    small = smalls.at[0]
    half, cx, cy = cols // 2, nx // 2, ny // 2
    even = spot % 2 == 0
    for g in range(half):
        for i in range(cx):
            both = jnp.where(even, coarse[g, i], coarse[g + half, i])
            c_ref[g, i] = both
            small[pl.ds(0, 8), :] = both
            at = (g * cx + i) * CO
            slo[pl.ds(at, CO), :] = small[pl.ds(0, CO), :]
            shi[pl.ds(at, CO), :] = small[pl.ds(cy - CO, CO), :]


def coarse_pack_kernel(deep, flags, c_ref, ylo, yhi, xa, xb):
    half, cx, cy, _ = c_ref.shape
    even = flags[4]
    tall = cy + 2 * deep
    for g in range(half):
        for out, first in ((xa, even * (cx - deep)), (xb, (1 - even) * (cx - deep))):
            for i in range(deep):
                at = (g * deep + i) * tall
                src = (g * cx + first + i) * deep
                out[pl.ds(at, deep), :] = ylo[pl.ds(src, deep), :]
                out[pl.ds(at + deep, cy), :] = c_ref[g, first + i]
                out[pl.ds(at + deep + cy, deep), :] = yhi[pl.ds(src, deep), :]


def coarse_kernel(
    flags, c_ref, ylo, yhi, xa, xb, corr_ref, slo, shi, works, others, rhss
):
    half, cx, cy, _ = c_ref.shape
    tall = cy + 2 * CO
    full = 16
    wide = cx + 2 * CO
    even = flags[4]
    lanes = lane_index(full)
    has = [flags[k].astype(F32) for k in range(4)]
    row = lax.broadcasted_iota(jnp.int32, (full, 128), 0)
    mask_y = COARSE_RELAX * jnp.where(row < CO, has[2], jnp.where(row >= cy + CO, has[3], 1.0))
    zero = jnp.zeros((8, 128), F32)
    for i in range(wide):
        for u in range(2):
            rhss[u, i, pl.ds(8, 8), :] = zero
            for buf in (works, others):
                buf[u, i, pl.ds(0, PAD), :] = zero
                buf[u, i, pl.ds(PAD + full, 8), :] = zero

    def relax_of(i):
        if i < CO:
            return mask_y * has[0]
        if i >= cx + CO:
            return mask_y * has[1]
        return mask_y

    data = pl.ds(PAD, full)

    def one(g, u):
        work, other, rhs = works.at[u], others.at[u], rhss.at[u]
        for i in range(CO):
            for buf, high in ((xa, even), (xb, 1 - even)):
                plane = high * (cx + CO) + i
                rhs[plane, pl.ds(0, tall), :] = buf[pl.ds((g * CO + i) * tall, tall), :]
        for i in range(cx):
            at = pl.ds((g * cx + i) * CO, CO)
            rhs[i + CO, pl.ds(0, CO), :] = ylo[at, :]
            rhs[i + CO, pl.ds(CO, cy), :] = c_ref[g, i]
            rhs[i + CO, pl.ds(CO + cy, CO), :] = yhi[at, :]
        for i in range(wide):
            work[i, data, :] = relax_of(i) * rhs[i]
        src, dst = work, other
        for depth in (1, 2, 3):
            before = src[depth - 1, data, :]
            center = src[depth, data, :]
            for i in range(depth, wide - depth):
                after = src[i + 1, data, :]
                near = beside(src, i, PAD, full, center, before, after, lanes, 2)
                dst[i, data, :] = center + relax_of(i) * (rhs[i] - 4.0 * (6.0 * center - near))
                before, center = center, after
            src, dst = dst, src
        for i in range(cx):
            corr_ref[g, i] = src[i + CO, pl.ds(PAD + CO, cy), :]
            at = pl.ds((g * cx + i) * CP, CP)
            slo[at, :] = src[i + CO, pl.ds(PAD + CO, CP), :]
            shi[at, :] = src[i + CO, pl.ds(PAD + CO + cy - CP, CP), :]

    by_pairs(half, one)


def post_pack_kernel(flags, corr_ref, ylo, yhi, xa, xb):
    cols, nx, ny, _ = corr_ref.shape
    even = flags[4]
    tall = ny + 2 * POST

    def body(f, carry):
        for out, first in ((xa, even * (nx - POST)), (xb, (1 - even) * (nx - POST))):
            for i in range(POST):
                at = (f * POST + i) * tall
                src = pl.ds((first + i) * POST, POST)
                out[pl.ds(at, POST), :] = ylo[f, src, :]
                out[pl.ds(at + POST, ny), :] = corr_ref[f, first + i]
                out[pl.ds(at + POST + ny, POST), :] = yhi[f, src, :]
        return carry

    lax.fori_loop(0, cols, body, 0)


def post_kernel(
    flags, e_ref, ylo, yhi, xa, xb, c_ref, cylo, cyhi, cxa, cxb, r_ref,
    w_ref, image_ref, works, others, coarses, smalls,
):
    cols, nx, ny, _ = e_ref.shape
    _, cx, cy, _ = c_ref.shape
    ctall = cy + 2 * CP
    parity = lane_index(16) % 2
    coarses[:, :, pl.ds(8, 8), :] = jnp.zeros((2, cx + 2 * CP, 8, 128), F32)
    tall = ny + 2 * DEEP
    wide = nx + 2 * POST
    span = ny + 2 * POST
    gap = DEEP - POST
    even = flags[4]
    lanes = lane_index(tall)
    own = lane_index(ny)
    has = [flags[k].astype(F32) for k in range(4)]
    row = lax.broadcasted_iota(jnp.int32, (tall, 128), 0)
    mask_y = RELAX * jnp.where(row < DEEP, has[2], jnp.where(row >= ny + DEEP, has[3], 1.0))
    zero = jnp.zeros((PAD + 8, 128), F32)
    for i in range(wide):
        for buf in (works, others):
            for u in range(2):
                buf[u, i, pl.ds(0, PAD + 8), :] = zero
                buf[u, i, pl.ds(PAD + tall - 8, 16), :] = zero

    def relax_of(i):
        if i < POST:
            return mask_y * has[0]
        if i >= nx + POST:
            return mask_y * has[1]
        return mask_y

    data = pl.ds(PAD, tall)

    def one(f, u):
        work, other, coarse, small = works.at[u], others.at[u], coarses.at[0], smalls.at[u]
        if u == 0:
            g = f
            for i in range(CP):
                at = pl.ds((g * CP + i) * ctall, ctall)
                for buf, high in ((cxa, even), (cxb, 1 - even)):
                    coarse[high * (cx + CP) + i, pl.ds(0, ctall), :] = buf[at, :]
            for i in range(cx):
                at = pl.ds((g * cx + i) * CP, CP)
                coarse[i + CP, pl.ds(0, CP), :] = cylo[at, :]
                coarse[i + CP, pl.ds(CP, cy), :] = c_ref[g, i]
                coarse[i + CP, pl.ds(CP + cy, CP), :] = cyhi[at, :]
        for i in range(POST):
            at = pl.ds((f * POST + i) * span, span)
            for buf, high in ((xa, even), (xb, 1 - even)):
                work[high * (nx + POST) + i, pl.ds(PAD + gap, span), :] = buf[at, :]
        for i in range(nx):
            at = pl.ds(i * POST, POST)
            work[i + POST, pl.ds(PAD + gap, POST), :] = ylo[f, at, :]
            work[i + POST, pl.ds(PAD + DEEP, ny), :] = e_ref[f, i]
            work[i + POST, pl.ds(PAD + DEEP + ny, POST), :] = yhi[f, at, :]
        for m in range(cx + 2 * CP):
            both = coarse[m]
            value = jnp.where(parity == u, both, pltpu.roll(both, 127 if u else 1, 1))
            small[m % 2, pl.ds(0, 16, stride=2), :] = value
            small[m % 2, pl.ds(1, 16, stride=2), :] = value
            up = small[m % 2, pl.ds(0, tall), :]
            for i in (2 * m - 1, 2 * m):
                if 0 <= i < wide:
                    work[i, data, :] = work[i, data, :] + up
        src, dst = work, other
        for depth in (1, 2):
            before = src[depth - 1, data, :]
            center = src[depth, data, :]
            for i in range(depth, wide - depth):
                after = src[i + 1, data, :]
                near = beside(src, i, PAD, tall, center, before, after, lanes)
                dst[i, data, :] = center + relax_of(i) * (r_ref[f, i - 1] - 6.0 * center + near)
                before, center = center, after
            src, dst = dst, src
        own_rows = pl.ds(PAD + DEEP, ny)
        before = src[POST - 1, own_rows, :]
        center = src[POST, own_rows, :]
        for i in range(POST, nx + POST):
            after = src[i + 1, own_rows, :]
            near = beside(src, i, PAD + DEEP, ny, center, before, after, own)
            rows = pl.ds((i - POST) * ny * cols + f, ny, stride=cols)
            w_ref[rows, :] = center
            image_ref[rows, :] = 6.0 * center - near
            before, center = center, after

    by_pairs(cols, one)


def image_kernel(flags, x_ref, p_ref, ylo, yhi, xa, xb, tx_ref, tp_ref, ax_ref, ap_ref, work):
    cols, nx, ny, _ = x_ref.shape
    even = flags[4]
    lanes = lane_index(ny)

    def body(f, carry):
        for ref, same, out, first, base, deep in (
            (x_ref, tx_ref, ax_ref, 0, 0, DEEP),
            (p_ref, tp_ref, ap_ref, DEEP, nx * DEEP, 1),
        ):
            for buf, high in ((xa, even), (xb, 1 - even)):
                plane = first + (1 - high) * (deep - 1)
                work[high * (nx + 1), pl.ds(PAD, ny), :] = buf[f, plane]
            for i in range(nx):
                work[i + 1, pl.ds(PAD, ny), :] = ref[f, i]
                work[i + 1, pl.ds(PAD - 1, 1), :] = ylo[f, pl.ds(base + i * deep + deep - 1, 1), :]
                work[i + 1, pl.ds(PAD + ny, 1), :] = yhi[f, pl.ds(base + i * deep, 1), :]
            before = work[0, pl.ds(PAD, ny), :]
            center = work[1, pl.ds(PAD, ny), :]
            for i in range(nx):
                after = work[i + 2, pl.ds(PAD, ny), :]
                near = beside(work, i + 1, PAD, ny, center, before, after, lanes)
                rows = pl.ds(i * ny * cols + f, ny, stride=cols)
                same[rows, :] = center
                out[rows, :] = 6.0 * center - near
                before, center = center, after
        return carry

    lax.fori_loop(0, cols, body, 0)


def from_low(value, axis):
    count = lax.axis_size(axis)
    return lax.ppermute(value, axis, [(i, i + 1) for i in range(count - 1)])


def from_high(value, axis):
    count = lax.axis_size(axis)
    return lax.ppermute(value, axis, [(i + 1, i) for i in range(count - 1)])


def swap(one, two, axis):
    count = lax.axis_size(axis)
    pairs = [[], []]
    for i in range(count - 1):
        pairs[i % 2] += [(i, i + 1), (i + 1, i)]
    two = lax.ppermute(two, axis, pairs[1])
    return lax.ppermute(one, axis, pairs[0]), two


def radices(count):
    out = []
    if count % 2 == 0 and count % 4 == 0 and (count.bit_length() - 1) % 2 == 1:
        out.append(2)
        count //= 2
    while count % 4 == 0:
        out.append(4)
        count //= 4
    if count > 1:
        out.append(count)
    return out


def sum_all(value):
    for axis in ("gy", "gx"):
        count = lax.axis_size(axis)
        stride = 1
        for radix in radices(count):
            index = lax.axis_index(axis)
            parts = [value]
            for k in range(1, radix):
                pairs = []
                for i in range(count):
                    digit = i // stride % radix
                    target = i + ((digit + k) % radix - digit) * stride
                    pairs.append((i, target))
                parts.append(lax.ppermute(value, axis, pairs))
            digit = index // stride % radix
            if radix == 2:
                value = parts[0] + parts[1]
            elif radix == 4:
                even = parts[0] + parts[2]
                odd = parts[1] + parts[3]
                value = even + odd
            else:
                value = functools.reduce(jnp.add, parts)
            stride *= radix
    return value


BF16 = jnp.bfloat16


def gram_kernel(x_ref, w_ref, p_ref, ax_ref, aw_ref, ap_ref, out_ref, s_ref, image):
    chunks, rows, wide = s_ref.shape
    cols = rows // 6
    ny = wide // 128

    def body(c, carry):
        for k, (b_ref, a_ref) in enumerate(((x_ref, ax_ref), (w_ref, aw_ref), (p_ref, ap_ref))):
            for y in range(ny):
                pick = pl.ds(pl.multiple_of((c * ny + y) * cols, cols), cols)
                at = pl.ds(y * 128, 128)
                for ref, put in (
                    (b_ref, lambda r, v: s_ref.__setitem__((c, r, at), v)),
                    (a_ref, lambda r, v: image.__setitem__((r, at), v)),
                ):
                    value = ref[pick, :]
                    high = value.astype(BF16)
                    low = (value - high.astype(F32)).astype(BF16)
                    put(pl.ds(k * cols, cols), high)
                    put(pl.ds((3 + k) * cols, cols), low)
        left = s_ref[c]
        dims = (((1,), (1,)), ((), ()))
        proj = lax.dot_general(left, image[...], dims, preferred_element_type=F32)
        gram = lax.dot_general(left, left, dims, preferred_element_type=F32)
        return (carry[0] + proj, carry[1] + gram)

    zero = jnp.zeros((rows, rows), F32)
    proj, gram = lax.fori_loop(0, chunks, body, (zero, zero))
    nb = 3 * cols
    for k, full in enumerate((proj, gram)):
        full = full[:nb] + full[nb:]
        out_ref[:, pl.ds(k * nb, nb)] = full[:, :nb] + full[:, nb:]


def eliminate(left, right, first):
    size = left.shape[0]
    tiles = size // 8
    lefts = [left[8 * t : 8 * t + 8] for t in range(tiles)]
    rights = [right[8 * t : 8 * t + 8] for t in range(tiles)]
    row = lax.broadcasted_iota(jnp.int32, (8, 1), 0)
    scales = [jnp.zeros((8, 1), F32) for _ in range(tiles)]
    for k in range(size):
        own, at = k // 8, k % 8
        line, other = lefts[own][at : at + 1], rights[own][at : at + 1]
        pivot = line[:, first + k : first + k + 1]
        inverse = 1.0 / pivot
        line, other = line * inverse, other * inverse
        scales[own] = jnp.where(row == at, pivot, scales[own])
        for t in range(own, tiles):
            column = lefts[t][:, first + k : first + k + 1]
            if t == own:
                column = jnp.where(row > at, column, 0.0)
            lefts[t] = lefts[t] - column * line
            rights[t] = rights[t] - column * other
    scales = [lax.rsqrt(scale) for scale in scales]
    return (
        jnp.concatenate([v * scale for v, scale in zip(lefts, scales)], axis=0),
        jnp.concatenate([v * scale for v, scale in zip(rights, scales)], axis=0),
    )


def finish_kernel(ncells, sums_ref, s_ref, block_ref, search_ref, bufs, sems):
    nb = sums_ref.shape[0]
    cols = nb // 3
    chunks, rows, wide = s_ref.shape
    ny = wide // 128
    row = lax.broadcasted_iota(jnp.int32, (nb, 128), 0)
    lane = lax.broadcasted_iota(jnp.int32, (nb, 128), 1)
    eye = jnp.where((lane == row) | (lane == row + nb), 1.0, 0.0)
    left, inverse = eliminate(sums_ref[...], eye, nb)
    flat = -dot_nt(inverse[:cols, :nb], left[:, :nb])
    flat = flat + jnp.where(lane[:cols, :nb] == row[:cols, :nb], SHIFT, 0.0)
    _, scaled = eliminate(dot_nt(flat, flat), flat, 0)
    coef = jnp.dot(
        scaled, inverse, precision=lax.Precision.HIGHEST, preferred_element_type=F32
    )
    coef = coef[:, :rows] * jnp.sqrt(F32(ncells))
    slot = lax.broadcasted_iota(jnp.int32, (cols, rows), 1)
    first = (slot < cols) | ((slot >= nb) & (slot < nb + cols))
    terms = []
    for part in (jnp.where(first, coef, 0.0), jnp.where(first, 0.0, coef)):
        high = part.astype(BF16)
        terms += [high, (part - high.astype(F32)).astype(BF16)]
    terms = jnp.concatenate(terms, axis=0)

    def copies(c):
        return [
            pltpu.make_async_copy(bufs.at[c, k], ref.at[:, c], sems.at[c, k])
            for k, ref in enumerate((block_ref, search_ref))
        ]

    def chunk(c, carry):
        for y in range(0, ny, 2):
            got = jnp.dot(
                terms, s_ref[c, :, pl.ds(y * 128, 256)], preferred_element_type=F32
            )
            search = got[2 * cols : 3 * cols] + got[3 * cols :]
            block = search + (got[:cols] + got[cols : 2 * cols])
            for k, value in enumerate((block, search)):
                for j in range(2):
                    flat = bufs.at[c, k].reshape(cols * ny, 128)
                    flat[pl.ds(y + j, cols, stride=ny), :] = value[:, j * 128 : (j + 1) * 128]
        for copy in copies(c):
            copy.start()
        return carry

    def finish(c, carry):
        for copy in copies(c):
            copy.wait()
        return carry

    lax.fori_loop(0, chunks, chunk, 0, unroll=4 if chunks % 4 == 0 else 1)
    lax.fori_loop(0, chunks, finish, 0)


def step(x, p):
    cols, nx, ny, nz = x.shape
    ngx, ngy = lax.axis_size("gx"), lax.axis_size("gy")
    ix, iy = lax.axis_index("gx"), lax.axis_index("gy")
    flags = jnp.stack([ix > 0, ix < ngx - 1, iy > 0, iy < ngy - 1, ix % 2 == 0]).astype(jnp.int32)
    half, cx, cy = cols // 2, nx // 2, ny // 2
    work = pltpu.VMEM

    yrows = nx * DEEP + nx
    to_ylo, to_yhi, to_xlo, to_xhi = call(
        pack_kernel,
        [shape(cols, yrows, nz)] * 2 + [shape(cols, DEEP + 1, ny, nz)] * 2,
        [], (flags, x, p), smem=1,
    )
    ylo, yhi = from_low(to_yhi, "gy"), from_high(to_ylo, "gy")
    xlo, xhi = swap(to_xlo, to_xhi, "gx")

    devices = ngx * ngy
    sums, to_clo, to_chi = call(
        theta_kernel,
        [shape(devices, 8, 128)] + [shape(cols, nx * DEEP, nz)] * 2,
        [work((2, nx + 2, PAD + ny + 8, nz), F32), work((128 * 8, nz), F32)],
        (flags, x, ylo, yhi, xlo, xhi), smem=1,
    )
    clo, chi = swap(to_clo, to_chi, "gx")
    sums = lax.all_to_all(sums, ("gx", "gy"), 0, 0)

    tall, wide = ny + 2 * DEEP, nx + 2 * DEEP
    plane = PAD + tall + 8
    r, e, c, to_ylo, to_yhi, to_eylo, to_eyhi = call(
        pre_kernel,
        [shape(cols, wide - 4, tall, nz), shape(cols, nx, ny, nz), shape(half, cx, cy, nz)]
        + [shape(half * cx * CO, nz)] * 2
        + [shape(cols, nx * POST, nz)] * 2,
        [work((2, wide, plane, nz), F32)] * 2
        + [work((2, wide, tall, nz), F32), work((2, ny, nz), F32), work((cols, cx, cy, nz), F32)],
        (flags, sums, x, ylo, yhi, xlo, xhi, clo, chi), smem=1,
    )

    cylo, cyhi = from_low(to_yhi, "gy"), from_high(to_ylo, "gy")
    eylo, eyhi = from_low(to_eyhi, "gy"), from_high(to_eylo, "gy")
    to_xlo, to_xhi = call(
        functools.partial(coarse_pack_kernel, CO),
        [shape(half * CO * (cy + 2 * CO), nz)] * 2, [], (flags, c, cylo, cyhi), smem=1,
    )
    cxlo, cxhi = swap(to_xlo, to_xhi, "gx")
    to_exlo, to_exhi = call(
        post_pack_kernel, [shape(cols * POST * (ny + 2 * POST), nz)] * 2, [],
        (flags, e, eylo, eyhi), smem=1,
    )
    exlo, exhi = swap(to_exlo, to_exhi, "gx")
    cwide = cx + 2 * CO
    d, to_ylo, to_yhi = call(
        coarse_kernel,
        [shape(half, cx, cy, nz)] + [shape(half * cx * CP, nz)] * 2,
        [work((2, cwide, PAD + 16 + 8, nz), F32)] * 2 + [work((2, cwide, 16, nz), F32)],
        (flags, c, cylo, cyhi, cxlo, cxhi), smem=1,
    )
    dylo, dyhi = from_low(to_yhi, "gy"), from_high(to_ylo, "gy")
    to_xlo, to_xhi = call(
        functools.partial(coarse_pack_kernel, CP),
        [shape(half * CP * (cy + 2 * CP), nz)] * 2, [], (flags, d, dylo, dyhi), smem=1,
    )
    dxlo, dxhi = swap(to_xlo, to_xhi, "gx")

    flat_x, flat_p, image_x, image_p = call(
        image_kernel, [shape(nx * ny * cols, nz)] * 4,
        [work((nx + 2, PAD + ny + 8, nz), F32)],
        (flags, x, p, ylo, yhi, xlo, xhi), smem=1,
    )
    w, image_w = call(
        post_kernel, [shape(nx * ny * cols, nz)] * 2,
        [work((2, nx + 2 * POST, plane, nz), F32)] * 2
        + [work((2, cx + 2 * CP, 16, nz), F32), work((2, 2, 32, nz), F32)],
        (flags, e, eylo, eyhi, exlo, exhi, d, dylo, dyhi, dxlo, dxhi, r), smem=1,
    )

    flat = (flat_x, w, flat_p, image_x, image_w, image_p)
    nb = 3 * cols
    part, split = call(
        gram_kernel,
        [shape(nb, 128), pltpu.VMEM((nx, 2 * nb, ny * nz), BF16)],
        [work((2 * nb, ny * nz), BF16)],
        flat,
    )
    part = sum_all(part)
    any_space = pl.BlockSpec(memory_space=pl.ANY)
    new_block, new_search = pl.pallas_call(
        functools.partial(finish_kernel, nx * ny * nz * devices),
        out_shape=[jax.ShapeDtypeStruct((cols, nx, ny, nz), F32)] * 2,
        in_specs=[VMEM, VMEM],
        out_specs=[any_space] * 2,
        scratch_shapes=[
            work((nx, 2, cols, ny, nz), F32),
            pltpu.SemaphoreType.DMA((nx, 2)),
        ],
        compiler_params=pltpu.CompilerParams(vmem_limit_bytes=GRANT),
        name="finish",
    )(part, split)
    return (new_block, new_search)


def solution(mesh):
    spec = P(None, "gx", "gy", None)
    return jax.shard_map(
        step, mesh=mesh, in_specs=(spec, spec), out_specs=(spec, spec), check_vma=False
    )
```

```python
import functools

import jax
import jax.numpy as jnp
from jax import lax
from jax.experimental import pallas as pl
from jax.experimental.pallas import tpu as pltpu
from jax.sharding import PartitionSpec as P


RELAX = 1.0 / 9.0
COARSE_RELAX = 1.0 / 36.0
SHIFT = 13.0
DEEP = 4
POST = 3
CO = 3
CP = 2
PAD = 8

GRANT = 20 << 20

F32 = jnp.float32
VMEM = pl.BlockSpec(memory_space=pltpu.VMEM)
SMEM = pl.BlockSpec(memory_space=pltpu.SMEM)


def shape(*dims):
    return pltpu.VMEM(dims, F32)


def call(kernel, outs, scratch, args, smem=0):
    specs = [SMEM] * smem + [VMEM] * (len(args) - smem)
    return pl.pallas_call(
        kernel,
        out_shape=outs,
        in_specs=specs,
        out_specs=[VMEM] * len(outs),
        scratch_shapes=scratch,
        compiler_params=pltpu.CompilerParams(vmem_limit_bytes=GRANT),
    )(*args)


def along_z(plane, step, lanes):
    size = plane.shape[-1]
    low = jnp.where(lanes >= step, pltpu.roll(plane, step, 1), 0.0)
    high = jnp.where(lanes < size - step, pltpu.roll(plane, size - step, 1), 0.0)
    return low + high


def beside(work, i, row, rows, center, before, after, lanes, step=1):
    total = before + after
    total = total + work[i, pl.ds(row - 1, rows), :] + work[i, pl.ds(row + 1, rows), :]
    return total + along_z(center, step, lanes)


def dot_nt(a, b):
    return lax.dot_general(
        a, b, (((1,), (1,)), ((), ())),
        precision=lax.Precision.HIGHEST, preferred_element_type=F32,
    )


def by_pairs(cols, one):
    def body(h, carry):
        for u in range(2):
            one(h + u * (cols // 2), u)
        return carry

    lax.fori_loop(0, cols // 2, body, 0)


def lane_index(rows):
    return lax.broadcasted_iota(jnp.int32, (rows, 128), 1)


def pack_kernel(flags, x_ref, p_ref, ylo, yhi, xa, xb):
    cols, nx, ny, _ = x_ref.shape
    even = flags[4]

    def body(f, carry):
        for i in range(nx):
            ylo[f, pl.ds(i * DEEP, DEEP), :] = x_ref[f, i, pl.ds(0, DEEP), :]
            yhi[f, pl.ds(i * DEEP, DEEP), :] = x_ref[f, i, pl.ds(ny - DEEP, DEEP), :]
            ylo[f, pl.ds(nx * DEEP + i, 1), :] = p_ref[f, i, pl.ds(0, 1), :]
            yhi[f, pl.ds(nx * DEEP + i, 1), :] = p_ref[f, i, pl.ds(ny - 1, 1), :]
        for out, high in ((xa, even), (xb, 1 - even)):
            for i in range(DEEP):
                out[f, i] = x_ref[f, high * (nx - DEEP) + i]
            out[f, DEEP] = p_ref[f, high * (nx - 1)]
        return carry

    lax.fori_loop(0, cols, body, 0)


def theta_kernel(flags, x_ref, ylo, yhi, xa, xb, out_ref, ca, cb, works, parts):
    cols, nx, ny, _ = x_ref.shape
    lanes = lane_index(ny)
    half = nx // 2 * DEEP
    even = flags[4]
    parts[pl.ds(2 * cols * 8, 128 * 8 - 2 * cols * 8), :] = jnp.ones((128 * 8 - 2 * cols * 8, 128), F32)

    def one(f, u):
        work = works.at[u]
        for buf, high in ((xa, even), (xb, 1 - even)):
            work[high * (nx + 1), pl.ds(PAD, ny), :] = buf[f, (1 - high) * (DEEP - 1)]
        for i in range(nx):
            work[i + 1, pl.ds(PAD, ny), :] = x_ref[f, i]
            work[i + 1, pl.ds(PAD - 1, 1), :] = ylo[f, pl.ds(i * DEEP + DEEP - 1, 1), :]
            work[i + 1, pl.ds(PAD + ny, 1), :] = yhi[f, pl.ds(i * DEEP, 1), :]
        numer = jnp.zeros((ny, 128), F32)
        denom = jnp.zeros((ny, 128), F32)
        before = work[0, pl.ds(PAD, ny), :]
        center = work[1, pl.ds(PAD, ny), :]
        for i in range(nx):
            after = work[i + 2, pl.ds(PAD, ny), :]
            image = 6.0 * center - beside(work, i + 1, PAD, ny, center, before, after, lanes)
            numer = numer + center * image
            denom = denom + center * center
            before, center = center, after
        parts[pl.ds(pl.multiple_of(f * 8, 8), 8), :] = numer[0:8] + numer[8:16]
        parts[pl.ds(pl.multiple_of((cols + f) * 8, 8), 8), :] = denom[0:8] + denom[8:16]
        for out, high in ((ca, even), (cb, 1 - even)):
            rows = pl.ds(pl.multiple_of(high * half, half), half)
            out[f, pl.ds(0, half), :] = ylo[f, rows, :]
            out[f, pl.ds(half, half), :] = yhi[f, rows, :]

    by_pairs(cols, one)
    total = parts[pl.ds(0, 128, stride=8), :]
    for k in range(1, 8):
        total = total + parts[pl.ds(k, 128, stride=8), :]
    sums = dot_nt(jnp.ones((8, 128), F32), total)

    def spread(k, carry):
        out_ref[k] = sums
        return carry

    lax.fori_loop(0, out_ref.shape[0], spread, 0)


def pre_kernel(
    flags, sums, x_ref, ylo, yhi, xa, xb, ca, cb,
    r_ref, e_ref, c_ref, slo, shi, elo, ehi,
    works, others, rhss, smalls, coarse,
):
    cols, nx, ny, _ = x_ref.shape
    tall = ny + 2 * DEEP
    wide = nx + 2 * DEEP
    lanes = lane_index(tall)
    own = lane_index(ny)
    spot = lane_index(8)
    has = [flags[k].astype(F32) for k in range(4)]
    row = lax.broadcasted_iota(jnp.int32, (tall, 128), 0)
    mask_y = RELAX * jnp.where(row < DEEP, has[2], jnp.where(row >= ny + DEEP, has[3], 1.0))

    def relax_of(i):
        if i < DEEP:
            return mask_y * has[0]
        if i >= nx + DEEP:
            return mask_y * has[1]
        return mask_y

    even = flags[4]
    total = sums[0]
    for k in range(1, sums.shape[0]):
        total = total + sums[k]
    theta = total / pltpu.roll(total, 128 - cols, 1)

    @pl.when(jnp.bool_(True))
    def _():
        zero = jnp.zeros((8, 128), F32)
        for i in range(wide):
            for buf in (works, others):
                for u in range(2):
                    buf[u, i, pl.ds(0, PAD), :] = zero
                    buf[u, i, pl.ds(PAD + tall, 8), :] = zero

    data = pl.ds(PAD, tall)

    def one(f, u):
        work, other, rhs, small = works.at[u], others.at[u], rhss.at[u], smalls.at[u]
        th = jnp.sum(jnp.where(spot == f, theta, 0.0)) * 0.125
        for i in range(DEEP):
            for buf, corner, high in ((xa, ca, even), (xb, cb, 1 - even)):
                plane = high * (nx + DEEP) + i
                work[plane, pl.ds(PAD + DEEP, ny), :] = buf[f, i]
                buf = corner
                work[plane, pl.ds(PAD, DEEP), :] = buf[f, pl.ds(i * DEEP, DEEP), :]
                work[plane, pl.ds(PAD + DEEP + ny, DEEP), :] = buf[
                    f, pl.ds(DEEP * DEEP + i * DEEP, DEEP), :
                ]
        for i in range(nx):
            work[i + DEEP, pl.ds(PAD + DEEP, ny), :] = x_ref[f, i]
            work[i + DEEP, pl.ds(PAD, DEEP), :] = ylo[f, pl.ds(i * DEEP, DEEP), :]
            work[i + DEEP, pl.ds(PAD + DEEP + ny, DEEP), :] = yhi[f, pl.ds(i * DEEP, DEEP), :]
        before = work[0, data, :]
        center = work[1, data, :]
        for i in range(1, wide - 1):
            after = work[i + 1, data, :]
            image = 6.0 * center - beside(work, i, PAD, tall, center, before, after, lanes)
            res = image - th * center
            rhs[i] = res
            other[i, data, :] = relax_of(i) * res
            before, center = center, after
        src, dst = other, work
        for depth in (2, 3):
            before = src[depth - 1, data, :]
            center = src[depth, data, :]
            for i in range(depth, wide - depth):
                after = src[i + 1, data, :]
                near = beside(src, i, PAD, tall, center, before, after, lanes)
                dst[i, data, :] = center + relax_of(i) * (rhs[i] - 6.0 * center + near)
                before, center = center, after
            src, dst = dst, src
        own_rows = pl.ds(PAD + DEEP, ny)
        before = src[DEEP - 1, own_rows, :]
        center = src[DEEP, own_rows, :]
        held = None
        for i in range(DEEP, nx + DEEP):
            after = src[i + 1, own_rows, :]
            near = beside(src, i, PAD + DEEP, ny, center, before, after, own)
            rest = rhs[i, pl.ds(DEEP, ny), :] - 6.0 * center + near
            k = i - DEEP
            e_ref[f, k] = center
            elo[f, pl.ds(k * POST, POST), :] = e_ref[f, k, pl.ds(0, POST), :]
            ehi[f, pl.ds(k * POST, POST), :] = e_ref[f, k, pl.ds(ny - POST, POST), :]
            if held is None:
                held = rest
            else:
                small[...] = held + rest
                pair = small[pl.ds(0, ny // 2, stride=2), :] + small[pl.ds(1, ny // 2, stride=2), :]
                mate = jnp.where(
                    spot % 2 == 0, pltpu.roll(pair, 127, 1), pltpu.roll(pair, 1, 1)
                )
                coarse[f, (i - DEEP) // 2] = pair + mate
                held = None
            before, center = center, after
        for i in range(2, wide - 2):
            r_ref[f, i - 2] = rhs[i]

    by_pairs(cols, one)
    small = smalls.at[0]
    half, cx, cy = cols // 2, nx // 2, ny // 2
    even = spot % 2 == 0
    for g in range(half):
        for i in range(cx):
            both = jnp.where(even, coarse[g, i], coarse[g + half, i])
            c_ref[g, i] = both
            small[pl.ds(0, 8), :] = both
            at = (g * cx + i) * CO
            slo[pl.ds(at, CO), :] = small[pl.ds(0, CO), :]
            shi[pl.ds(at, CO), :] = small[pl.ds(cy - CO, CO), :]


def coarse_pack_kernel(deep, flags, c_ref, ylo, yhi, xa, xb):
    half, cx, cy, _ = c_ref.shape
    even = flags[4]
    tall = cy + 2 * deep
    for g in range(half):
        for out, first in ((xa, even * (cx - deep)), (xb, (1 - even) * (cx - deep))):
            for i in range(deep):
                at = (g * deep + i) * tall
                src = (g * cx + first + i) * deep
                out[pl.ds(at, deep), :] = ylo[pl.ds(src, deep), :]
                out[pl.ds(at + deep, cy), :] = c_ref[g, first + i]
                out[pl.ds(at + deep + cy, deep), :] = yhi[pl.ds(src, deep), :]


def coarse_kernel(
    flags, c_ref, ylo, yhi, xa, xb, corr_ref, slo, shi, works, others, rhss
):
    half, cx, cy, _ = c_ref.shape
    tall = cy + 2 * CO
    full = 16
    wide = cx + 2 * CO
    even = flags[4]
    lanes = lane_index(full)
    has = [flags[k].astype(F32) for k in range(4)]
    row = lax.broadcasted_iota(jnp.int32, (full, 128), 0)
    mask_y = COARSE_RELAX * jnp.where(row < CO, has[2], jnp.where(row >= cy + CO, has[3], 1.0))
    zero = jnp.zeros((8, 128), F32)
    for i in range(wide):
        for u in range(2):
            rhss[u, i, pl.ds(8, 8), :] = zero
            for buf in (works, others):
                buf[u, i, pl.ds(0, PAD), :] = zero
                buf[u, i, pl.ds(PAD + full, 8), :] = zero

    def relax_of(i):
        if i < CO:
            return mask_y * has[0]
        if i >= cx + CO:
            return mask_y * has[1]
        return mask_y

    data = pl.ds(PAD, full)

    def one(g, u):
        work, other, rhs = works.at[u], others.at[u], rhss.at[u]
        for i in range(CO):
            for buf, high in ((xa, even), (xb, 1 - even)):
                plane = high * (cx + CO) + i
                rhs[plane, pl.ds(0, tall), :] = buf[pl.ds((g * CO + i) * tall, tall), :]
        for i in range(cx):
            at = pl.ds((g * cx + i) * CO, CO)
            rhs[i + CO, pl.ds(0, CO), :] = ylo[at, :]
            rhs[i + CO, pl.ds(CO, cy), :] = c_ref[g, i]
            rhs[i + CO, pl.ds(CO + cy, CO), :] = yhi[at, :]
        for i in range(wide):
            work[i, data, :] = relax_of(i) * rhs[i]
        src, dst = work, other
        for depth in (1, 2, 3):
            before = src[depth - 1, data, :]
            center = src[depth, data, :]
            for i in range(depth, wide - depth):
                after = src[i + 1, data, :]
                near = beside(src, i, PAD, full, center, before, after, lanes, 2)
                dst[i, data, :] = center + relax_of(i) * (rhs[i] - 4.0 * (6.0 * center - near))
                before, center = center, after
            src, dst = dst, src
        for i in range(cx):
            corr_ref[g, i] = src[i + CO, pl.ds(PAD + CO, cy), :]
            at = pl.ds((g * cx + i) * CP, CP)
            slo[at, :] = src[i + CO, pl.ds(PAD + CO, CP), :]
            shi[at, :] = src[i + CO, pl.ds(PAD + CO + cy - CP, CP), :]

    by_pairs(half, one)


def post_pack_kernel(flags, corr_ref, ylo, yhi, xa, xb):
    cols, nx, ny, _ = corr_ref.shape
    even = flags[4]
    tall = ny + 2 * POST

    def body(f, carry):
        for out, first in ((xa, even * (nx - POST)), (xb, (1 - even) * (nx - POST))):
            for i in range(POST):
                at = (f * POST + i) * tall
                src = pl.ds((first + i) * POST, POST)
                out[pl.ds(at, POST), :] = ylo[f, src, :]
                out[pl.ds(at + POST, ny), :] = corr_ref[f, first + i]
                out[pl.ds(at + POST + ny, POST), :] = yhi[f, src, :]
        return carry

    lax.fori_loop(0, cols, body, 0)


def post_kernel(
    flags, e_ref, ylo, yhi, xa, xb, c_ref, cylo, cyhi, cxa, cxb, r_ref,
    w_ref, image_ref, works, others, coarses, smalls,
):
    cols, nx, ny, _ = e_ref.shape
    _, cx, cy, _ = c_ref.shape
    ctall = cy + 2 * CP
    parity = lane_index(16) % 2
    coarses[:, :, pl.ds(8, 8), :] = jnp.zeros((2, cx + 2 * CP, 8, 128), F32)
    tall = ny + 2 * DEEP
    wide = nx + 2 * POST
    span = ny + 2 * POST
    gap = DEEP - POST
    even = flags[4]
    lanes = lane_index(tall)
    own = lane_index(ny)
    has = [flags[k].astype(F32) for k in range(4)]
    row = lax.broadcasted_iota(jnp.int32, (tall, 128), 0)
    mask_y = RELAX * jnp.where(row < DEEP, has[2], jnp.where(row >= ny + DEEP, has[3], 1.0))
    zero = jnp.zeros((PAD + 8, 128), F32)
    for i in range(wide):
        for buf in (works, others):
            for u in range(2):
                buf[u, i, pl.ds(0, PAD + 8), :] = zero
                buf[u, i, pl.ds(PAD + tall - 8, 16), :] = zero

    def relax_of(i):
        if i < POST:
            return mask_y * has[0]
        if i >= nx + POST:
            return mask_y * has[1]
        return mask_y

    data = pl.ds(PAD, tall)

    def one(f, u):
        work, other, coarse, small = works.at[u], others.at[u], coarses.at[0], smalls.at[u]
        if u == 0:
            g = f
            for i in range(CP):
                at = pl.ds((g * CP + i) * ctall, ctall)
                for buf, high in ((cxa, even), (cxb, 1 - even)):
                    coarse[high * (cx + CP) + i, pl.ds(0, ctall), :] = buf[at, :]
            for i in range(cx):
                at = pl.ds((g * cx + i) * CP, CP)
                coarse[i + CP, pl.ds(0, CP), :] = cylo[at, :]
                coarse[i + CP, pl.ds(CP, cy), :] = c_ref[g, i]
                coarse[i + CP, pl.ds(CP + cy, CP), :] = cyhi[at, :]
        for i in range(POST):
            at = pl.ds((f * POST + i) * span, span)
            for buf, high in ((xa, even), (xb, 1 - even)):
                work[high * (nx + POST) + i, pl.ds(PAD + gap, span), :] = buf[at, :]
        for i in range(nx):
            at = pl.ds(i * POST, POST)
            work[i + POST, pl.ds(PAD + gap, POST), :] = ylo[f, at, :]
            work[i + POST, pl.ds(PAD + DEEP, ny), :] = e_ref[f, i]
            work[i + POST, pl.ds(PAD + DEEP + ny, POST), :] = yhi[f, at, :]
        for m in range(cx + 2 * CP):
            both = coarse[m]
            value = jnp.where(parity == u, both, pltpu.roll(both, 127 if u else 1, 1))
            small[m % 2, pl.ds(0, 16, stride=2), :] = value
            small[m % 2, pl.ds(1, 16, stride=2), :] = value
            up = small[m % 2, pl.ds(0, tall), :]
            for i in (2 * m - 1, 2 * m):
                if 0 <= i < wide:
                    work[i, data, :] = work[i, data, :] + up
        src, dst = work, other
        for depth in (1, 2):
            before = src[depth - 1, data, :]
            center = src[depth, data, :]
            for i in range(depth, wide - depth):
                after = src[i + 1, data, :]
                near = beside(src, i, PAD, tall, center, before, after, lanes)
                dst[i, data, :] = center + relax_of(i) * (r_ref[f, i - 1] - 6.0 * center + near)
                before, center = center, after
            src, dst = dst, src
        own_rows = pl.ds(PAD + DEEP, ny)
        before = src[POST - 1, own_rows, :]
        center = src[POST, own_rows, :]
        for i in range(POST, nx + POST):
            after = src[i + 1, own_rows, :]
            near = beside(src, i, PAD + DEEP, ny, center, before, after, own)
            rows = pl.ds((i - POST) * ny * cols + f, ny, stride=cols)
            w_ref[rows, :] = center
            image_ref[rows, :] = 6.0 * center - near
            before, center = center, after

    by_pairs(cols, one)


def image_kernel(flags, x_ref, p_ref, ylo, yhi, xa, xb, tx_ref, tp_ref, ax_ref, ap_ref, works):
    cols, nx, ny, _ = x_ref.shape
    even = flags[4]
    lanes = lane_index(ny)

    def one(f, u):
        work = works.at[u]
        for ref, same, out, first, base, deep in (
            (x_ref, tx_ref, ax_ref, 0, 0, DEEP),
            (p_ref, tp_ref, ap_ref, DEEP, nx * DEEP, 1),
        ):
            for buf, high in ((xa, even), (xb, 1 - even)):
                plane = first + (1 - high) * (deep - 1)
                work[high * (nx + 1), pl.ds(PAD, ny), :] = buf[f, plane]
            for i in range(nx):
                work[i + 1, pl.ds(PAD, ny), :] = ref[f, i]
                work[i + 1, pl.ds(PAD - 1, 1), :] = ylo[f, pl.ds(base + i * deep + deep - 1, 1), :]
                work[i + 1, pl.ds(PAD + ny, 1), :] = yhi[f, pl.ds(base + i * deep, 1), :]
            before = work[0, pl.ds(PAD, ny), :]
            center = work[1, pl.ds(PAD, ny), :]
            for i in range(nx):
                after = work[i + 2, pl.ds(PAD, ny), :]
                near = beside(work, i + 1, PAD, ny, center, before, after, lanes)
                rows = pl.ds(i * ny * cols + f, ny, stride=cols)
                same[rows, :] = center
                out[rows, :] = 6.0 * center - near
                before, center = center, after

    by_pairs(cols, one)


def from_low(value, axis):
    count = lax.axis_size(axis)
    return lax.ppermute(value, axis, [(i, i + 1) for i in range(count - 1)])


def from_high(value, axis):
    count = lax.axis_size(axis)
    return lax.ppermute(value, axis, [(i + 1, i) for i in range(count - 1)])


def swap(one, two, axis):
    count = lax.axis_size(axis)
    pairs = [[], []]
    for i in range(count - 1):
        pairs[i % 2] += [(i, i + 1), (i + 1, i)]
    two = lax.ppermute(two, axis, pairs[1])
    return lax.ppermute(one, axis, pairs[0]), two


def radices(count):
    out = []
    if count % 2 == 0 and count % 4 == 0 and (count.bit_length() - 1) % 2 == 1:
        out.append(2)
        count //= 2
    while count % 4 == 0:
        out.append(4)
        count //= 4
    if count > 1:
        out.append(count)
    return out


def sum_all(value):
    for axis in ("gy", "gx"):
        count = lax.axis_size(axis)
        stride = 1
        for radix in radices(count):
            index = lax.axis_index(axis)
            parts = [value]
            for k in range(1, radix):
                pairs = []
                for i in range(count):
                    digit = i // stride % radix
                    target = i + ((digit + k) % radix - digit) * stride
                    pairs.append((i, target))
                parts.append(lax.ppermute(value, axis, pairs))
            digit = index // stride % radix
            if radix == 2:
                value = parts[0] + parts[1]
            elif radix == 4:
                even = parts[0] + parts[2]
                odd = parts[1] + parts[3]
                value = even + odd
            else:
                value = functools.reduce(jnp.add, parts)
            stride *= radix
    return value


BF16 = jnp.bfloat16


def gram_kernel(x_ref, w_ref, p_ref, ax_ref, aw_ref, ap_ref, out_ref, s_ref, image):
    chunks, rows, wide = s_ref.shape
    cols = rows // 6
    ny = wide // 128

    def body(c, carry):
        for k, (b_ref, a_ref) in enumerate(((x_ref, ax_ref), (w_ref, aw_ref), (p_ref, ap_ref))):
            for y in range(ny):
                pick = pl.ds(pl.multiple_of((c * ny + y) * cols, cols), cols)
                at = pl.ds(y * 128, 128)
                for ref, put in (
                    (b_ref, lambda r, v: s_ref.__setitem__((c, r, at), v)),
                    (a_ref, lambda r, v: image.__setitem__((r, at), v)),
                ):
                    value = ref[pick, :]
                    high = value.astype(BF16)
                    low = (value - high.astype(F32)).astype(BF16)
                    put(pl.ds(k * cols, cols), high)
                    put(pl.ds((3 + k) * cols, cols), low)
        left = s_ref[c]
        dims = (((1,), (1,)), ((), ()))
        proj = lax.dot_general(left, image[...], dims, preferred_element_type=F32)
        gram = lax.dot_general(left, left, dims, preferred_element_type=F32)
        return (carry[0] + proj, carry[1] + gram)

    zero = jnp.zeros((rows, rows), F32)
    proj, gram = lax.fori_loop(0, chunks, body, (zero, zero))
    nb = 3 * cols
    for k, full in enumerate((proj, gram)):
        full = full[:nb] + full[nb:]
        out_ref[:, pl.ds(k * nb, nb)] = full[:, :nb] + full[:, nb:]


def eliminate(left, right, first):
    size = left.shape[0]
    tiles = size // 8
    lefts = [left[8 * t : 8 * t + 8] for t in range(tiles)]
    rights = [right[8 * t : 8 * t + 8] for t in range(tiles)]
    row = lax.broadcasted_iota(jnp.int32, (8, 1), 0)
    scales = [jnp.zeros((8, 1), F32) for _ in range(tiles)]
    for k in range(size):
        own, at = k // 8, k % 8
        line, other = lefts[own][at : at + 1], rights[own][at : at + 1]
        pivot = line[:, first + k : first + k + 1]
        inverse = 1.0 / pivot
        line, other = line * inverse, other * inverse
        scales[own] = jnp.where(row == at, pivot, scales[own])
        for t in range(own, tiles):
            column = lefts[t][:, first + k : first + k + 1]
            if t == own:
                column = jnp.where(row > at, column, 0.0)
            lefts[t] = lefts[t] - column * line
            rights[t] = rights[t] - column * other
    scales = [lax.rsqrt(scale) for scale in scales]
    return (
        jnp.concatenate([v * scale for v, scale in zip(lefts, scales)], axis=0),
        jnp.concatenate([v * scale for v, scale in zip(rights, scales)], axis=0),
    )


def finish_kernel(ncells, sums_ref, s_ref, block_ref, search_ref, bufs, sems):
    nb = sums_ref.shape[0]
    cols = nb // 3
    chunks, rows, wide = s_ref.shape
    ny = wide // 128
    row = lax.broadcasted_iota(jnp.int32, (nb, 128), 0)
    lane = lax.broadcasted_iota(jnp.int32, (nb, 128), 1)
    eye = jnp.where((lane == row) | (lane == row + nb), 1.0, 0.0)
    left, inverse = eliminate(sums_ref[...], eye, nb)
    flat = -dot_nt(inverse[:cols, :nb], left[:, :nb])
    flat = flat + jnp.where(lane[:cols, :nb] == row[:cols, :nb], SHIFT, 0.0)
    _, scaled = eliminate(dot_nt(flat, flat), flat, 0)
    coef = jnp.dot(
        scaled, inverse, precision=lax.Precision.HIGHEST, preferred_element_type=F32
    )
    coef = coef[:, :rows] * jnp.sqrt(F32(ncells))
    slot = lax.broadcasted_iota(jnp.int32, (cols, rows), 1)
    first = (slot < cols) | ((slot >= nb) & (slot < nb + cols))
    terms = []
    for part in (jnp.where(first, coef, 0.0), jnp.where(first, 0.0, coef)):
        high = part.astype(BF16)
        terms += [high, (part - high.astype(F32)).astype(BF16)]
    terms = jnp.concatenate(terms, axis=0)

    def copies(c):
        return [
            pltpu.make_async_copy(bufs.at[c, k], ref.at[:, c], sems.at[c, k])
            for k, ref in enumerate((block_ref, search_ref))
        ]

    def chunk(c, carry):
        for y in range(0, ny, 2):
            got = jnp.dot(
                terms, s_ref[c, :, pl.ds(y * 128, 256)], preferred_element_type=F32
            )
            search = got[2 * cols : 3 * cols] + got[3 * cols :]
            block = search + (got[:cols] + got[cols : 2 * cols])
            for k, value in enumerate((block, search)):
                for j in range(2):
                    flat = bufs.at[c, k].reshape(cols * ny, 128)
                    flat[pl.ds(y + j, cols, stride=ny), :] = value[:, j * 128 : (j + 1) * 128]
        for copy in copies(c):
            copy.start()
        return carry

    def finish(c, carry):
        for copy in copies(c):
            copy.wait()
        return carry

    lax.fori_loop(0, chunks, chunk, 0, unroll=4 if chunks % 4 == 0 else 1)
    lax.fori_loop(0, chunks, finish, 0)


def step(x, p):
    cols, nx, ny, nz = x.shape
    ngx, ngy = lax.axis_size("gx"), lax.axis_size("gy")
    ix, iy = lax.axis_index("gx"), lax.axis_index("gy")
    flags = jnp.stack([ix > 0, ix < ngx - 1, iy > 0, iy < ngy - 1, ix % 2 == 0]).astype(jnp.int32)
    half, cx, cy = cols // 2, nx // 2, ny // 2
    work = pltpu.VMEM

    yrows = nx * DEEP + nx
    to_ylo, to_yhi, to_xlo, to_xhi = call(
        pack_kernel,
        [shape(cols, yrows, nz)] * 2 + [shape(cols, DEEP + 1, ny, nz)] * 2,
        [], (flags, x, p), smem=1,
    )
    ylo, yhi = from_low(to_yhi, "gy"), from_high(to_ylo, "gy")
    xlo, xhi = swap(to_xlo, to_xhi, "gx")

    devices = ngx * ngy
    sums, to_clo, to_chi = call(
        theta_kernel,
        [shape(devices, 8, 128)] + [shape(cols, nx * DEEP, nz)] * 2,
        [work((2, nx + 2, PAD + ny + 8, nz), F32), work((128 * 8, nz), F32)],
        (flags, x, ylo, yhi, xlo, xhi), smem=1,
    )
    clo, chi = swap(to_clo, to_chi, "gx")
    sums = lax.all_to_all(sums, ("gx", "gy"), 0, 0)

    tall, wide = ny + 2 * DEEP, nx + 2 * DEEP
    plane = PAD + tall + 8
    r, e, c, to_ylo, to_yhi, to_eylo, to_eyhi = call(
        pre_kernel,
        [shape(cols, wide - 4, tall, nz), shape(cols, nx, ny, nz), shape(half, cx, cy, nz)]
        + [shape(half * cx * CO, nz)] * 2
        + [shape(cols, nx * POST, nz)] * 2,
        [work((2, wide, plane, nz), F32)] * 2
        + [work((2, wide, tall, nz), F32), work((2, ny, nz), F32), work((cols, cx, cy, nz), F32)],
        (flags, sums, x, ylo, yhi, xlo, xhi, clo, chi), smem=1,
    )

    cylo, cyhi = from_low(to_yhi, "gy"), from_high(to_ylo, "gy")
    eylo, eyhi = from_low(to_eyhi, "gy"), from_high(to_eylo, "gy")
    to_xlo, to_xhi = call(
        functools.partial(coarse_pack_kernel, CO),
        [shape(half * CO * (cy + 2 * CO), nz)] * 2, [], (flags, c, cylo, cyhi), smem=1,
    )
    cxlo, cxhi = swap(to_xlo, to_xhi, "gx")
    to_exlo, to_exhi = call(
        post_pack_kernel, [shape(cols * POST * (ny + 2 * POST), nz)] * 2, [],
        (flags, e, eylo, eyhi), smem=1,
    )
    exlo, exhi = swap(to_exlo, to_exhi, "gx")
    cwide = cx + 2 * CO
    d, to_ylo, to_yhi = call(
        coarse_kernel,
        [shape(half, cx, cy, nz)] + [shape(half * cx * CP, nz)] * 2,
        [work((2, cwide, PAD + 16 + 8, nz), F32)] * 2 + [work((2, cwide, 16, nz), F32)],
        (flags, c, cylo, cyhi, cxlo, cxhi), smem=1,
    )
    dylo, dyhi = from_low(to_yhi, "gy"), from_high(to_ylo, "gy")
    to_xlo, to_xhi = call(
        functools.partial(coarse_pack_kernel, CP),
        [shape(half * CP * (cy + 2 * CP), nz)] * 2, [], (flags, d, dylo, dyhi), smem=1,
    )
    dxlo, dxhi = swap(to_xlo, to_xhi, "gx")

    flat_x, flat_p, image_x, image_p = call(
        image_kernel, [shape(nx * ny * cols, nz)] * 4,
        [work((2, nx + 2, PAD + ny + 8, nz), F32)],
        (flags, x, p, ylo, yhi, xlo, xhi), smem=1,
    )
    w, image_w = call(
        post_kernel, [shape(nx * ny * cols, nz)] * 2,
        [work((2, nx + 2 * POST, plane, nz), F32)] * 2
        + [work((2, cx + 2 * CP, 16, nz), F32), work((2, 2, 32, nz), F32)],
        (flags, e, eylo, eyhi, exlo, exhi, d, dylo, dyhi, dxlo, dxhi, r), smem=1,
    )

    flat = (flat_x, w, flat_p, image_x, image_w, image_p)
    nb = 3 * cols
    part, split = call(
        gram_kernel,
        [shape(nb, 128), pltpu.VMEM((nx, 2 * nb, ny * nz), BF16)],
        [work((2 * nb, ny * nz), BF16)],
        flat,
    )
    part = sum_all(part)
    any_space = pl.BlockSpec(memory_space=pl.ANY)
    new_block, new_search = pl.pallas_call(
        functools.partial(finish_kernel, nx * ny * nz * devices),
        out_shape=[jax.ShapeDtypeStruct((cols, nx, ny, nz), F32)] * 2,
        in_specs=[VMEM, VMEM],
        out_specs=[any_space] * 2,
        scratch_shapes=[
            work((nx, 2, cols, ny, nz), F32),
            pltpu.SemaphoreType.DMA((nx, 2)),
        ],
        compiler_params=pltpu.CompilerParams(vmem_limit_bytes=GRANT),
        name="finish",
    )(part, split)
    return (new_block, new_search)


def solution(mesh):
    spec = P(None, "gx", "gy", None)
    return jax.shard_map(
        step, mesh=mesh, in_specs=(spec, spec), out_specs=(spec, spec), check_vma=False
    )
```
